32 devices in a mesh: rep: 2 (over core), fsdp: 16 (over z, y, x).
Axes of the slice: x: 2, y: 2, z: 4, core: 2. Of those that a mesh axis runs over, the one named last changes fastest.
Arguments:
- tokens: bfloat16 [64, 384, 768], P(('rep', 'fsdp')), may hold values from -6 to 6
- grids: int32 [64, 2], P(('rep', 'fsdp')), may hold values from 8 to 24, as said below
- keep_attn: int32 [64], P(('rep', 'fsdp')), may hold values 0 or 1
- keep_mlp: int32 [64], P(('rep', 'fsdp')), may hold values 0 or 1
- cotangent: bfloat16 [64, 384, 768], P(('rep', 'fsdp')), may hold values from -6 to 6
- ln1_gain: bfloat16 [768], P('fsdp'), may hold values from 0.5 to 1.5
- ln1_shift: bfloat16 [768], P('fsdp'), may hold values from -3 to 3
- w_qkv: bfloat16 [768, 2304], P('fsdp'), may hold values from -0.21875 to 0.21875
- bias_qv: bfloat16 [1536], P('fsdp'), may hold values from -3 to 3
- w_proj: bfloat16 [768, 768], P('fsdp'), may hold values from -0.875 to 0.875
- bias_proj: bfloat16 [768], P('fsdp'), may hold values from -3 to 3
- ln2_gain: bfloat16 [768], P('fsdp'), may hold values from 0.5 to 1.5
- ln2_shift: bfloat16 [768], P('fsdp'), may hold values from -3 to 3
- w_fc1: bfloat16 [768, 3072], P('fsdp'), may hold values from -0.21875 to 0.21875
- bias_fc1: bfloat16 [3072], P('fsdp'), may hold values from -3 to 3
- w_fc2: bfloat16 [3072, 768], P('fsdp'), may hold values from -0.109375 to 0.109375
- bias_fc2: bfloat16 [768], P('fsdp'), may hold values from -3 to 3
Outputs:
- layer_out: bfloat16 [64, 384, 768], P(('rep', 'fsdp'))
- grad_tokens: float32 [64, 384, 768], P(('rep', 'fsdp'))
- grad_ln1_gain: float32 [768], P('fsdp')
- grad_ln1_shift: float32 [768], P('fsdp')
- grad_w_qkv: float32 [768, 2304], P('fsdp')
- grad_bias_qv: float32 [1536], P('fsdp')
- grad_w_proj: float32 [768, 768], P('fsdp')
- grad_bias_proj: float32 [768], P('fsdp')
- grad_ln2_gain: float32 [768], P('fsdp')
- grad_ln2_shift: float32 [768], P('fsdp')
- grad_w_fc1: float32 [768, 3072], P('fsdp')
- grad_bias_fc1: float32 [3072], P('fsdp')
- grad_w_fc2: float32 [3072, 768], P('fsdp')
- grad_bias_fc2: float32 [768], P('fsdp')
The draws below stay inside these ranges and needn't reach their ends.
Inputs may be any that keep to these rules, and one draw needn't show every extreme that they name: `grids`: each row is (rows, columns) of an image's patch grid: rows from 8 to 20, columns = max(14, min(24, 280 // rows)); some image has 8 rows and some 20, so the most valid tokens of an image is 282.
All inputs are finite; a program needn't handle non-finite values. No bound on the sum of `keep_attn` or of `keep_mlp` on one device may be relied on, other than what follows from the above.
Results may differ from the reference program's by a relative error of at most 0.013.
Values may be sent and summed in bfloat16 or wider, within the bound.
A program may use at most 192 MiB of HBM per device.

```python
import jax
import jax.numpy as jnp
from jax import lax

D = 768
HEAD = 64
FF = 3072
SEQ = 384
ROWS_LO = 8
ROWS_HI = 20
COLS_LO = 14
COLS_HI = 24
PATCHES = 280
IMAGES = 64


def draw_grids(key, part):
    heights = jax.random.randint(key, (IMAGES,), ROWS_LO, ROWS_HI + 1)
    position = jnp.arange(IMAGES, dtype=jnp.int32)
    heights = jnp.where(position == 0, ROWS_LO, jnp.where(position == 1, ROWS_HI, heights))
    widths = jnp.maximum(COLS_LO, jnp.minimum(COLS_HI, PATCHES // heights))
    return jnp.stack([heights, widths], axis=1).astype(jnp.int32)


def place_ends(drawn, key, smallest, largest):
    index_at = [jax.random.randint(jax.random.fold_in(key, axis), (), 0, length) for axis, length in enumerate(drawn.shape)]
    widest = drawn.shape.index(max(drawn.shape))
    neighbour = index_at[:widest] + [(index_at[widest] + 1) % drawn.shape[widest]] + index_at[widest + 1:]
    return drawn.at[tuple(index_at)].set(smallest).at[tuple(neighbour)].set(largest)


def with_spikes(entries, rng, source, target, shards_of, factor):
    owner, partner = [(jnp.arange(entries.shape[dim]) // (entries.shape[dim] // shards_of)).reshape([-1 if axis == dim else 1 for axis in range(entries.ndim)]) for dim in (source, target)]
    chosen = jax.random.permutation(rng, shards_of)[partner]
    strong = (owner == chosen) | (owner == (partner + shards_of // 2) % shards_of)
    return jnp.where(strong, factor * entries, entries)


def steps_of(stream_key, dims, split, smallest, top_value):
    loudness, own = 1.0, jax.random.fold_in(stream_key, 6)
    for axis_at, shards_of in split:
        steps = jnp.exp(jax.random.uniform(jax.random.fold_in(own, axis_at), (shards_of,), jnp.float32, smallest / len(split), top_value / len(split)))
        loudness = loudness * jnp.repeat(steps, dims[axis_at] // shards_of).reshape([-1 if axis == axis_at else 1 for axis in range(len(dims))])
    return loudness


def centred(key, shape, width, reach, pieces=(), kind=jnp.bfloat16):
    values = jax.random.normal(key, shape, jnp.float32) * width
    if len(pieces) > 0:
        values = steps_of(key, shape, pieces, -0.22, 0.18) * values
    return jnp.clip(values, min=-reach, max=reach).astype(kind)


def bell_draw_with(key, extent, scale, bound, split, heavy, kind=jnp.bfloat16):
    entries = scale * jax.random.normal(key, extent, jnp.float32)
    if split:
        entries = entries * steps_of(key, extent, split, -0.22, 0.18)
    return jnp.clip(with_spikes(entries, jax.random.fold_in(key, 3), *heavy), -bound, bound).astype(kind)


def setup_inputs(seed: int = 0) -> dict:
    arg_keys = jax.random.split(jax.random.key(seed), 18)
    return {
        "tokens": centred(arg_keys[0], (IMAGES, SEQ, D), 1.0, 6.0, ((0, 32),)),
        "grids": draw_grids(jax.random.fold_in(arg_keys[17], 71), 0),
        "keep_attn": place_ends((jax.random.randint(arg_keys[2], (IMAGES,), 0, 10) < 9).astype(jnp.int32), jax.random.fold_in(arg_keys[2], 1), 0, 1),
        "keep_mlp": place_ends((jax.random.randint(arg_keys[3], (IMAGES,), 0, 10) < 9).astype(jnp.int32), jax.random.fold_in(arg_keys[3], 1), 0, 1),
        "cotangent": bell_draw_with(arg_keys[4], (IMAGES, SEQ, D), 1.0, 6.0, ((0, 32),), (0, 2, 32, 2.75)),
        "ln1_gain": jnp.clip(0.5 + 1.0 * jax.random.uniform(arg_keys[5], (D,), jnp.float32) ** steps_of(arg_keys[5], (D,), ((0, 16),), -0.2, 0.2), 0.5, 1.5).astype(jnp.bfloat16),
        "ln1_shift": centred(arg_keys[6], (D,), 0.5, 3.0, ((0, 16),)),
        "w_qkv": centred(arg_keys[7], (D, 3 * D), D ** -0.5, 0.21875, ((0, 16),)),
        "bias_qv": centred(arg_keys[8], (2 * D,), 0.5, 3.0, ((0, 16),)),
        "w_proj": centred(arg_keys[9], (D, D), (D // 16) ** -0.5, 0.875, ((0, 16),)),
        "bias_proj": centred(arg_keys[10], (D,), 0.5, 3.0, ((0, 16),)),
        "ln2_gain": jnp.clip(0.5 + 1.0 * jax.random.uniform(arg_keys[11], (D,), jnp.float32) ** steps_of(arg_keys[11], (D,), ((0, 16),), -0.2, 0.2), 0.5, 1.5).astype(jnp.bfloat16),
        "ln2_shift": centred(arg_keys[12], (D,), 0.5, 3.0, ((0, 16),)),
        "w_fc1": centred(arg_keys[13], (D, FF), D ** -0.5, 0.21875, ((0, 16),)),
        "bias_fc1": centred(arg_keys[14], (FF,), 0.5, 3.0, ((0, 16),)),
        "w_fc2": centred(arg_keys[15], (FF, D), FF ** -0.5, 0.109375, ((0, 16),)),
        "bias_fc2": centred(arg_keys[16], (D,), 0.5, 3.0, ((0, 16),)),
    }


epsilon = 1e-06
root_half = 0.7071067811865476
highest = lax.Precision.HIGHEST

@jax.custom_vjp
def low(v):
    return lax.optimization_barrier(v.astype(jnp.bfloat16)).astype(jnp.float32)

@jax.custom_vjp
def low_back(v):
    return v

def low_keep(v):
    return (low(v), None)

def low_pass(kept, grad):
    return (grad,)

def back_keep(v):
    return (v, None)

def back_low(kept, grad):
    return (low(grad),)
low.defvjp(low_keep, low_pass)
low_back.defvjp(back_keep, back_low)

def normalize(stream, gain, shift):
    center = lax.optimization_barrier(jnp.mean(stream, axis=-1, keepdims=True))
    shifted = stream - center
    spread = lax.optimization_barrier(jnp.mean(shifted * shifted, axis=-1, keepdims=True))
    return shifted * lax.rsqrt(spread + epsilon) * gain + shift

def gelu_exact(values):
    return 0.5 * values * (1.0 + lax.erf(values * root_half))

def block_forward(params, stream, grids, keep_attn, keep_mlp):
    ln1_gain, ln1_shift, w_qkv, bias_qv, w_proj, bias_proj, ln2_gain, ln2_shift, w_fc1, bias_fc1, w_fc2, bias_fc2 = params
    images, seq_len, feat_dim = stream.shape
    num_heads = feat_dim // HEAD
    lengths = grids[:, 0] * grids[:, 1] + 2
    key_valid = jnp.arange(seq_len, dtype=jnp.int32)[None, :] < lengths[:, None]
    scale_attn = (keep_attn.astype(jnp.float32) / 0.9)[:, None, None]
    scale_mlp = (keep_mlp.astype(jnp.float32) / 0.9)[:, None, None]
    normed_one = low(normalize(stream, ln1_gain, ln1_shift))
    full_bias = jnp.concatenate([bias_qv[:feat_dim], jnp.zeros((feat_dim,), jnp.float32), bias_qv[feat_dim:]])
    triple = jnp.einsum('bsd,df->bsf', normed_one, w_qkv, precision=highest) + full_bias
    triple = low_back(low(triple)).reshape(images, seq_len, 3, num_heads, HEAD)
    scores = jnp.einsum('bqhe,bkhe->bhqk', triple[:, :, 0], triple[:, :, 1], precision=highest) * 0.125
    scores = low_back(jnp.where(key_valid[:, None, None, :], scores, -1000000000.0))
    row_max = lax.optimization_barrier(jnp.max(scores, axis=-1, keepdims=True))
    exp_scores = jnp.exp(scores - row_max)
    probs_low = low(exp_scores / lax.optimization_barrier(jnp.sum(exp_scores, axis=-1, keepdims=True)))
    mixed_low = jnp.einsum('bhqk,bkhe->bqhe', probs_low, triple[:, :, 2], precision=highest)
    mixed_low = low_back(low(mixed_low.reshape(images, seq_len, feat_dim)))
    branch = jnp.einsum('bsd,df->bsf', mixed_low, w_proj, precision=highest) + bias_proj
    middle = stream + scale_attn * low_back(branch)
    normed_two = low(normalize(middle, ln2_gain, ln2_shift))
    pre_act = low_back(jnp.einsum('bsd,df->bsf', normed_two, w_fc1, precision=highest) + bias_fc1)
    act_low = low(gelu_exact(pre_act))
    branch_two = low_back(jnp.einsum('bsf,fd->bsd', act_low, w_fc2, precision=highest) + bias_fc2)
    return middle + scale_mlp * branch_two

def reference(tokens, grids, keep_attn, keep_mlp, cotangent, ln1_gain, ln1_shift, w_qkv, bias_qv, w_proj, bias_proj, ln2_gain, ln2_shift, w_fc1, bias_fc1, w_fc2, bias_fc2):
    params = tuple((weight.astype(jnp.float32) for weight in (ln1_gain, ln1_shift, w_qkv, bias_qv, w_proj, bias_proj, ln2_gain, ln2_shift, w_fc1, bias_fc1, w_fc2, bias_fc2)))
    stream = tokens.astype(jnp.float32)
    group_size = 8

    def whole_layer(params, stream):

        def one_group(block_items):
            return block_forward(params, block_items[0], block_items[1], block_items[2], block_items[3])
        blocks = (stream.reshape(-1, group_size, SEQ, D), grids.reshape(-1, group_size, 2), keep_attn.reshape(-1, group_size), keep_mlp.reshape(-1, group_size))
        return lax.map(jax.checkpoint(one_group), blocks).reshape(IMAGES, SEQ, D)
    result, pullback = jax.vjp(whole_layer, params, stream)
    grad_params, grad_tokens = pullback(cotangent.astype(jnp.float32))
    return (result.astype(jnp.bfloat16), grad_tokens, grad_params[0], grad_params[1], grad_params[2], grad_params[3], grad_params[4], grad_params[5], grad_params[6], grad_params[7], grad_params[8], grad_params[9], grad_params[10], grad_params[11])
```

```python
import functools

import jax
import jax.numpy as jnp
from jax import lax
from jax.experimental import pallas as pl
from jax.experimental.pallas import tpu as pltpu
from jax.sharding import PartitionSpec as P

HEAD = 64
MESH = pl.DeviceIdType.MESH
F32 = jnp.float32
BF16 = jnp.bfloat16
epsilon = 1e-06
root_half = 0.7071067811865476

ROWS = 48
WIDE = 768
HALF = 384


class Place:
    def __init__(self):
        self.r = lax.axis_index("rep")
        self.i = lax.axis_index("fsdp")
        r, i = self.r, self.i
        self.z = i // 4
        self.y = (i // 2) % 2
        self.x = i % 2
        fx, fy = 1 - 2 * self.x, 1 - 2 * self.y
        self.to_a = i + (1 - r) * fx + r * 2 * fy
        self.to_b = i + (1 - r) * 2 * fy + r * fx
        self.own = (self.y, self.x)
        self.col_a = (self.y + r * fy, self.x + (1 - r) * fx)
        self.col_b = (self.y + (1 - r) * fy, self.x + r * fx)
        self.col_ab = (1 - self.y, 1 - self.x)

    def z_dev(self, k):
        zz = (self.z + k) % 4
        return zz, (self.r, zz * 4 + self.i % 4)

    @property
    def dev_a(self):
        return (self.r, self.to_a)

    @property
    def dev_b(self):
        return (self.r, self.to_b)

    @property
    def dev_d(self):
        return (1 - self.r, self.i)


def greet(place):
    barrier = pltpu.get_barrier_semaphore()
    for dev in (place.z_dev(1)[1], place.z_dev(2)[1], place.z_dev(3)[1], place.dev_a, place.dev_b, place.dev_d):
        pl.semaphore_signal(barrier, inc=1, device_id=dev, device_id_type=MESH)
    pl.semaphore_wait(barrier, 6)


def remote(src, dst, send, recv, dev):
    return pltpu.make_async_remote_copy(
        src_ref=src, dst_ref=dst, send_sem=send, recv_sem=recv, device_id=dev, device_id_type=MESH
    )


class Gather:
    def __init__(self, place, part, own, send, recv, local, halves=True):
        self.p, self.part, self.own = place, part, own
        self.send, self.recv, self.local, self.halves = send, recv, local, halves

    def _z(self, k):
        p = self.p
        _, dev = p.z_dev(k)
        return remote(
            self.own(p.r), self.part(p.z, *p.own, p.r), self.send.at[k - 1], self.recv.at[k - 1], dev
        )

    def _col(self, col, slot, dev):
        piece = self.part(slice(None), *col, self.p.r)
        return remote(piece, piece, self.send.at[slot], self.recv.at[slot], dev)

    def _keep(self):
        p = self.p
        return pltpu.make_async_copy(self.own(p.r), self.part(p.z, *p.own, p.r), self.local)

    def start(self):
        self._keep().start()
        for k in (1, 2, 3):
            self._z(k).start()

    def after_z(self):
        p = self.p
        self._keep().wait()
        for k in (1, 2, 3):
            self._z(k).wait_recv()
        self._col(p.own, 3, p.dev_a).start()
        self._col(p.own, 4, p.dev_b).start()
        if self.halves:
            self._col(p.own, 6, p.dev_d).start()

    def after_a(self):
        p = self.p
        self._col(p.own, 3, p.dev_a).wait_recv()
        self._col(p.col_a, 5, p.dev_b).start()
        if self.halves:
            self._col(p.col_a, 7, p.dev_d).start()

    def after_b(self):
        p = self.p
        self._col(p.own, 4, p.dev_b).wait_recv()
        if self.halves:
            self._col(p.col_b, 8, p.dev_d).start()
        self._col(p.own, 5, p.dev_b).wait_recv()
        if self.halves:
            self._col(p.col_ab, 9, p.dev_d).start()

    def done(self):
        p = self.p
        if self.halves:
            for slot in (6, 7, 8, 9):
                self._col(p.own, slot, p.dev_d).wait_recv()

    def drain(self):
        p = self.p
        for k in (1, 2, 3):
            self._z(k).wait_send()
        for slot in range(3, 10 if self.halves else 6):
            self._col(p.own, slot, p.dev_d).wait_send()


def add_into(dst, src, rows):
    dst[...] = (dst[...].astype(F32) + src[...].astype(F32)).astype(dst.dtype)


class Scatter:
    def __init__(self, place, part, bufs, out, send, recv):
        self.p, self.part, self.out = place, part, out
        self.dbuf, self.bbuf, self.abuf, self.zbuf = bufs
        self.send, self.recv = send, recv

    def _d(self, zz):
        p = self.p
        return remote(
            self.part(zz, slice(None), slice(None), 1 - p.r), self.dbuf.at[zz], self.send.at[zz], self.recv.at[zz], p.dev_d
        )

    def _b(self, slot):
        p = self.p
        col = (p.col_b, p.col_ab)[slot]
        return remote(
            self.part(slice(None), *col, p.r), self.bbuf.at[slot], self.send.at[4 + slot], self.recv.at[4 + slot], p.dev_b
        )

    def _a(self):
        p = self.p
        return remote(self.part(slice(None), *p.col_a, p.r), self.abuf, self.send.at[6], self.recv.at[6], p.dev_a)

    def _z(self, k):
        p = self.p
        zz, dev = p.z_dev(k)
        return remote(
            self.part(zz, *p.own, p.r), self.zbuf.at[k - 1], self.send.at[6 + k], self.recv.at[6 + k], dev
        )

    def _f(self):
        p = self.p
        return remote(self.out(p.r), self.out(p.r), self.send.at[10], self.recv.at[10], p.dev_d)

    def start(self):
        for zz in range(4):
            self._d(zz).start()

    def after_d(self):
        p = self.p
        for zz in range(4):
            self._d(zz).wait_recv()
        for slot, col in enumerate((p.col_b, p.col_ab, p.col_a, p.own)):
            for zz in range(4):
                add_into(self.part(zz, *col, p.r), self.dbuf.at[(zz,) + col], ROWS)
            if slot < 2:
                self._b(slot).start()

    def after_b(self):
        p = self.p
        self._b(1).wait_recv()
        for zz in range(4):
            add_into(self.part(zz, *p.col_a, p.r), self.bbuf.at[1, zz], ROWS)
        self._a().start()
        self._b(0).wait_recv()
        for zz in range(4):
            add_into(self.part(zz, *p.own, p.r), self.bbuf.at[0, zz], ROWS)

    def after_a(self):
        p = self.p
        self._a().wait_recv()
        for zz in range(4):
            add_into(self.part(zz, *p.own, p.r), self.abuf.at[zz], ROWS)
        for k in (1, 2, 3):
            self._z(k).start()

    def after_z(self):
        p = self.p
        for k in (1, 2, 3):
            self._z(k).wait_recv()
        total = self.part(p.z, *p.own, p.r)[...].astype(F32)
        for k in range(3):
            total = total + self.zbuf[k].astype(F32)
        self.out(p.r)[...] = total
        self._f().start()

    def done(self):
        self._f().wait_recv()

    def drain(self):
        for zz in range(4):
            self._d(zz).wait_send()
        for slot in range(2):
            self._b(slot).wait_send()
        self._a().wait_send()
        for k in (1, 2, 3):
            self._z(k).wait_send()
        self._f().wait_send()


class ScatterSmall:
    def __init__(self, place, ref, bufs, out, send, recv):
        self.p, self.ref, self.out = place, ref, out
        self.bbuf, self.abuf, self.zbuf, self.fbuf = bufs
        self.send, self.recv = send, recv

    def _b(self, slot):
        p = self.p
        col = (p.col_b, p.col_ab)[slot]
        return remote(self.ref.at[(slice(None),) + col], self.bbuf.at[slot], self.send.at[slot], self.recv.at[slot], p.dev_b)

    def _a(self):
        p = self.p
        return remote(self.ref.at[(slice(None),) + p.col_a], self.abuf, self.send.at[2], self.recv.at[2], p.dev_a)

    def _z(self, k):
        p = self.p
        zz, dev = p.z_dev(k)
        return remote(self.ref.at[(zz,) + p.own], self.zbuf.at[k - 1], self.send.at[2 + k], self.recv.at[2 + k], dev)

    def _f(self):
        p = self.p
        return remote(self.out, self.fbuf, self.send.at[6], self.recv.at[6], p.dev_d)

    def start(self):
        self._b(0).start()
        self._b(1).start()

    def after_b(self):
        p = self.p
        self._b(0).wait_recv()
        self._b(1).wait_recv()
        self.ref[(slice(None),) + p.col_a] += self.bbuf[1]
        self.ref[(slice(None),) + p.own] += self.bbuf[0]
        self._a().start()

    def after_a(self):
        p = self.p
        self._a().wait_recv()
        self.ref[(slice(None),) + p.own] += self.abuf[...]
        for k in (1, 2, 3):
            self._z(k).start()

    def after_z(self):
        p = self.p
        for k in (1, 2, 3):
            self._z(k).wait_recv()
        self.out[...] = self.ref[(p.z,) + p.own] + self.zbuf[0] + self.zbuf[1] + self.zbuf[2]
        self._f().start()

    def done(self):
        self._f().wait_recv()
        self._f().wait_send()
        self.out[...] = self.out[...] + self.fbuf[...]

    def drain(self):
        self._b(0).wait_send()
        self._b(1).wait_send()
        self._a().wait_send()
        for k in (1, 2, 3):
            self._z(k).wait_send()


UNITS = tuple(("qkv", t) for t in range(3)) + (("proj", 0),) + tuple(("fc1", t) for t in range(4)) + tuple(("fc2", t) for t in range(4))


def pick(name, t, core):
    if name == "fc2":
        return (pl.ds(ROWS * t, ROWS), pl.ds(pl.multiple_of(core * HALF, 128), HALF))
    return (slice(None), pl.ds(pl.multiple_of(WIDE * t + core * HALF, 128), HALF))


def gather_kernel(qkv, proj, fc1, fc2, small, gqkv, gproj, gfc1, gfc2, gsmall, send, recv, ssend, srecv, local, slocal):
    place = Place()
    shards = {"qkv": qkv, "proj": proj, "fc1": fc1, "fc2": fc2}
    wholes = {"qkv": gqkv, "proj": gproj, "fc1": gfc1, "fc2": gfc2}
    greet(place)
    tiny = Gather(
        place, lambda zs, y, x, core: gsmall.at[zs, y, x], lambda core: small, ssend, srecv, slocal, halves=False
    )
    units = [
        Gather(
            place,
            lambda zs, y, x, core, name=name, t=t: wholes[name].at[(zs, y, x) + pick(name, t, core)],
            lambda core, name=name, t=t: shards[name].at[pick(name, t, core)],
            send.at[n],
            recv.at[n],
            local.at[n],
        )
        for n, (name, t) in enumerate(UNITS)
    ]
    count = len(units)
    tiny.start()
    units[0].start()
    tiny.after_z()
    tiny.after_a()
    tiny.after_b()
    for step in range(count + 3):
        if step + 1 < count:
            units[step + 1].start()
        if step < count:
            units[step].after_z()
        if 0 <= step - 1 < count:
            units[step - 1].after_a()
        if 0 <= step - 2 < count:
            units[step - 2].after_b()
    for unit in units:
        unit.done()
    for unit in units + [tiny]:
        unit.drain()


def whole_vmem(count):
    return [pl.BlockSpec(memory_space=pltpu.VMEM)] * count


def gather_weights(w_qkv, w_proj, w_fc1, w_fc2, small):
    shapes = [(4, 2, 2) + v.shape for v in (w_qkv, w_proj, w_fc1, w_fc2)]
    n = len(UNITS)
    out = pl.pallas_call(
        gather_kernel,
        out_shape=[jax.ShapeDtypeStruct(s, BF16) for s in shapes] + [jax.ShapeDtypeStruct((4, 2, 2) + small.shape, F32)],
        in_specs=whole_vmem(5),
        out_specs=whole_vmem(5),
        scratch_shapes=[
            pltpu.SemaphoreType.DMA((n, 10)),
            pltpu.SemaphoreType.DMA((n, 10)),
            pltpu.SemaphoreType.DMA((6,)),
            pltpu.SemaphoreType.DMA((6,)),
            pltpu.SemaphoreType.DMA((n,)),
            pltpu.SemaphoreType.DMA,
        ],
        compiler_params=pltpu.CompilerParams(collective_id=0, has_side_effects=True, vmem_limit_bytes=56 << 20),
        name="gather_weights",
    )(w_qkv, w_proj, w_fc1, w_fc2, small)
    return [o.reshape((-1, o.shape[-1])) for o in out[:4]] + [out[4].reshape(16, 16, 128)]


def scatter_kernel(
    gqkv, gproj, gfc1, gfc2, gsmall, oqkv, oproj, ofc1, ofc2, osmall, vq, vp, v1, v2, vs, dbuf, bbuf, abuf, zbuf, sb, sa, sz, sf, send, recv, ssend, srecv, load
):
    place = Place()
    loads = [
        pltpu.make_async_copy(s, d, load.at[n])
        for n, (s, d) in enumerate(((gfc2, v2), (gfc1, v1), (gproj, vp), (gqkv, vq), (gsmall, vs)))
    ]
    for copy in loads:
        copy.start()
    sums = {"qkv": vq, "proj": vp, "fc1": v1, "fc2": v2}
    outs = {"qkv": oqkv, "proj": oproj, "fc1": ofc1, "fc2": ofc2}
    greet(place)
    order = tuple(reversed(UNITS))
    units = [
        Scatter(
            place,
            lambda zs, y, x, core, name=name, t=t: sums[name].at[(zs, y, x) + pick(name, t, core)],
            (dbuf.at[n], bbuf.at[n], abuf.at[n], zbuf.at[n]),
            lambda core, name=name, t=t: outs[name].at[pick(name, t, core)],
            send.at[n],
            recv.at[n],
        )
        for n, (name, t) in enumerate(order)
    ]
    tiny = ScatterSmall(place, vs, (sb, sa, sz, sf), osmall, ssend, srecv)
    for copy in loads:
        copy.wait()
    tiny.start()
    count = len(units)
    for step in range(count + 5):
        if step < count:
            units[step].start()
        if 0 <= step - 1 < count:
            units[step - 1].after_d()
        if 0 <= step - 2 < count:
            units[step - 2].after_b()
        if 0 <= step - 3 < count:
            units[step - 3].after_a()
        if 0 <= step - 4 < count:
            units[step - 4].after_z()
        if step == 2:
            tiny.after_b()
        if step == 4:
            tiny.after_a()
        if step == 6:
            tiny.after_z()
    for unit in units + [tiny]:
        unit.done()
    for unit in units + [tiny]:
        unit.drain()


def scatter_grads(g_qkv, g_proj, g_fc1, g_fc2, small):
    n = len(UNITS)
    shapes = [(ROWS, g_qkv.shape[1]), (ROWS, g_proj.shape[1]), (ROWS, g_fc1.shape[1]), (g_fc2.shape[0] // 16, g_fc2.shape[1])]
    tiles = [(4, 2, 2) + s for s in shapes]
    args = [g.astype(BF16).reshape(s) for g, s in zip((g_qkv, g_proj, g_fc1, g_fc2), tiles)]
    out = pl.pallas_call(
        scatter_kernel,
        out_shape=[jax.ShapeDtypeStruct(s, F32) for s in shapes] + [jax.ShapeDtypeStruct((16, 128), F32)],
        in_specs=[pl.BlockSpec(memory_space=pltpu.HBM)] * 5,
        out_specs=whole_vmem(5),
        scratch_shapes=[pltpu.VMEM(s, BF16) for s in tiles]
        + [pltpu.VMEM((4, 2, 2, 16, 128), F32)]
        + [
            pltpu.VMEM((n, 4, 2, 2, ROWS, HALF), BF16),
            pltpu.VMEM((n, 2, 4, ROWS, HALF), BF16),
            pltpu.VMEM((n, 4, ROWS, HALF), BF16),
            pltpu.VMEM((n, 3, ROWS, HALF), BF16),
            pltpu.VMEM((2, 4, 16, 128), F32),
            pltpu.VMEM((4, 16, 128), F32),
            pltpu.VMEM((3, 16, 128), F32),
            pltpu.VMEM((16, 128), F32),
            pltpu.SemaphoreType.DMA((n, 11)),
            pltpu.SemaphoreType.DMA((n, 11)),
            pltpu.SemaphoreType.DMA((7,)),
            pltpu.SemaphoreType.DMA((7,)),
            pltpu.SemaphoreType.DMA((5,)),
        ],
        compiler_params=pltpu.CompilerParams(collective_id=1, has_side_effects=True, vmem_limit_bytes=56 << 20),
        name="scatter_grads",
    )(*args, small.reshape(4, 2, 2, 16, 128))
    return out


def layer_norm(stream, gain, shift):
    center = jnp.mean(stream, axis=-1, keepdims=True)
    shifted = stream - center
    inverse = lax.rsqrt(jnp.mean(shifted * shifted, axis=-1, keepdims=True) + epsilon)
    normed = shifted * inverse
    return (normed * gain + shift, normed, inverse)


def norm_back(grad_normed, normed, inverse, gain):
    scaled = grad_normed * gain
    grad_input = inverse * (
        scaled
        - jnp.mean(scaled, axis=-1, keepdims=True)
        - normed * jnp.mean(scaled * normed, axis=-1, keepdims=True)
    )
    return (grad_input, jnp.sum(grad_normed * normed, axis=0), jnp.sum(grad_normed, axis=0))


def gelu_exact(values):
    return 0.5 * values * (1.0 + lax.erf(values * root_half))


def outer_sum(left, right):
    return lax.dot_general(left, right, (((0,), (0,)), ((), ())), preferred_element_type=F32)


def back_dot(left, right):
    return lax.dot_general(left, right, (((1,), (1,)), ((), ())), preferred_element_type=F32)


def layer(tokens, grids, keep_attn, keep_mlp, cotangent, params):
    ln1_gain, ln1_shift, w_qkv, bias_qv, w_proj, bias_proj, ln2_gain, ln2_shift, w_fc1, bias_fc1, w_fc2, bias_fc2 = params
    images, seq_len, feat_dim = tokens.shape
    num_heads = feat_dim // HEAD
    row_count = images * seq_len
    lengths = grids[:, 0] * grids[:, 1] + 2
    key_valid = lax.broadcasted_iota(jnp.int32, (images, seq_len), 1) < lengths[:, None]
    scale_attn = jnp.broadcast_to((keep_attn.astype(F32) / 0.9)[:, None], (images, seq_len)).reshape(row_count, 1)
    scale_mlp = jnp.broadcast_to((keep_mlp.astype(F32) / 0.9)[:, None], (images, seq_len)).reshape(row_count, 1)
    stream = tokens.astype(F32).reshape(row_count, feat_dim)
    normed_out, normed_one, inverse_one = layer_norm(stream, ln1_gain, ln1_shift)
    normed_low_one = normed_out.astype(BF16)
    full_bias = jnp.concatenate([bias_qv[:feat_dim], jnp.zeros((feat_dim,), F32), bias_qv[feat_dim:]])
    triple = jnp.dot(normed_low_one, w_qkv, preferred_element_type=F32) + full_bias
    triple = triple.astype(BF16).reshape(images, seq_len, 3, num_heads, HEAD)
    queries, key_rows, values = triple[:, :, 0], triple[:, :, 1], triple[:, :, 2]
    scores = jnp.einsum("bqhe,bkhe->bhqk", queries, key_rows, preferred_element_type=F32) * 0.125
    scores = jnp.where(key_valid[:, None, None, :], scores, -1000000000.0)
    probs_full = jax.nn.softmax(scores, axis=-1)
    probs_low = probs_full.astype(BF16)
    mixed_low = jnp.einsum("bhqk,bkhe->bqhe", probs_low, values, preferred_element_type=F32)
    mixed_low = mixed_low.reshape(row_count, feat_dim).astype(BF16)
    branch = jnp.dot(mixed_low, w_proj, preferred_element_type=F32) + bias_proj
    middle = stream + scale_attn * branch
    normed_out, normed_two, inverse_two = layer_norm(middle, ln2_gain, ln2_shift)
    normed_low_two = normed_out.astype(BF16)
    pre_act = jnp.dot(normed_low_two, w_fc1, preferred_element_type=F32) + bias_fc1
    act_value, act_pullback = jax.vjp(gelu_exact, pre_act)
    act_low = act_value.astype(BF16)
    branch_two = jnp.dot(act_low, w_fc2, preferred_element_type=F32) + bias_fc2
    layer_out = (middle + scale_mlp * branch_two).astype(BF16).reshape(images, seq_len, feat_dim)
    grad_out = cotangent.astype(F32).reshape(row_count, feat_dim)
    grad_branch_two = (grad_out * scale_mlp).astype(BF16)
    grad_fc2 = outer_sum(act_low, grad_branch_two)
    grad_fc2_bias = jnp.sum(grad_branch_two.astype(F32), axis=0)
    grad_act = back_dot(grad_branch_two, w_fc2)
    grad_pre = act_pullback(grad_act)[0].astype(BF16)
    grad_fc1 = outer_sum(normed_low_two, grad_pre)
    grad_fc1_bias = jnp.sum(grad_pre.astype(F32), axis=0)
    grad_normed_two = back_dot(grad_pre, w_fc1)
    grad_middle, grad_gain_two, grad_shift_two = norm_back(grad_normed_two, normed_two, inverse_two, ln2_gain)
    grad_middle = grad_middle + grad_out
    grad_branch = (grad_middle * scale_attn).astype(BF16)
    grad_proj = outer_sum(mixed_low, grad_branch)
    grad_proj_bias = jnp.sum(grad_branch.astype(F32), axis=0)
    grad_mixed = back_dot(grad_branch, w_proj).astype(BF16).reshape(images, seq_len, num_heads, HEAD)
    grad_values = jnp.einsum("bhqk,bqhe->bkhe", probs_low, grad_mixed, preferred_element_type=F32)
    grad_probs = jnp.einsum("bqhe,bkhe->bhqk", grad_mixed, values, preferred_element_type=F32)
    row_delta = jnp.sum(probs_full * grad_probs, axis=-1, keepdims=True)
    grad_scores = (probs_full * (grad_probs - row_delta)).astype(BF16)
    grad_queries = jnp.einsum("bhqk,bkhe->bqhe", grad_scores, key_rows, preferred_element_type=F32) * 0.125
    grad_keys = jnp.einsum("bhqk,bqhe->bkhe", grad_scores, queries, preferred_element_type=F32) * 0.125
    grad_triple = jnp.stack([grad_queries, grad_keys, grad_values], axis=2).astype(BF16).reshape(row_count, 3 * feat_dim)
    grad_qkv = outer_sum(normed_low_one, grad_triple)
    column_sums = jnp.sum(grad_triple.astype(F32), axis=0)
    grad_pair = jnp.concatenate([column_sums[:feat_dim], column_sums[2 * feat_dim :]])
    grad_normed_one = back_dot(grad_triple, w_qkv)
    grad_input, grad_gain_one, grad_shift_one = norm_back(grad_normed_one, normed_one, inverse_one, ln1_gain)
    grad_input = (grad_input + grad_middle).reshape(images, seq_len, feat_dim)
    grads = (
        grad_gain_one, grad_shift_one, grad_qkv, grad_pair, grad_proj, grad_proj_bias,
        grad_gain_two, grad_shift_two, grad_fc1, grad_fc1_bias, grad_fc2, grad_fc2_bias,
    )
    return layer_out, grad_input, grads


def pack_rows(shards):
    rows = []
    for v in shards:
        v = v.astype(F32)
        pieces = 2 if v.shape[-1] > 128 else 1
        w = v.shape[-1] // pieces
        for k in range(pieces):
            piece = v[..., k * w : (k + 1) * w]
            rows.append(jnp.pad(piece, [(0, 0)] * (v.ndim - 1) + [(0, 128 - w)]))
    while len(rows) < 16:
        rows.append(jnp.zeros_like(rows[0]))
    return jnp.stack(rows, axis=-2)


def unpack_rows(pack, widths):
    out, row = [], 0
    for w in widths:
        pieces = 2 if w > 128 else 1
        out.append(jnp.concatenate([pack[..., row + k, : w // pieces] for k in range(pieces)], axis=-1))
        row += pieces
    return out


def by_block(tokens, grids, keep_attn, keep_mlp, cotangent, *params):
    smalls = [p for p in params if p.ndim == 1]
    widths = [p.shape[0] for p in smalls]
    g_qkv, g_proj, g_fc1, g_fc2, packs = gather_weights(params[2], params[4], params[8], params[10], pack_rows(smalls))
    full = [v.reshape(-1) for v in unpack_rows(packs, widths)]
    whole = (full[0], full[1], g_qkv, full[2], g_proj, full[3], full[4], full[5], g_fc1, full[6], g_fc2, full[7])
    layer_out, grad_input, grads = layer(tokens, grids, keep_attn, keep_mlp, cotangent, whole)
    gsmall = pack_rows([g.reshape(16, -1) for g in grads if g.ndim == 1])
    o_qkv, o_proj, o_fc1, o_fc2, o_small = scatter_grads(grads[2], grads[4], grads[8], grads[10], gsmall)
    sm = unpack_rows(o_small, widths)
    return (layer_out, grad_input, sm[0], sm[1], o_qkv, sm[2], o_proj, sm[3], sm[4], sm[5], o_fc1, sm[6], o_fc2, sm[7])


def by_collectives(tokens, grids, keep_attn, keep_mlp, cotangent, *params):
    whole = [lax.all_gather(p, "fsdp", axis=0, tiled=True) for p in params]
    whole = [p.astype(F32) if p.ndim == 1 else p for p in whole]
    layer_out, grad_input, grads = layer(tokens, grids, keep_attn, keep_mlp, cotangent, whole)
    shards = [lax.psum_scatter(g, "fsdp", scatter_dimension=0, tiled=True) for g in grads]
    totals = [lax.psum(g.astype(BF16), "rep").astype(F32) for g in shards]
    return (layer_out, grad_input) + tuple(totals)


def solution(mesh):
    vec, mat, rows = P("fsdp"), P("fsdp", None), P(("rep", "fsdp"))
    image = P(("rep", "fsdp"), None, None)
    weights = (vec, vec, mat, vec, mat, vec, vec, vec, mat, vec, mat, vec)
    in_specs = (image, P(("rep", "fsdp"), None), rows, rows, image) + weights
    out_specs = (image, image) + weights
    block = mesh.shape["fsdp"] == 16 and mesh.shape["rep"] == 2
    return jax.shard_map(
        by_block if block else by_collectives, mesh=mesh, in_specs=in_specs, out_specs=out_specs, check_vma=False
    )
```

```python
import functools

import jax
import jax.numpy as jnp
from jax import lax
from jax.experimental import pallas as pl
from jax.experimental.pallas import tpu as pltpu
from jax.sharding import PartitionSpec as P

HEAD = 64
MESH = pl.DeviceIdType.MESH
F32 = jnp.float32
BF16 = jnp.bfloat16
epsilon = 1e-06
root_half = 0.7071067811865476

ROWS = 48
WIDE = 768
HALF = 384


class Place:
    def __init__(self):
        self.r = lax.axis_index("rep")
        self.i = lax.axis_index("fsdp")
        r, i = self.r, self.i
        self.z = i // 4
        self.y = (i // 2) % 2
        self.x = i % 2
        fx, fy = 1 - 2 * self.x, 1 - 2 * self.y
        self.to_a = i + (1 - r) * fx + r * 2 * fy
        self.to_b = i + (1 - r) * 2 * fy + r * fx
        self.own = (self.y, self.x)
        self.col_a = (self.y + r * fy, self.x + (1 - r) * fx)
        self.col_b = (self.y + (1 - r) * fy, self.x + r * fx)
        self.col_ab = (1 - self.y, 1 - self.x)

    def z_dev(self, k):
        zz = (self.z + k) % 4
        return zz, (self.r, zz * 4 + self.i % 4)

    @property
    def dev_a(self):
        return (self.r, self.to_a)

    @property
    def dev_b(self):
        return (self.r, self.to_b)

    @property
    def dev_d(self):
        return (1 - self.r, self.i)


def greet(place):
    barrier = pltpu.get_barrier_semaphore()
    for dev in (place.z_dev(1)[1], place.z_dev(2)[1], place.z_dev(3)[1], place.dev_a, place.dev_b, place.dev_d):
        pl.semaphore_signal(barrier, inc=1, device_id=dev, device_id_type=MESH)
    pl.semaphore_wait(barrier, 6)


def remote(src, dst, send, recv, dev):
    return pltpu.make_async_remote_copy(
        src_ref=src, dst_ref=dst, send_sem=send, recv_sem=recv, device_id=dev, device_id_type=MESH
    )


class Gather:
    def __init__(self, place, part, own, send, recv, local, halves=True):
        self.p, self.part, self.own = place, part, own
        self.send, self.recv, self.local, self.halves = send, recv, local, halves

    def _z(self, k):
        p = self.p
        _, dev = p.z_dev(k)
        return remote(
            self.own(p.r), self.part(p.z, *p.own, p.r), self.send.at[k - 1], self.recv.at[k - 1], dev
        )

    def _col(self, col, slot, dev):
        piece = self.part(slice(None), *col, self.p.r)
        return remote(piece, piece, self.send.at[slot], self.recv.at[slot], dev)

    def _keep(self):
        p = self.p
        return pltpu.make_async_copy(self.own(p.r), self.part(p.z, *p.own, p.r), self.local)

    def start(self):
        self._keep().start()
        for k in (1, 2, 3):
            self._z(k).start()

    def after_z(self):
        p = self.p
        self._keep().wait()
        for k in (1, 2, 3):
            self._z(k).wait_recv()
        self._col(p.own, 3, p.dev_a).start()
        self._col(p.own, 4, p.dev_b).start()
        if self.halves:
            self._col(p.own, 6, p.dev_d).start()

    def after_a(self):
        p = self.p
        self._col(p.own, 3, p.dev_a).wait_recv()
        self._col(p.col_a, 5, p.dev_b).start()
        if self.halves:
            self._col(p.col_a, 7, p.dev_d).start()

    def after_b(self):
        p = self.p
        self._col(p.own, 4, p.dev_b).wait_recv()
        if self.halves:
            self._col(p.col_b, 8, p.dev_d).start()
        self._col(p.own, 5, p.dev_b).wait_recv()
        if self.halves:
            self._col(p.col_ab, 9, p.dev_d).start()

    def done(self):
        p = self.p
        if self.halves:
            for slot in (6, 7, 8, 9):
                self._col(p.own, slot, p.dev_d).wait_recv()

    def drain(self):
        p = self.p
        for k in (1, 2, 3):
            self._z(k).wait_send()
        for slot in range(3, 10 if self.halves else 6):
            self._col(p.own, slot, p.dev_d).wait_send()


def add_into(dst, src, rows):
    dst[...] = (dst[...].astype(F32) + src[...].astype(F32)).astype(dst.dtype)


class Scatter:
    def __init__(self, place, part, bufs, out, send, recv, plane=None):
        self.p, self.part, self.out, self.plane = place, part, out, plane
        self.dbuf, self.bbuf, self.abuf, self.zbuf = bufs
        self.send, self.recv = send, recv

    def _d(self, zz):
        p = self.p
        return remote(
            self.part(zz, slice(None), slice(None), 1 - p.r), self.dbuf.at[zz], self.send.at[zz], self.recv.at[zz], p.dev_d
        )

    def _b(self, slot):
        p = self.p
        col = (p.col_b, p.col_ab)[slot]
        return remote(
            self.part(slice(None), *col, p.r), self.bbuf.at[slot], self.send.at[4 + slot], self.recv.at[4 + slot], p.dev_b
        )

    def _a(self):
        p = self.p
        return remote(self.part(slice(None), *p.col_a, p.r), self.abuf, self.send.at[6], self.recv.at[6], p.dev_a)

    def _z(self, k):
        p = self.p
        zz, dev = p.z_dev(k)
        mine = zz if self.plane is None else slice(None)
        return remote(
            self.part(mine, *p.own, p.r), self.zbuf.at[k - 1], self.send.at[6 + k], self.recv.at[6 + k], dev
        )

    def _each_z(self, act):
        p = self.p
        for k in (1, 2, 3):
            if self.plane is None:
                act(k)
            else:
                pl.when(p.z == (self.plane + 4 - k) % 4)(functools.partial(act, k))

    def _here(self, act):
        if self.plane is None:
            act()
        else:
            pl.when(self.p.z == self.plane)(act)

    def _f(self):
        p = self.p
        return remote(self.out(p.r), self.out(p.r), self.send.at[10], self.recv.at[10], p.dev_d)

    def start(self):
        for zz in range(4):
            self._d(zz).start()

    def after_d(self):
        p = self.p
        for zz in range(4):
            self._d(zz).wait_recv()
        for slot, col in enumerate((p.col_b, p.col_ab, p.col_a, p.own)):
            for zz in range(4):
                add_into(self.part(zz, *col, p.r), self.dbuf.at[(zz,) + col], ROWS)
            if slot < 2:
                self._b(slot).start()

    def after_b(self):
        p = self.p
        self._b(1).wait_recv()
        for zz in range(4):
            add_into(self.part(zz, *p.col_a, p.r), self.bbuf.at[1, zz], ROWS)
        self._a().start()
        self._b(0).wait_recv()
        for zz in range(4):
            add_into(self.part(zz, *p.own, p.r), self.bbuf.at[0, zz], ROWS)

    def after_a(self):
        p = self.p
        self._a().wait_recv()
        for zz in range(4):
            add_into(self.part(zz, *p.own, p.r), self.abuf.at[zz], ROWS)
        self._each_z(lambda k: self._z(k).start())

    def _finish(self):
        p = self.p
        for k in (1, 2, 3):
            self._z(k).wait_recv()
        total = self.part(p.z if self.plane is None else slice(None), *p.own, p.r)[...].astype(F32)
        for k in range(3):
            total = total + self.zbuf[k].astype(F32)
        self.out(p.r)[...] = total
        self._f().start()

    def after_z(self):
        self._here(self._finish)

    def done(self):
        self._here(lambda: self._f().wait_recv())

    def drain(self):
        for zz in range(4):
            self._d(zz).wait_send()
        for slot in range(2):
            self._b(slot).wait_send()
        self._a().wait_send()
        self._each_z(lambda k: self._z(k).wait_send())
        self._here(lambda: self._f().wait_send())


class ScatterSmall:
    def __init__(self, place, ref, bufs, out, send, recv):
        self.p, self.ref, self.out = place, ref, out
        self.bbuf, self.abuf, self.zbuf, self.fbuf = bufs
        self.send, self.recv = send, recv

    def _b(self, slot):
        p = self.p
        col = (p.col_b, p.col_ab)[slot]
        return remote(self.ref.at[(slice(None),) + col], self.bbuf.at[slot], self.send.at[slot], self.recv.at[slot], p.dev_b)

    def _a(self):
        p = self.p
        return remote(self.ref.at[(slice(None),) + p.col_a], self.abuf, self.send.at[2], self.recv.at[2], p.dev_a)

    def _z(self, k):
        p = self.p
        zz, dev = p.z_dev(k)
        return remote(self.ref.at[(zz,) + p.own], self.zbuf.at[k - 1], self.send.at[2 + k], self.recv.at[2 + k], dev)

    def _f(self):
        p = self.p
        return remote(self.out, self.fbuf, self.send.at[6], self.recv.at[6], p.dev_d)

    def start(self):
        self._b(0).start()
        self._b(1).start()

    def after_b(self):
        p = self.p
        self._b(0).wait_recv()
        self._b(1).wait_recv()
        self.ref[(slice(None),) + p.col_a] += self.bbuf[1]
        self.ref[(slice(None),) + p.own] += self.bbuf[0]
        self._a().start()

    def after_a(self):
        p = self.p
        self._a().wait_recv()
        self.ref[(slice(None),) + p.own] += self.abuf[...]
        for k in (1, 2, 3):
            self._z(k).start()

    def after_z(self):
        p = self.p
        for k in (1, 2, 3):
            self._z(k).wait_recv()
        self.out[...] = self.ref[(p.z,) + p.own] + self.zbuf[0] + self.zbuf[1] + self.zbuf[2]
        self._f().start()

    def done(self):
        self._f().wait_recv()
        self._f().wait_send()
        self.out[...] = self.out[...] + self.fbuf[...]

    def drain(self):
        self._b(0).wait_send()
        self._b(1).wait_send()
        self._a().wait_send()
        for k in (1, 2, 3):
            self._z(k).wait_send()


ROWS_ALL = 768
IMAGE = 384
KEYS = 288
ALWAYS = 192
SLOTS = 4
LAG_B, LAG_A, LAG_Z = 3, 5, 6
NT = (((1,), (1,)), ((), ()))
TN = (((0,), (0,)), ((), ()))


def dots(a, b, dims=None):
    if dims is None:
        return jnp.dot(a, b, preferred_element_type=F32)
    return lax.dot_general(a, b, dims, preferred_element_type=F32)


def tiles(count, size, body):
    def step(t, carry):
        body(t, pl.ds(pl.multiple_of(t * size, size), size))
        return carry

    lax.fori_loop(0, count, step, 0)


def moments(v):
    centre = v - jnp.mean(v, axis=-1, keepdims=True)
    inverse = lax.rsqrt(jnp.mean(centre * centre, axis=-1, keepdims=True) + epsilon)
    return centre * inverse, inverse


def half(core):
    return pl.ds(pl.multiple_of(core * HALF, 128), HALF)


def layer_kernel(
    tokens, cot, grids, keep_a, keep_m, g1, s1, bqv, bp, g2, s2, b1, b2, wq, wp, w1, w2,
    out_h, gt_h, oq, op, o1, o2, og1, os1, obqv, obp, og2, os2, ob1, ob2,
    x, ct, dz, h1, qkv, probs, mixed, y1, h2, dact, act, acc, dh,
    gu, gw2, stage, pack, packs, vec, vqkv, vb1, dvec, dbqv, db1, outq, smalls, opack,
    dbuf, bbuf, abuf, zbuf, zplane, sb, sa, sz, sf,
    gsend, grecv, glocal, tsend, trecv, tlocal, ssend, srecv, usend, urecv, local,
):
    place = Place()
    r = place.r
    load_x = pltpu.make_async_copy(tokens, x, local.at[0])
    load_c = pltpu.make_async_copy(cot, ct, local.at[1])
    load_x.start()
    load_c.start()
    pack[...] = jnp.zeros_like(pack)
    for row, ref in enumerate((g1, s1, bp, g2, s2, b2)):
        pack[row : row + 1, 0:48] = ref[...].astype(F32).reshape(1, 48)
    pack[6:7, 0:96] = bqv[...].astype(F32).reshape(1, 96)
    both = b1[...].astype(F32).reshape(1, 192)
    pack[7:8, 0:96] = both[:, :96]
    pack[8:9, 0:96] = both[:, 96:]
    for g in range(3):
        for k in range(3):
            stage[g, :, 256 * k : 256 * k + 256] = wq[:, 768 * k + 256 * g : 768 * k + 256 * g + 256]
    dvec[...] = jnp.zeros_like(dvec)
    dbqv[...] = jnp.zeros_like(dbqv)
    greet(place)

    tiny = Gather(place, lambda zs, y, xx, core: packs.at[zs, y, xx], lambda core: pack, tsend, trecv, tlocal, halves=False)

    def block(u):
        return lambda zs, y, xx, core: gu.at[u, zs, y, xx, :, half(core)]

    def rows_of(t):
        return lambda zs, y, xx, core: gw2.at[zs, y, xx, t, :, half(core)]

    parts = [block(u) for u in range(4)] + [rows_of(t) for t in range(4)] + [block(4 + j) for j in range(4)]
    owns = (
        [lambda core, g=g: stage.at[g, :, half(core)] for g in range(3)]
        + [lambda core: wp.at[:, half(core)]]
        + [lambda core, t=t: w2.at[t, :, half(core)] for t in range(4)]
        + [lambda core, j=j: w1.at[:, pl.ds(pl.multiple_of(WIDE * j + core * HALF, 128), HALF)] for j in range(4)]
    )
    units = [Gather(place, parts[n], owns[n], gsend.at[n], grecv.at[n], glocal.at[n]) for n in range(12)]

    def step(s):
        if s + 4 < 12:
            units[s + 4].start()
        if s + 1 < 12:
            units[s + 1].after_z()
        if s < 12:
            units[s].after_a()
        if 0 <= s - 1 < 12:
            units[s - 1].after_b()

    tiny.start()
    for u in range(4):
        units[u].start()
    tiny.after_z()
    units[0].after_z()
    tiny.after_a()
    step(0)
    tiny.after_b()
    for s in range(16):
        at = (s // 4, (s // 2) % 2, s % 2)
        vec[:, 48 * s : 48 * s + 48] = packs[at + (slice(0, 8), slice(0, 48))]
        vb1[:, 192 * s : 192 * s + 96] = packs[at + (slice(7, 8), slice(0, 96))]
        vb1[:, 192 * s + 96 : 192 * s + 192] = packs[at + (slice(8, 9), slice(0, 96))]
        col = 96 * s
        vqkv[:, col + 768 * (s // 8) : col + 768 * (s // 8) + 96] = packs[at + (slice(6, 7), slice(0, 96))]
    vqkv[:, 768:1536] = jnp.zeros((1, 768), F32)

    load_x.wait()

    def norm_one(t, rows):
        n, _ = moments(x[rows, :].astype(F32))
        h1[rows, :] = (n * vec[0:1, :] + vec[1:2, :]).astype(BF16)

    tiles(6, 128, norm_one)
    step(1)

    lane = lax.broadcasted_iota(jnp.int32, (1, 128), 1) // HEAD

    def pair(g, b, p2):
        at = [pl.ds(pl.multiple_of(256 * k + 128 * p2, 128), 128) for k in range(3)]
        q = qkv[g, pl.ds(IMAGE * b, IMAGE), at[0]] * BF16(0.125)
        k = qkv[g, pl.ds(IMAGE * b, KEYS), at[1]]
        v = qkv[g, pl.ds(IMAGE * b, KEYS), at[2]]
        return at, q, k, v

    def attend(g, b):
        length = grids[b, 0] * grids[b, 1] + 2
        key = lax.broadcasted_iota(jnp.int32, (KEYS - ALWAYS, IMAGE), 0) + ALWAYS

        def body(p2, carry):
            at, q, k, v = pair(g, b, p2)
            total = None
            for h in range(2):
                qh = jnp.where(lane == h, q, BF16(0))
                vh = jnp.where(lane == h, v, BF16(0))
                s = dots(k, qh, NT)
                s = jnp.concatenate([s[:ALWAYS], jnp.where(key < length, s[ALWAYS:], -1000000000.0)], axis=0)
                e = jnp.exp(s - jnp.max(s, axis=0, keepdims=True))
                p = (e * (1.0 / jnp.sum(e, axis=0, keepdims=True))).astype(BF16)
                probs[8 * g + 4 * b + 2 * p2 + h] = p
                o = dots(p, vh, TN)
                total = o if total is None else total + o
            mixed[pl.ds(IMAGE * b, IMAGE), pl.ds(pl.multiple_of(256 * g + 128 * p2, 128), 128)] = total.astype(BF16)
            return carry

        lax.fori_loop(0, 2, body, 0)

    step(2)
    for g in range(3):
        units[g].done()
        bias = jnp.concatenate([vqkv[:, 768 * k + 256 * g : 768 * k + 256 * g + 256] for k in range(3)], axis=1)
        qkv[g] = (dots(h1[...], gu[g].reshape(768, 768)) + bias).astype(BF16)
        attend(g, 0)
        if g > 0:
            step(g + 2)
        attend(g, 1)

    units[3].done()
    whole_p = gu[3].reshape(768, 768)
    keep = [keep_a[b].astype(F32) * (1.0 / 0.9) for b in range(2)]
    kmlp = [keep_m[b].astype(F32) * (1.0 / 0.9) for b in range(2)]
    for b in range(2):
        rows = pl.ds(IMAGE * b, IMAGE)
        y = x[rows, :].astype(F32) + keep[b] * (dots(mixed[rows, :], whole_p) + vec[2:3, :])
        y1[rows, :] = y
        n, _ = moments(y)
        h2[rows, :] = (n * vec[3:4, :] + vec[4:5, :]).astype(BF16)
    step(5)
    load_c.wait()

    def scale_dz(t, rows):
        d = (ct[rows, :].astype(F32) * (keep_m[t // 3].astype(F32) * (1.0 / 0.9))).astype(BF16)
        dz[rows, :] = d
        dvec[5:6, :] += jnp.sum(d.astype(F32), axis=0, keepdims=True)

    tiles(6, 128, scale_dz)
    for s in (6, 7, 8):
        step(s)
    for u in range(4, 8):
        units[u].done()
        if u == 6:
            step(9)

    def plane_part(j):
        return lambda zs, y, xx, core: gw2.at[j, y, xx, zs, :, half(core)]

    def gq_part(g):
        return lambda zs, y, xx, core: dact.at[g, zs, y, xx, :, half(core)]

    plans = []
    for j in range(4):
        plans.append((plane_part(j), zplane, lambda core: o2.at[:, :, half(core)], j))
        plans.append((block(4 + j), zbuf.at[j], lambda core, j=j: o1.at[:, pl.ds(pl.multiple_of(WIDE * j + core * HALF, 128), HALF)], None))
    plans.append((block(3), zbuf.at[4], lambda core: op.at[:, half(core)], None))
    for g in range(3):
        plans.append((gq_part(g), zbuf.at[5 + g], lambda core, g=g: outq.at[g, :, half(core)], None))
    sends = [
        Scatter(place, part, (dbuf.at[n % SLOTS], bbuf.at[n], abuf.at[n], zb), out, ssend.at[n], srecv.at[n], plane)
        for n, (part, zb, out, plane) in enumerate(plans)
    ]

    def slot(n):
        if n < 12:
            sends[n].start()
        if 0 <= n - 1 < 12:
            sends[n - 1].after_d()
        if 0 <= n - LAG_B < 12:
            sends[n - LAG_B].after_b()
        if 0 <= n - LAG_A < 12:
            sends[n - LAG_A].after_a()
        if 0 <= n - LAG_Z < 12:
            sends[n - LAG_Z].after_z()

    acc[...] = jnp.zeros_like(acc)
    dh[...] = jnp.zeros_like(dh)
    for j in range(4):
        dact[j] = dots(dz[...], gw2[j].reshape(768, 768), NT).astype(BF16).reshape(4, 2, 2, ROWS, 768)
    for u in range(3, 8):
        units[u].drain()
    for j in range(4):
        units[8 + j].done()
        w = gu[4 + j].reshape(768, 768)
        pre = dots(h2[...], w) + vb1[:, 768 * j : 768 * j + 768]
        u = 0.5 * (1.0 + lax.erf(pre * root_half))
        a = (pre * u).astype(BF16)
        act[...] = a
        d = dact[j].reshape(768, 768).astype(F32) * (u + pre * jnp.exp(-0.5 * pre * pre) * 0.3989422804014327)
        db1[j] = jnp.sum(d, axis=0, keepdims=True)
        d = d.astype(BF16)
        dact[j] = d.reshape(4, 2, 2, ROWS, 768)
        acc[...] += dots(a, gw2[j].reshape(768, 768))
        if j < 2:
            step(10 + 2 * j)
        gw2[j] = dots(act[...], dz[...], TN).astype(BF16).reshape(2, 2, 4, ROWS, 768)
        slot(2 * j)
        dh[...] += dots(dact[j].reshape(768, 768), gu[4 + j].reshape(768, 768), NT)
        units[8 + j].drain()
        gu[4 + j] = dots(h2[...], dact[j].reshape(768, 768), TN).astype(BF16).reshape(4, 2, 2, ROWS, 768)
        if j < 1:
            step(11)
        slot(2 * j + 1)

    def norm_two_back(t, rows):
        b = t // 3
        y = y1[rows, :]
        act[rows, :] = (y + keep_m[b].astype(F32) * (1.0 / 0.9) * (acc[rows, :] + vec[5:6, :])).astype(BF16)
        n, inverse = moments(y)
        d = dh[rows, :]
        e = d * vec[3:4, :]
        back = inverse * (e - jnp.mean(e, axis=-1, keepdims=True) - n * jnp.mean(e * n, axis=-1, keepdims=True))
        back = ct[rows, :].astype(F32) + back
        dh[rows, :] = back
        da = (back * (keep_a[b].astype(F32) * (1.0 / 0.9))).astype(BF16)
        h2[rows, :] = da
        dvec[3:4, :] += jnp.sum(d * n, axis=0, keepdims=True)
        dvec[4:5, :] += jnp.sum(d, axis=0, keepdims=True)
        dvec[2:3, :] += jnp.sum(da.astype(F32), axis=0, keepdims=True)

    tiles(6, 128, norm_two_back)
    save_out = pltpu.make_async_copy(act, out_h, local.at[2])
    save_out.start()
    dz[...] = dots(h2[...], gu[3].reshape(768, 768), NT).astype(BF16)
    gu[3] = dots(mixed[...], h2[...], TN).astype(BF16).reshape(4, 2, 2, ROWS, 768)
    slot(8)

    def attend_back(g, b):
        def body(p2, carry):
            at, q, k, v = pair(g, b, p2)
            col = pl.ds(pl.multiple_of(256 * g + 128 * p2, 128), 128)
            do = dz[pl.ds(IMAGE * b, IMAGE), col]
            dq = dk = dv = None
            for h in range(2):
                qh = jnp.where(lane == h, q, BF16(0))
                kh = jnp.where(lane == h, k, BF16(0))
                doh = jnp.where(lane == h, do, BF16(0))
                p = probs[8 * g + 4 * b + 2 * p2 + h]
                pf = p.astype(F32)
                dp = dots(v, doh, NT)
                ds = (pf * (dp - jnp.sum(pf * dp, axis=0, keepdims=True))).astype(BF16)
                new = (dots(ds, kh, TN), dots(ds, qh), dots(p, doh))
                dq, dk, dv = new if dq is None else (dq + new[0], dk + new[1], dv + new[2])
            dq = dq * 0.125
            qkv[g, pl.ds(IMAGE * b, IMAGE), at[0]] = dq.astype(BF16)
            qkv[g, pl.ds(IMAGE * b, KEYS), at[1]] = dk.astype(BF16)
            qkv[g, pl.ds(IMAGE * b, KEYS), at[2]] = dv.astype(BF16)
            none = jnp.zeros((IMAGE - KEYS, 128), BF16)
            qkv[g, pl.ds(IMAGE * b + KEYS, IMAGE - KEYS), at[1]] = none
            qkv[g, pl.ds(IMAGE * b + KEYS, IMAGE - KEYS), at[2]] = none
            dbqv[0, :, col] += jnp.sum(dq, axis=0, keepdims=True)
            dbqv[1, :, col] += jnp.sum(dv, axis=0, keepdims=True)
            return carry

        lax.fori_loop(0, 2, body, 0)

    for g in range(3):
        attend_back(g, 0)
        attend_back(g, 1)
        dact[g] = dots(h1[...], qkv[g], TN).astype(BF16).reshape(4, 2, 2, ROWS, 768)
        slot(9 + g)
        grown = dots(qkv[g], gu[g].reshape(768, 768), NT)
        if g == 0:
            acc[...] = grown
        else:
            acc[...] += grown

    def norm_one_back(t, rows):
        n, inverse = moments(x[rows, :].astype(F32))
        d = acc[rows, :]
        e = d * vec[0:1, :]
        back = inverse * (e - jnp.mean(e, axis=-1, keepdims=True) - n * jnp.mean(e * n, axis=-1, keepdims=True))
        dh[rows, :] += back
        dvec[0:1, :] += jnp.sum(d * n, axis=0, keepdims=True)
        dvec[1:2, :] += jnp.sum(d, axis=0, keepdims=True)

    tiles(6, 128, norm_one_back)
    save_gt = pltpu.make_async_copy(dh, gt_h, local.at[3])
    save_gt.start()
    smalls[...] = jnp.zeros_like(smalls)
    for s in range(16):
        at = (s // 4, (s // 2) % 2, s % 2)
        smalls[at + (slice(0, 8), slice(0, 48))] = dvec[:, 48 * s : 48 * s + 48]
        c = 96 * (s % 8)
        smalls[at + (slice(6, 7), slice(0, 96))] = dbqv[s // 8, :, c : c + 96]
        c = 192 * (s % 4)
        smalls[at + (slice(7, 8), slice(0, 96))] = db1[s // 4, :, c : c + 96]
        smalls[at + (slice(8, 9), slice(0, 96))] = db1[s // 4, :, c + 96 : c + 192]
    small = ScatterSmall(place, smalls, (sb, sa, sz, sf), opack, usend, urecv)
    small.start()
    slot(12)
    small.after_b()
    slot(13)
    small.after_a()
    slot(14)
    small.after_z()
    for n in range(15, 12 + LAG_Z):
        slot(n)
    small.done()
    for unit in sends:
        unit.done()
    for g in range(3):
        for k in range(3):
            oq[:, 768 * k + 256 * g : 768 * k + 256 * g + 256] = outq[g, :, 256 * k : 256 * k + 256]
    for row, ref in enumerate((og1, os1, obp, og2, os2, ob2)):
        ref[...] = opack[row : row + 1, 0:48].reshape(48)
    obqv[...] = opack[6:7, 0:96].reshape(96)
    ob1[...] = jnp.concatenate([opack[7:8, 0:96], opack[8:9, 0:96]], axis=1).reshape(192)
    for unit in [units[0], units[1], units[2], tiny, small] + sends:
        unit.drain()
    save_out.wait()
    save_gt.wait()


def by_block(tokens, grids, keep_attn, keep_mlp, cotangent, *params):
    g1, s1, wq, bqv, wp, bp, g2, s2, w1, b1, w2, b2 = params
    flat = lambda v: v.reshape(ROWS_ALL, 768)
    vm, sm, hbm = (pl.BlockSpec(memory_space=m) for m in (pltpu.VMEM, pltpu.SMEM, pltpu.HBM))
    S = jax.ShapeDtypeStruct
    v = lambda *shape: pltpu.VMEM(shape, BF16)
    f = lambda *shape: pltpu.VMEM(shape, F32)
    dma = lambda *shape: pltpu.SemaphoreType.DMA(shape)
    outs = pl.pallas_call(
        layer_kernel,
        out_shape=[S((ROWS_ALL, 768), BF16), S((ROWS_ALL, 768), F32)]
        + [S(w.shape, F32) for w in (wq, wp, w1)]
        + [S((4, ROWS, 768), F32)]
        + [S(w.shape, F32) for w in (g1, s1, bqv, bp, g2, s2, b1, b2)],
        in_specs=[hbm] * 2 + [sm] * 3 + [vm] * 12,
        out_specs=[hbm] * 2 + [vm] * 12,
        scratch_shapes=[
            v(768, 768), v(768, 768), v(768, 768), v(768, 768), v(3, 768, 768), v(24, KEYS, IMAGE), v(768, 768), f(768, 768),
            v(768, 768), v(4, 4, 2, 2, ROWS, 768), v(768, 768), f(768, 768), f(768, 768),
            v(8, 4, 2, 2, ROWS, 768), v(4, 2, 2, 4, ROWS, 768), v(3, ROWS, 768), f(16, 128), f(4, 2, 2, 16, 128),
            f(8, 768), f(1, 2304), f(1, 3072), f(8, 768), f(2, 1, 768), f(4, 1, 768), f(3, ROWS, 768), f(4, 2, 2, 16, 128), f(16, 128),
            v(SLOTS, 4, 2, 2, ROWS, HALF), v(12, 2, 4, ROWS, HALF), v(12, 4, ROWS, HALF), v(8, 3, ROWS, HALF), v(3, 4, ROWS, HALF),
            f(2, 4, 16, 128), f(4, 16, 128), f(3, 16, 128), f(16, 128),
            dma(12, 10), dma(12, 10), dma(12), dma(6), dma(6), dma(), dma(12, 11), dma(12, 11), dma(7), dma(7), dma(4),
        ],
        compiler_params=pltpu.CompilerParams(collective_id=0, has_side_effects=True, vmem_limit_bytes=62 << 20),
        cost_estimate=pl.CostEstimate(flops=36 * 10**9, bytes_accessed=10**7, transcendentals=10**7),
        name="layer",
    )(
        flat(tokens), flat(cotangent), grids, keep_attn, keep_mlp, g1, s1, bqv, bp, g2, s2, b1, b2, wq, wp, w1,
        w2.reshape(4, ROWS, 768),
    )
    out, gt, oq, op, o1, o2, og1, os1, obqv, obp, og2, os2, ob1, ob2 = outs
    return (
        out.reshape(tokens.shape), gt.reshape(tokens.shape), og1, os1, oq, obqv, op, obp, og2, os2, o1, ob1,
        o2.reshape(w2.shape), ob2,
    )


def layer_norm(stream, gain, shift):
    center = jnp.mean(stream, axis=-1, keepdims=True)
    shifted = stream - center
    inverse = lax.rsqrt(jnp.mean(shifted * shifted, axis=-1, keepdims=True) + epsilon)
    normed = shifted * inverse
    return (normed * gain + shift, normed, inverse)


def norm_back(grad_normed, normed, inverse, gain):
    scaled = grad_normed * gain
    grad_input = inverse * (
        scaled
        - jnp.mean(scaled, axis=-1, keepdims=True)
        - normed * jnp.mean(scaled * normed, axis=-1, keepdims=True)
    )
    return (grad_input, jnp.sum(grad_normed * normed, axis=0), jnp.sum(grad_normed, axis=0))


def gelu_exact(values):
    return 0.5 * values * (1.0 + lax.erf(values * root_half))


def outer_sum(left, right):
    return lax.dot_general(left, right, (((0,), (0,)), ((), ())), preferred_element_type=F32)


def back_dot(left, right):
    return lax.dot_general(left, right, (((1,), (1,)), ((), ())), preferred_element_type=F32)


def layer(tokens, grids, keep_attn, keep_mlp, cotangent, params):
    ln1_gain, ln1_shift, w_qkv, bias_qv, w_proj, bias_proj, ln2_gain, ln2_shift, w_fc1, bias_fc1, w_fc2, bias_fc2 = params
    images, seq_len, feat_dim = tokens.shape
    num_heads = feat_dim // HEAD
    row_count = images * seq_len
    lengths = grids[:, 0] * grids[:, 1] + 2
    key_valid = lax.broadcasted_iota(jnp.int32, (images, seq_len), 1) < lengths[:, None]
    scale_attn = jnp.broadcast_to((keep_attn.astype(F32) / 0.9)[:, None], (images, seq_len)).reshape(row_count, 1)
    scale_mlp = jnp.broadcast_to((keep_mlp.astype(F32) / 0.9)[:, None], (images, seq_len)).reshape(row_count, 1)
    stream = tokens.astype(F32).reshape(row_count, feat_dim)
    normed_out, normed_one, inverse_one = layer_norm(stream, ln1_gain, ln1_shift)
    normed_low_one = normed_out.astype(BF16)
    full_bias = jnp.concatenate([bias_qv[:feat_dim], jnp.zeros((feat_dim,), F32), bias_qv[feat_dim:]])
    triple = jnp.dot(normed_low_one, w_qkv, preferred_element_type=F32) + full_bias
    triple = triple.astype(BF16).reshape(images, seq_len, 3, num_heads, HEAD)
    queries, key_rows, values = triple[:, :, 0], triple[:, :, 1], triple[:, :, 2]
    scores = jnp.einsum("bqhe,bkhe->bhqk", queries, key_rows, preferred_element_type=F32) * 0.125
    scores = jnp.where(key_valid[:, None, None, :], scores, -1000000000.0)
    probs_full = jax.nn.softmax(scores, axis=-1)
    probs_low = probs_full.astype(BF16)
    mixed_low = jnp.einsum("bhqk,bkhe->bqhe", probs_low, values, preferred_element_type=F32)
    mixed_low = mixed_low.reshape(row_count, feat_dim).astype(BF16)
    branch = jnp.dot(mixed_low, w_proj, preferred_element_type=F32) + bias_proj
    middle = stream + scale_attn * branch
    normed_out, normed_two, inverse_two = layer_norm(middle, ln2_gain, ln2_shift)
    normed_low_two = normed_out.astype(BF16)
    pre_act = jnp.dot(normed_low_two, w_fc1, preferred_element_type=F32) + bias_fc1
    act_value, act_pullback = jax.vjp(gelu_exact, pre_act)
    act_low = act_value.astype(BF16)
    branch_two = jnp.dot(act_low, w_fc2, preferred_element_type=F32) + bias_fc2
    layer_out = (middle + scale_mlp * branch_two).astype(BF16).reshape(images, seq_len, feat_dim)
    grad_out = cotangent.astype(F32).reshape(row_count, feat_dim)
    grad_branch_two = (grad_out * scale_mlp).astype(BF16)
    grad_fc2 = outer_sum(act_low, grad_branch_two)
    grad_fc2_bias = jnp.sum(grad_branch_two.astype(F32), axis=0)
    grad_act = back_dot(grad_branch_two, w_fc2)
    grad_pre = act_pullback(grad_act)[0].astype(BF16)
    grad_fc1 = outer_sum(normed_low_two, grad_pre)
    grad_fc1_bias = jnp.sum(grad_pre.astype(F32), axis=0)
    grad_normed_two = back_dot(grad_pre, w_fc1)
    grad_middle, grad_gain_two, grad_shift_two = norm_back(grad_normed_two, normed_two, inverse_two, ln2_gain)
    grad_middle = grad_middle + grad_out
    grad_branch = (grad_middle * scale_attn).astype(BF16)
    grad_proj = outer_sum(mixed_low, grad_branch)
    grad_proj_bias = jnp.sum(grad_branch.astype(F32), axis=0)
    grad_mixed = back_dot(grad_branch, w_proj).astype(BF16).reshape(images, seq_len, num_heads, HEAD)
    grad_values = jnp.einsum("bhqk,bqhe->bkhe", probs_low, grad_mixed, preferred_element_type=F32)
    grad_probs = jnp.einsum("bqhe,bkhe->bhqk", grad_mixed, values, preferred_element_type=F32)
    row_delta = jnp.sum(probs_full * grad_probs, axis=-1, keepdims=True)
    grad_scores = (probs_full * (grad_probs - row_delta)).astype(BF16)
    grad_queries = jnp.einsum("bhqk,bkhe->bqhe", grad_scores, key_rows, preferred_element_type=F32) * 0.125
    grad_keys = jnp.einsum("bhqk,bqhe->bkhe", grad_scores, queries, preferred_element_type=F32) * 0.125
    grad_triple = jnp.stack([grad_queries, grad_keys, grad_values], axis=2).astype(BF16).reshape(row_count, 3 * feat_dim)
    grad_qkv = outer_sum(normed_low_one, grad_triple)
    column_sums = jnp.sum(grad_triple.astype(F32), axis=0)
    grad_pair = jnp.concatenate([column_sums[:feat_dim], column_sums[2 * feat_dim :]])
    grad_normed_one = back_dot(grad_triple, w_qkv)
    grad_input, grad_gain_one, grad_shift_one = norm_back(grad_normed_one, normed_one, inverse_one, ln1_gain)
    grad_input = (grad_input + grad_middle).reshape(images, seq_len, feat_dim)
    grads = (
        grad_gain_one, grad_shift_one, grad_qkv, grad_pair, grad_proj, grad_proj_bias,
        grad_gain_two, grad_shift_two, grad_fc1, grad_fc1_bias, grad_fc2, grad_fc2_bias,
    )
    return layer_out, grad_input, grads


def by_collectives(tokens, grids, keep_attn, keep_mlp, cotangent, *params):
    whole = [lax.all_gather(p, "fsdp", axis=0, tiled=True) for p in params]
    whole = [p.astype(F32) if p.ndim == 1 else p for p in whole]
    layer_out, grad_input, grads = layer(tokens, grids, keep_attn, keep_mlp, cotangent, whole)
    shards = [lax.psum_scatter(g, "fsdp", scatter_dimension=0, tiled=True) for g in grads]
    totals = [lax.psum(g.astype(BF16), "rep").astype(F32) for g in shards]
    return (layer_out, grad_input) + tuple(totals)


def solution(mesh):
    vec, mat, rows = P("fsdp"), P("fsdp", None), P(("rep", "fsdp"))
    image = P(("rep", "fsdp"), None, None)
    weights = (vec, vec, mat, vec, mat, vec, vec, vec, mat, vec, mat, vec)
    in_specs = (image, P(("rep", "fsdp"), None), rows, rows, image) + weights
    out_specs = (image, image) + weights
    block = mesh.shape["fsdp"] == 16 and mesh.shape["rep"] == 2
    return jax.shard_map(
        by_block if block else by_collectives, mesh=mesh, in_specs=in_specs, out_specs=out_specs, check_vma=False
    )
```

```python
import functools

import jax
import jax.numpy as jnp
from jax import lax
from jax.experimental import pallas as pl
from jax.experimental.pallas import tpu as pltpu
from jax.sharding import PartitionSpec as P

HEAD = 64
MESH = pl.DeviceIdType.MESH
F32 = jnp.float32
BF16 = jnp.bfloat16
epsilon = 1e-06
root_half = 0.7071067811865476

ROWS = 48
WIDE = 768
HALF = 384
ALL = slice(None)


class Place:
    def __init__(self):
        self.r = lax.axis_index("rep")
        self.i = lax.axis_index("fsdp")
        r, i = self.r, self.i
        self.z = i // 4
        self.y = (i // 2) % 2
        self.x = i % 2
        fx, fy = 1 - 2 * self.x, 1 - 2 * self.y
        self.dev_a = (r, i + (1 - r) * fx + r * 2 * fy)
        self.dev_b = (r, i + (1 - r) * 2 * fy + r * fx)
        self.dev_d = (1 - r, i)
        self.own = (self.y, self.x)
        self.col_a = (self.y + r * fy, self.x + (1 - r) * fx)
        self.col_b = (self.y + (1 - r) * fy, self.x + r * fx)
        self.col_ab = (1 - self.y, 1 - self.x)

    def z_dev(self, k):
        zz = (self.z + k) % 4
        return zz, (self.r, zz * 4 + self.i % 4)


def greet(place):
    barrier = pltpu.get_barrier_semaphore()
    for dev in (place.z_dev(1)[1], place.z_dev(2)[1], place.z_dev(3)[1], place.dev_a, place.dev_b, place.dev_d):
        pl.semaphore_signal(barrier, inc=1, device_id=dev, device_id_type=MESH)
    pl.semaphore_wait(barrier, 6)


def remote(src, dst, send, recv, dev):
    return pltpu.make_async_remote_copy(
        src_ref=src, dst_ref=dst, send_sem=send, recv_sem=recv, device_id=dev, device_id_type=MESH
    )


class LineGather:
    def __init__(self, gather, col, base, direct=False):
        self.g, self.col, self.base, self.direct = gather, col, base, direct

    def _straight(self, src, k):
        g = self.g
        p = g.p
        piece = g.part(p.z, *self.col, p.r)
        return g._copy(piece if src is None else src, piece, self.base + k - 1, p.z_dev(k)[1])

    def _send(self, src, zz, n, step):
        g = self.g
        p = g.p
        piece = g.part(ALL if g.plane is not None else zz, *self.col, p.r)
        dev = (p.r, p.i + 4 * step)
        return g._copy(piece if src is None else src, piece, self.base + n, dev)

    def sends(self, k, act, src=None):
        z, plane = self.g.p.z, self.g.plane
        if self.direct:
            for n in (3, 2, 1) if k == 0 else ():
                act(self._straight(src, n))
        elif plane is None:
            pl.when(jnp.logical_and(z >= k, z < 3))(lambda: act(self._send(src, z - k, k, 1)))
            pl.when(jnp.logical_and(z <= 3 - k, z > 0))(lambda: act(self._send(src, z + k, 3 + k, -1)))
        else:
            if plane + k < 3:
                pl.when(z == plane + k)(lambda: act(self._send(src, z, 0, 1)))
            if plane - k > 0:
                pl.when(z == plane - k)(lambda: act(self._send(src, z, 3, -1)))

    def start(self, src):
        self.sends(0, lambda copy: copy.start(), src)

    def hop(self, k):
        z, plane = self.g.p.z, self.g.plane
        if self.direct:
            for n in (1, 2, 3) if k == 3 else ():
                self._straight(None, n).wait_recv()
        elif plane is None:
            pl.when(z >= k)(lambda: self._send(None, z, k - 1, 0).wait_recv())
            pl.when(z <= 3 - k)(lambda: self._send(None, z, 2 + k, 0).wait_recv())
        else:
            if plane + k <= 3:
                pl.when(z == plane + k)(lambda: self._send(None, z, 0, 0).wait_recv())
            if plane - k >= 0:
                pl.when(z == plane - k)(lambda: self._send(None, z, 3, 0).wait_recv())
        if k < 3:
            self.sends(k, lambda copy: copy.start())

    def drain(self):
        for k in range(3):
            self.sends(k, lambda copy: copy.wait_send())


class Gather:
    def __init__(self, place, part, own, sems, local, halves=True, wide=False, plane=None, direct=False):
        self.p, self.part, self.own, self.plane = place, part, own, plane
        self.send, self.recv = sems
        self.local, self.halves, self.wide = local, halves, wide
        self.line = LineGather(self, place.own, 10, direct)
        self.line_a = LineGather(self, place.col_a, 16)

    def _mine(self):
        p = self.p
        return self.part(p.z if self.plane is None else ALL, *p.own, p.r)

    def _source(self, act):
        if self.plane is None:
            act()
        else:
            pl.when(self.p.z == self.plane)(act)

    def _copy(self, src, dst, n, dev):
        return remote(src, dst, self.send.at[n], self.recv.at[n], dev)

    def _a(self):
        p = self.p
        if self.wide:
            return self._copy(self.own(p.r), self.part(p.z, *p.own, p.r), 0, p.dev_a)
        return self._col(p.own, 0, p.dev_a)

    def _col(self, col, n, dev):
        piece = self.part(ALL, *col, self.p.r)
        return self._copy(piece, piece, n, dev)

    def _d(self, n):
        p = self.p
        return self._col((p.own, p.col_a, p.col_b, p.col_ab)[n], 3 + n, p.dev_d)

    def _keep(self):
        return pltpu.make_async_copy(self.own(self.p.r), self._mine(), self.local)

    def start(self):
        if self.wide:
            self._a().start()
        self._source(lambda: self._keep().start())
        self.line.start(self.own(self.p.r))

    def hop_one(self):
        self.line.hop(1)
        if self.wide:
            self._a().wait_recv()
            self.line_a.start(None)

    def hop_two(self):
        self.line.hop(2)
        if self.wide:
            self.line_a.hop(1)

    def after_z(self):
        p = self.p
        self._source(lambda: self._keep().wait())
        self.line.hop(3)
        if not self.wide:
            self._a().start()
        self._col(p.own, 1, p.dev_b).start()
        if self.halves:
            self._d(0).start()
        if self.wide:
            self.line_a.hop(2)

    def after_a(self):
        p = self.p
        if self.wide:
            self.line_a.hop(3)
        else:
            self._a().wait_recv()
        self._col(p.col_a, 2, p.dev_b).start()
        if self.halves:
            self._d(1).start()

    def after_b(self):
        p = self.p
        self._col(p.own, 1, p.dev_b).wait_recv()
        if self.halves:
            self._d(2).start()
        self._col(p.own, 2, p.dev_b).wait_recv()
        if self.halves:
            self._d(3).start()

    def done(self):
        if self.halves:
            for n in range(4):
                self._d(n).wait_recv()

    def drain(self):
        p = self.p
        self.line.drain()
        if self.wide:
            self.line_a.drain()
        self._a().wait_send()
        self._col(p.own, 1, p.dev_b).wait_send()
        self._col(p.own, 2, p.dev_b).wait_send()
        if self.halves:
            for n in range(4):
                self._d(n).wait_send()


def add_into(dst, src):
    dst[...] = dst[...] + src[...]


class LineScatter:
    def __init__(self, scatter, col, base, down, up, direct=False):
        self.s, self.col, self.base, self.down, self.up, self.direct = scatter, col, base, down, up, direct

    def _straight(self, k):
        s = self.s
        zz, dev = s.p.z_dev(k)
        return s._copy(self._piece(zz), self.down.at[k], self.base + k, dev)

    def _piece(self, zs):
        s = self.s
        return s.part(zs, *self.col, s.p.r)

    def _send(self, lo, hi, step):
        s = self.s
        buf, n = (self.up, 0) if step > 0 else (self.down, 1)
        return s._copy(self._piece(slice(lo, hi)), buf.at[slice(lo, hi)], self.base + n, (s.p.r, s.p.i + 4 * step))

    def _moves(self):
        j = self.s.plane
        if j is None:
            return [(0, 3, 0, 3, -1), (0, 0, 1, 4, 1), (1, 2, 0, 2, -1), (1, 1, 2, 4, 1), (2, 1, 0, 1, -1), (2, 2, 3, 4, 1)]
        return [(3 - z, z, 0, 4, -1) for z in range(3, j, -1)] + [(z, z, 0, 4, 1) for z in range(j)]

    def _take(self, lo, hi, step):
        buf = self.up if step > 0 else self.down
        self._send(lo, hi, step).wait_recv()
        add_into(self._piece(slice(lo, hi)), buf.at[slice(lo, hi)])

    def step(self, k):
        if self.direct:
            if k == 0:
                for n in (3, 2, 1):
                    self._straight(n).start()
            if k == 3:
                for n in (1, 2, 3):
                    self._straight(n).wait_recv()
                    add_into(self._piece(self.s.p.z), self.down.at[n])
            return
        moves = self._moves()
        for rnd, z, lo, hi, way in moves:
            if rnd == k - 1:
                pl.when(self.s.p.z == z + way)(functools.partial(self._take, lo, hi, way))
        for rnd, z, lo, hi, way in moves:
            if rnd == k:
                pl.when(self.s.p.z == z)(lambda lo=lo, hi=hi, way=way: self._send(lo, hi, way).start())

    def drain(self):
        if self.direct:
            for n in (1, 2, 3):
                self._straight(n).wait_send()
            return
        for _, z, lo, hi, way in self._moves():
            pl.when(self.s.p.z == z)(lambda lo=lo, hi=hi, way=way: self._send(lo, hi, way).wait_send())


class Scatter:
    def __init__(self, place, part, bufs, out, sems, plane=None, wide=False, direct=False):
        self.p, self.part, self.out, self.plane, self.wide = place, part, out, plane, wide
        self.dbuf, self.bbuf, self.abuf, down, up, down_a, up_a = bufs
        self.send, self.recv = sems
        self.line = LineScatter(self, place.own, 8, down, up, direct)
        self.line_a = LineScatter(self, place.col_a, 10, down_a, up_a)

    def _copy(self, src, dst, n, dev):
        return remote(src, dst, self.send.at[n], self.recv.at[n], dev)

    def _d(self, zz):
        p = self.p
        return self._copy(self.part(zz, ALL, ALL, 1 - p.r), self.dbuf.at[zz], zz, p.dev_d)

    def _b(self, n):
        p = self.p
        col = (p.col_b, p.col_ab)[n]
        return self._copy(self.part(ALL, *col, p.r), self.bbuf.at[n], 4 + n, p.dev_b)

    def _a(self):
        p = self.p
        if self.wide:
            return self._copy(self.part(p.z, *p.col_a, p.r), self.abuf.at[0], 6, p.dev_a)
        return self._copy(self.part(ALL, *p.col_a, p.r), self.abuf, 6, p.dev_a)

    def _here(self, act):
        if self.plane is None:
            act()
        else:
            pl.when(self.p.z == self.plane)(act)

    def _f(self):
        p = self.p
        return self._copy(self.out(p.r), self.out(p.r), 7, p.dev_d)

    def start(self):
        for zz in range(4):
            self._d(zz).start()

    def after_d(self):
        p = self.p
        for zz in range(4):
            self._d(zz).wait_recv()
        for n, col in enumerate((p.col_b, p.col_ab, p.col_a, p.own)):
            add_into(self.part(ALL, *col, p.r), self.dbuf.at[(ALL,) + col])
            if n < 2:
                self._b(n).start()

    def after_b(self):
        p = self.p
        self._b(1).wait_recv()
        add_into(self.part(ALL, *p.col_a, p.r), self.bbuf.at[1])
        if self.wide:
            self.line_a.step(0)
        else:
            self._a().start()
        self._b(0).wait_recv()
        add_into(self.part(ALL, *p.own, p.r), self.bbuf.at[0])
        if self.wide:
            self.line.step(0)

    def after_a(self):
        p = self.p
        if self.wide:
            self.line_a.step(1)
            self.line.step(1)
        else:
            self._a().wait_recv()
            add_into(self.part(ALL, *p.own, p.r), self.abuf)
            self.line.step(0)

    def line_one(self):
        if self.wide:
            self.line_a.step(2)
            self.line.step(2)
        else:
            self.line.step(1)

    def line_two(self):
        if self.wide:
            self.line_a.step(3)
            self._a().start()
        else:
            self.line.step(2)

    def last(self):
        self.line.step(3)
        self._here(self._finish)

    def _finish(self):
        p = self.p
        total = self.part(p.z if self.plane is None else ALL, *p.own, p.r)[...].astype(F32)
        if self.wide:
            self._a().wait_recv()
            total = total + self.abuf[0].astype(F32)
        self.out(p.r)[...] = total
        self._f().start()

    def done(self):
        self._here(lambda: self._f().wait_recv())

    def drain(self):
        for zz in range(4):
            self._d(zz).wait_send()
        for n in range(2):
            self._b(n).wait_send()
        self._a().wait_send()
        self.line.drain()
        if self.wide:
            self.line_a.drain()
        self._here(lambda: self._f().wait_send())


class ScatterSmall:
    def __init__(self, place, ref, bufs, out, sems):
        self.p, self.ref, self.out = place, ref, out
        self.bbuf, self.abuf, self.zbuf, self.fbuf = bufs
        self.send, self.recv = sems

    def _copy(self, src, dst, n, dev):
        return remote(src, dst, self.send.at[n], self.recv.at[n], dev)

    def _b(self, n):
        p = self.p
        col = (p.col_b, p.col_ab)[n]
        return self._copy(self.ref.at[(ALL,) + col], self.bbuf.at[n], n, p.dev_b)

    def _a(self):
        p = self.p
        return self._copy(self.ref.at[(ALL,) + p.col_a], self.abuf, 2, p.dev_a)

    def _z(self, k):
        p = self.p
        zz, dev = p.z_dev(k)
        return self._copy(self.ref.at[(zz,) + p.own], self.zbuf.at[k - 1], 2 + k, dev)

    def _f(self):
        p = self.p
        return self._copy(self.out, self.fbuf, 6, p.dev_d)

    def start(self):
        self._b(0).start()
        self._b(1).start()

    def after_b(self):
        p = self.p
        self._b(0).wait_recv()
        self._b(1).wait_recv()
        self.ref[(ALL,) + p.col_a] += self.bbuf[1]
        self.ref[(ALL,) + p.own] += self.bbuf[0]
        self._a().start()

    def after_a(self):
        p = self.p
        self._a().wait_recv()
        self.ref[(ALL,) + p.own] += self.abuf[...]
        for k in (1, 2, 3):
            self._z(k).start()

    def after_z(self):
        p = self.p
        for k in (1, 2, 3):
            self._z(k).wait_recv()
        self.out[...] = self.ref[(p.z,) + p.own] + self.zbuf[0] + self.zbuf[1] + self.zbuf[2]
        self._f().start()

    def done(self):
        self._f().wait_recv()
        self._f().wait_send()
        self.out[...] = self.out[...] + self.fbuf[...]

    def drain(self):
        self._b(0).wait_send()
        self._b(1).wait_send()
        self._a().wait_send()
        for k in (1, 2, 3):
            self._z(k).wait_send()


ROWS_ALL = 768
IMAGE = 384
KEYS = 288
ALWAYS = 192
SLOTS = 4
WIDE_GATHER = (5, 7, 9, 11)
WIDE_SCATTER = (1, 3, 5, 7)
DIRECT_GATHER = (0,)
DIRECT_SCATTER = (9, 10, 11)
NT = (((1,), (1,)), ((), ()))
TN = (((0,), (0,)), ((), ()))


def dots(a, b, dims=None):
    if dims is None:
        return jnp.dot(a, b, preferred_element_type=F32)
    return lax.dot_general(a, b, dims, preferred_element_type=F32)


def loop(count, body):
    def step(t, carry):
        body(t)
        return carry

    lax.fori_loop(0, count, step, 0)


def tiles(count, size, body):
    loop(count, lambda t: body(t, pl.ds(pl.multiple_of(t * size, size), size)))


def moments(v):
    centre = v - jnp.mean(v, axis=-1, keepdims=True)
    inverse = lax.rsqrt(jnp.mean(centre * centre, axis=-1, keepdims=True) + epsilon)
    return centre * inverse, inverse


def half(core):
    return pl.ds(pl.multiple_of(core * HALF, 128), HALF)


(OPEN, VECTORS, NORMED, GROUP, MIXED, PROJECT, SCALED, FEED, TWO, MIXED_BACK, PROJECT_BACK, BACK, GROWN, ONE, CLOSE) = range(15)
STEPS = (
    (Gather.start, Gather.hop_one, Gather.hop_two, Gather.after_z, Gather.after_a, Gather.after_b, Gather.done),
    (Scatter.start, Scatter.after_d, Scatter.after_b, Scatter.after_a, Scatter.line_one, Scatter.line_two, Scatter.last),
    (ScatterSmall.after_b, ScatterSmall.after_a, ScatterSmall.after_z),
)


PLAN = (
    ((OPEN,), ((0, 0, 0), (0, 1, 0), (0, 2, 0), (3, 0, 3), (0, 0, 1), (0, 0, 2), (3, 0, 4), (0, 0, 3), (0, 3, 0),
        (0, 4, 0), (0, 1, 1), (0, 2, 1), (0, 5, 0), (3, 0, 5), (0, 0, 4), (0, 1, 2), (0, 2, 2), (0, 3, 1),)),
    ((NORMED,), ((0, 1, 3), (0, 4, 1), (0, 5, 1), (0, 6, 0),)),
    ((GROUP, 0, -1), ((0, 0, 5), (0, 2, 3), (0, 7, 0), (0, 3, 2), (0, 0, 6),)),
    ((GROUP, 0, -2), ((0, 1, 4),)),
    ((GROUP, 0, 1), ((0, 4, 2),)),
    ((GROUP, 0, 3), ((0, 2, 4), (0, 5, 2),)),
    ((GROUP, 1, -1), ((0, 3, 3), (0, 6, 1), (0, 1, 5), (0, 7, 1), (0, 4, 3), (0, 2, 5), (0, 1, 6),)),
    ((GROUP, 1, -2), ((0, 5, 3), (0, 3, 4), (0, 8, 0), (0, 9, 0),)),
    ((GROUP, 1, 3), ((0, 4, 4), (0, 6, 2), (0, 6, 3),)),
    ((GROUP, 2, -1), ((0, 2, 6),)),
    ((GROUP, 2, -2), ((0, 7, 2), (0, 10, 0),)),
    ((GROUP, 2, 0), ((0, 5, 4),)),
    ((MIXED,), ((0, 3, 5), (0, 8, 1), (0, 9, 1), (0, 10, 1), (0, 3, 6),)),
    ((PROJECT, 0), ((0, 4, 5), (0, 7, 3),)),
    ((PROJECT, 1), ((0, 6, 4),)),
    ((FEED, 0, 0), ((0, 4, 6),)),
    ((FEED, 0, 1), ((0, 5, 5), (0, 8, 2), (0, 8, 3),)),
    ((FEED, 0, 2), ((0, 9, 2), (0, 11, 0), (0, 10, 2), (0, 7, 4), (0, 5, 6),)),
    ((FEED, 0, 3), ((0, 6, 5), (0, 9, 3),)),
    ((FEED, 0, 4), ((0, 8, 4),)),
    ((FEED, 0, 5), ((1, 0, 0), (0, 11, 1),)),
    ((FEED, 0, 6), ((0, 7, 5), (0, 10, 3),)),
    ((FEED, 0, 7), ((1, 1, 0), (0, 9, 4), (1, 0, 1),)),
    ((FEED, 1, 0), ((0, 6, 6),)),
    ((FEED, 1, 1), ((0, 11, 2), (0, 8, 5),)),
    ((FEED, 1, 2), ((0, 7, 6),)),
    ((FEED, 1, 3), ((0, 10, 4), (1, 1, 1),)),
    ((FEED, 1, 4), ((0, 11, 3),)),
    ((FEED, 1, 5), ((1, 2, 0), (0, 9, 5),)),
    ((FEED, 1, 6), ((0, 11, 4),)),
    ((FEED, 1, 7), ((1, 3, 0), (1, 2, 1),)),
    ((FEED, 2, 0), ((0, 8, 6),)),
    ((FEED, 2, 1), ((1, 0, 2),)),
    ((FEED, 2, 2), ((0, 9, 6),)),
    ((FEED, 2, 3), ((0, 10, 5), (1, 3, 1),)),
    ((FEED, 2, 4), ((1, 1, 2),)),
    ((FEED, 2, 5), ((1, 4, 0),)),
    ((FEED, 2, 7), ((1, 5, 0), (0, 11, 5), (1, 4, 1),)),
    ((FEED, 3, 0), ((0, 10, 6),)),
    ((FEED, 3, 2), ((1, 2, 2), (1, 5, 1), (1, 1, 3), (0, 11, 6),)),
    ((FEED, 3, 3), ((1, 0, 3),)),
    ((FEED, 3, 5), ((1, 6, 0), (1, 1, 4), (1, 3, 2),)),
    ((FEED, 3, 7), ((1, 7, 0), (1, 0, 4), (1, 4, 2), (1, 6, 1),)),
    ((TWO, 0), ((1, 1, 5),)),
    ((TWO, 2), ((1, 2, 3),)),
    ((TWO, 3), ((1, 7, 1),)),
    ((MIXED_BACK,), ((1, 3, 3), (1, 0, 5), (1, 5, 2),)),
    ((PROJECT_BACK,), ((1, 8, 0), (1, 4, 3),)),
    ((BACK, 0, 1), ((1, 2, 4),)),
    ((BACK, 0, 2), ((1, 8, 1),)),
    ((BACK, 0, 3), ((1, 0, 6), (1, 1, 6), (1, 3, 4), (1, 6, 2),)),
    ((BACK, 0, -1), ((1, 9, 0),)),
    ((BACK, 1, 0), ((1, 5, 3), (1, 7, 2), (1, 2, 5), (1, 2, 6),)),
    ((BACK, 1, 1), ((1, 3, 5),)),
    ((BACK, 1, 2), ((1, 9, 1),)),
    ((BACK, 1, 3), ((1, 4, 4), (1, 8, 2),)),
    ((BACK, 1, -1), ((1, 10, 0), (1, 5, 4), (1, 6, 3),)),
    ((BACK, 2, 0), ((1, 3, 6),)),
    ((BACK, 2, 2), ((1, 7, 3), (1, 10, 1),)),
    ((BACK, 2, 3), ((1, 4, 5), (1, 4, 6), (1, 5, 5), (1, 9, 2),)),
    ((BACK, 2, -1), ((1, 11, 0), (1, 6, 4), (1, 8, 3),)),
    ((GROWN, 1), ((1, 7, 4), (1, 10, 2), (1, 11, 1), (1, 5, 6),)),
    ((ONE, 0), ((1, 8, 4), (1, 9, 3), (1, 9, 4), (1, 9, 5),)),
    ((ONE, 1), ((1, 6, 5),)),
    ((ONE, 2), ((1, 7, 5),)),
    ((ONE, 3), ((1, 10, 3), (1, 10, 4), (1, 10, 5),)),
    ((CLOSE,), ((1, 8, 5), (1, 11, 2), (1, 7, 6), (2, 0, 0), (1, 9, 6), (1, 6, 6), (1, 11, 3), (1, 11, 4),
        (1, 11, 5), (2, 0, 1), (1, 10, 6), (2, 0, 2), (1, 8, 6), (1, 11, 6),)),
)


class Agenda:
    def __init__(self):
        self.calls = {}

    def at(self, point, *calls):
        self.calls.setdefault(point, []).extend(calls)

    def run(self, point):
        for call in self.calls.pop(point, []):
            call()

    def here(self, *place):
        for point in list(self.calls):
            if len(point) != len(place):
                continue
            test, fits = None, True
            for value, index in zip(point, place):
                if isinstance(index, int):
                    fits = fits and value == index
                elif value < 0:
                    fits = False
                else:
                    same = index == value
                    test = same if test is None else jnp.logical_and(test, same)
            if fits and test is None:
                self.run(point)
            elif fits:
                pl.when(test)(functools.partial(self.run, point))


def layer_kernel(
    tokens, cot, grids, keep_a, keep_m, g1, s1, bqv, bp, g2, s2, b1, b2, wq, wp, w1, w2,
    out_h, gt_h, oq, op, o1, o2, og1, os1, obqv, obp, og2, os2, ob1, ob2,
    x, ct, dz, h1, qkv, probs, mixed, y1, h2, dact, act, acc, dh,
    gu, gw2, stage, pack, packs, vec, flat, vqkv, vb1, dvec, dbqv, db1, outq, smalls, opack,
    dbuf, bbuf, abuf, lbuf, wbuf, sb, sa, sz, sf,
    gsend, grecv, glocal, tsend, trecv, tlocal, ssend, srecv, usend, urecv, local,
):
    place = Place()
    load_x = pltpu.make_async_copy(tokens, x, local.at[0])
    load_c = pltpu.make_async_copy(cot, ct, local.at[1])
    load_x.start()
    load_c.start()
    pack[...] = jnp.zeros_like(pack)
    for row, ref in enumerate((g1, s1, bp, g2, s2, b2)):
        pack[row : row + 1, 0:48] = ref[...].astype(F32).reshape(1, 48)
    pack[6:7, 0:96] = bqv[...].astype(F32).reshape(1, 96)
    both = b1[...].astype(F32).reshape(1, 192)
    pack[7:8, 0:96] = both[:, :96]
    pack[8:9, 0:96] = both[:, 96:]
    for g in range(3):
        for k in range(3):
            stage[g, :, 256 * k : 256 * k + 256] = wq[:, 768 * k + 256 * g : 768 * k + 256 * g + 256]
    greet(place)

    tiny = Gather(place, lambda zs, y, xx, core: packs.at[zs, y, xx], lambda core: pack, (tsend, trecv), tlocal, halves=False, direct=True)

    def block(u):
        return lambda zs, y, xx, core: gu.at[u, zs, y, xx, :, half(core)]

    def plane_part(j):
        return lambda zs, y, xx, core: gw2.at[j, y, xx, zs, :, half(core)]

    def fc1_cols(j, core):
        return pl.ds(pl.multiple_of(WIDE * j + core * HALF, 128), HALF)

    pieces = [(block(g), lambda core, g=g: stage.at[g, :, half(core)], None) for g in range(3)]
    pieces.append((block(3), lambda core: wp.at[:, half(core)], None))
    for j in range(4):
        pieces.append((plane_part(j), lambda core: w2.at[:, :, half(core)], j))
        pieces.append((block(4 + j), lambda core, j=j: w1.at[:, fc1_cols(j, core)], None))
    units = [
        Gather(place, part, own, (gsend.at[n], grecv.at[n]), glocal.at[n], wide=n in WIDE_GATHER, plane=plane, direct=n in DIRECT_GATHER)
        for n, (part, own, plane) in enumerate(pieces)
    ]

    def gq_part(g):
        return lambda zs, y, xx, core: dact.at[g, zs, y, xx, :, half(core)]

    plans = []
    for j in range(4):
        plans.append((plane_part(j), lambda core: o2.at[:, :, half(core)], j))
        plans.append((block(4 + j), lambda core, j=j: o1.at[:, fc1_cols(j, core)], None))
    plans.append((block(3), lambda core: op.at[:, half(core)], None))
    for g in range(3):
        plans.append((gq_part(g), lambda core, g=g: outq.at[g, :, half(core)], None))
    sends = []
    for n, (part, out, plane) in enumerate(plans):
        wide = n in WIDE_SCATTER
        extra = [wbuf.at[WIDE_SCATTER.index(n), k] for k in range(2)] if wide else [None, None]
        bufs = [dbuf.at[n % SLOTS], bbuf.at[n], abuf.at[n], lbuf.at[n, 0], lbuf.at[n, 1]] + extra
        sends.append(Scatter(place, part, bufs, out, (ssend.at[n], srecv.at[n]), plane, wide, n in DIRECT_SCATTER))
    small = ScatterSmall(place, smalls, (sb, sa, sz, sf), opack, (usend, urecv))

    agenda = Agenda()
    groups = (units, sends, [small], [tiny])
    for point, steps in PLAN:
        for kind, n, step in steps:
            step = STEPS[min(kind, 2)][step] if kind < 3 else STEPS[0][step]
            agenda.at(point, functools.partial(step, groups[kind][n]))

    tiny.start()
    agenda.here(OPEN)
    for s in range(16):
        at = (s // 4, (s // 2) % 2, s % 2)
        vec[:, 48 * s : 48 * s + 48] = packs[at + (slice(0, 8), slice(0, 48))]
        c = 192 * (s % 4)
        vb1[s // 4, :, c : c + 96] = packs[at + (slice(7, 8), slice(0, 96))]
        vb1[s // 4, :, c + 96 : c + 192] = packs[at + (slice(8, 9), slice(0, 96))]
        c = 96 * s + 768 * (s // 8)
        flat[:, c : c + 96] = packs[at + (slice(6, 7), slice(0, 96))]
    flat[:, 768:1536] = jnp.zeros((1, 768), F32)
    for g in range(3):
        for k in range(3):
            vqkv[g, :, 256 * k : 256 * k + 256] = flat[:, 768 * k + 256 * g : 768 * k + 256 * g + 256]
    dvec[...] = jnp.zeros_like(dvec)
    dbqv[...] = jnp.zeros_like(dbqv)

    agenda.here(VECTORS)
    load_x.wait()

    def norm_one(t, rows):
        n, _ = moments(x[rows, :].astype(F32))
        h1[rows, :] = (n * vec[0:1, :] + vec[1:2, :]).astype(BF16)

    tiles(6, 128, norm_one)
    agenda.here(NORMED)

    lane = lax.broadcasted_iota(jnp.int32, (1, 128), 1) // HEAD

    def pair(g, t):
        base = pl.multiple_of(t // 2 * IMAGE, IMAGE)
        at = [pl.ds(pl.multiple_of(256 * k + 128 * (t % 2), 128), 128) for k in range(3)]
        q = qkv[g, pl.ds(base, IMAGE), at[0]] * BF16(0.125)
        k = qkv[g, pl.ds(base, KEYS), at[1]]
        v = qkv[g, pl.ds(base, KEYS), at[2]]
        col = pl.ds(pl.multiple_of(256 * g + 128 * (t % 2), 128), 128)
        return base, at, q, k, v, col

    def attend(g, t):
        base, at, q, k, v, col = pair(g, t)
        length = grids[t // 2, 0] * grids[t // 2, 1] + 2
        key = lax.broadcasted_iota(jnp.int32, (KEYS - ALWAYS, IMAGE), 0) + ALWAYS
        total = None
        for h in range(2):
            qh = jnp.where(lane == h, q, BF16(0))
            vh = jnp.where(lane == h, v, BF16(0))
            s = dots(k, qh, NT)
            s = jnp.concatenate([s[:ALWAYS], jnp.where(key < length, s[ALWAYS:], -1000000000.0)], axis=0)
            e = jnp.exp(s - jnp.max(s, axis=0, keepdims=True))
            p = (e * (1.0 / jnp.sum(e, axis=0, keepdims=True))).astype(BF16)
            probs[8 * g + 2 * t + h] = p
            o = dots(p, vh, TN)
            total = o if total is None else total + o
        mixed[pl.ds(base, IMAGE), col] = total.astype(BF16)
        agenda.here(GROUP, g, t)

    def forward_group(g):
        agenda.here(GROUP, g, -1)
        qkv[g] = (dots(h1[...], gu[g].reshape(768, 768)) + vqkv[g]).astype(BF16)
        agenda.here(GROUP, g, -2)
        loop(4, functools.partial(attend, g))

    loop(3, forward_group)

    def kept(ref, b):
        return ref[b].astype(F32) * (1.0 / 0.9)

    agenda.here(MIXED)

    def project(b):
        rows = pl.ds(pl.multiple_of(b * IMAGE, IMAGE), IMAGE)
        y = x[rows, :].astype(F32) + kept(keep_a, b) * (dots(mixed[rows, :], gu[3].reshape(768, 768)) + vec[2:3, :])
        y1[rows, :] = y
        n, _ = moments(y)
        h2[rows, :] = (n * vec[3:4, :] + vec[4:5, :]).astype(BF16)
        agenda.here(PROJECT, b)

    loop(2, project)
    load_c.wait()

    def scale_dz(t, rows):
        d = (ct[rows, :].astype(F32) * kept(keep_m, t // 3)).astype(BF16)
        dz[rows, :] = d
        dvec[5:6, :] += jnp.sum(d.astype(F32), axis=0, keepdims=True)

    tiles(6, 128, scale_dz)
    acc[...] = jnp.zeros_like(acc)
    dh[...] = jnp.zeros_like(dh)
    agenda.here(SCALED)
    units[3].drain()

    def feed(j):
        agenda.here(FEED, j, 0)
        dact[j] = dots(dz[...], gw2[j].reshape(768, 768), NT).astype(BF16).reshape(4, 2, 2, ROWS, 768)
        agenda.here(FEED, j, 1)
        agenda.here(FEED, j, 2)
        pre = dots(h2[...], gu[j + 4].reshape(768, 768)) + vb1[j]
        u = 0.5 * (1.0 + lax.erf(pre * root_half))
        act[...] = (pre * u).astype(BF16)
        d = dact[j].reshape(768, 768).astype(F32) * (u + pre * jnp.exp(-0.5 * pre * pre) * 0.3989422804014327)
        db1[j] = jnp.sum(d, axis=0, keepdims=True)
        dact[j] = d.astype(BF16).reshape(4, 2, 2, ROWS, 768)
        agenda.here(FEED, j, 3)
        acc[...] += dots(act[...], gw2[j].reshape(768, 768))
        agenda.here(FEED, j, 4)
        for n in range(4):
            pl.when(j == n)(units[4 + 2 * n].drain)
        gw2[j] = dots(act[...], dz[...], TN).astype(BF16).reshape(2, 2, 4, ROWS, 768)
        agenda.here(FEED, j, 5)
        dh[...] += dots(dact[j].reshape(768, 768), gu[j + 4].reshape(768, 768), NT)
        agenda.here(FEED, j, 6)
        for n in range(4):
            pl.when(j == n)(units[5 + 2 * n].drain)
        gu[j + 4] = dots(h2[...], dact[j].reshape(768, 768), TN).astype(BF16).reshape(4, 2, 2, ROWS, 768)
        agenda.here(FEED, j, 7)

    loop(4, feed)

    def norm_two_back(t, rows):
        y = y1[rows, :]
        act[rows, :] = (y + kept(keep_m, t // 3) * (acc[rows, :] + vec[5:6, :])).astype(BF16)
        acc[rows, :] = jnp.zeros((128, 768), F32)
        n, inverse = moments(y)
        d = dh[rows, :]
        e = d * vec[3:4, :]
        back = inverse * (e - jnp.mean(e, axis=-1, keepdims=True) - n * jnp.mean(e * n, axis=-1, keepdims=True))
        back = ct[rows, :].astype(F32) + back
        dh[rows, :] = back
        da = (back * kept(keep_a, t // 3)).astype(BF16)
        h2[rows, :] = da
        dvec[3:4, :] += jnp.sum(d * n, axis=0, keepdims=True)
        dvec[4:5, :] += jnp.sum(d, axis=0, keepdims=True)
        dvec[2:3, :] += jnp.sum(da.astype(F32), axis=0, keepdims=True)
        agenda.here(TWO, t)

    tiles(6, 128, norm_two_back)
    save_out = pltpu.make_async_copy(act, out_h, local.at[2])
    save_out.start()
    dz[...] = dots(h2[...], gu[3].reshape(768, 768), NT).astype(BF16)
    agenda.here(MIXED_BACK)
    gu[3] = dots(mixed[...], h2[...], TN).astype(BF16).reshape(4, 2, 2, ROWS, 768)
    agenda.here(PROJECT_BACK)

    def attend_back(g, t):
        base, at, q, k, v, col = pair(g, t)
        do = dz[pl.ds(base, IMAGE), col]
        dq = dk = dv = None
        for h in range(2):
            qh = jnp.where(lane == h, q, BF16(0))
            kh = jnp.where(lane == h, k, BF16(0))
            doh = jnp.where(lane == h, do, BF16(0))
            p = probs[8 * g + 2 * t + h]
            pf = p.astype(F32)
            dp = dots(v, doh, NT)
            ds = (pf * (dp - jnp.sum(pf * dp, axis=0, keepdims=True))).astype(BF16)
            new = (dots(ds, kh, TN), dots(ds, qh), dots(p, doh))
            dq, dk, dv = new if dq is None else (dq + new[0], dk + new[1], dv + new[2])
        dq = dq * 0.125
        qkv[g, pl.ds(base, IMAGE), at[0]] = dq.astype(BF16)
        qkv[g, pl.ds(base, KEYS), at[1]] = dk.astype(BF16)
        qkv[g, pl.ds(base, KEYS), at[2]] = dv.astype(BF16)
        none = jnp.zeros((IMAGE - KEYS, 128), BF16)
        qkv[g, pl.ds(base + KEYS, IMAGE - KEYS), at[1]] = none
        qkv[g, pl.ds(base + KEYS, IMAGE - KEYS), at[2]] = none
        dbqv[0, :, col] += jnp.sum(dq, axis=0, keepdims=True)
        dbqv[1, :, col] += jnp.sum(dv, axis=0, keepdims=True)
        agenda.here(BACK, g, t)

    def back_group(g):
        loop(4, functools.partial(attend_back, g))
        dact[g] = dots(h1[...], qkv[g], TN).astype(BF16).reshape(4, 2, 2, ROWS, 768)
        agenda.here(BACK, g, -1)

    loop(3, back_group)

    def grow(g):
        acc[...] += dots(qkv[g], gu[g].reshape(768, 768), NT)
        agenda.here(GROWN, g)

    loop(3, grow)

    def norm_one_back(t, rows):
        n, inverse = moments(x[rows, :].astype(F32))
        d = acc[rows, :]
        e = d * vec[0:1, :]
        back = inverse * (e - jnp.mean(e, axis=-1, keepdims=True) - n * jnp.mean(e * n, axis=-1, keepdims=True))
        dh[rows, :] += back
        dvec[0:1, :] += jnp.sum(d * n, axis=0, keepdims=True)
        dvec[1:2, :] += jnp.sum(d, axis=0, keepdims=True)
        agenda.here(ONE, t)

    tiles(6, 128, norm_one_back)
    save_gt = pltpu.make_async_copy(dh, gt_h, local.at[3])
    save_gt.start()
    smalls[...] = jnp.zeros_like(smalls)
    for s in range(16):
        at = (s // 4, (s // 2) % 2, s % 2)
        smalls[at + (slice(0, 8), slice(0, 48))] = dvec[:, 48 * s : 48 * s + 48]
        c = 96 * (s % 8)
        smalls[at + (slice(6, 7), slice(0, 96))] = dbqv[s // 8, :, c : c + 96]
        c = 192 * (s % 4)
        smalls[at + (slice(7, 8), slice(0, 96))] = db1[s // 4, :, c : c + 96]
        smalls[at + (slice(8, 9), slice(0, 96))] = db1[s // 4, :, c + 96 : c + 192]
    small.start()
    agenda.here(CLOSE)
    small.done()
    for unit in sends:
        unit.done()
    assert not agenda.calls
    for g in range(3):
        for k in range(3):
            oq[:, 768 * k + 256 * g : 768 * k + 256 * g + 256] = outq[g, :, 256 * k : 256 * k + 256]
    for row, ref in enumerate((og1, os1, obp, og2, os2, ob2)):
        ref[...] = opack[row : row + 1, 0:48].reshape(48)
    obqv[...] = opack[6:7, 0:96].reshape(96)
    ob1[...] = jnp.concatenate([opack[7:8, 0:96], opack[8:9, 0:96]], axis=1).reshape(192)
    for unit in [units[0], units[1], units[2], tiny, small] + sends:
        unit.drain()
    save_out.wait()
    save_gt.wait()


def handover_kernel(*refs):
    count = len(refs) // 4
    ins, outs, held, sems = (refs[n * count : (n + 1) * count] for n in range(4))
    takes = [pltpu.make_async_copy(ins[n], held[n], sems[n].at[0]) for n in range(count)]
    gives = [pltpu.make_async_copy(held[n], outs[n], sems[n].at[1]) for n in range(count)]
    for copy in takes:
        copy.start()
    for take, give in zip(takes, gives):
        take.wait()
        give.start()
    for copy in gives:
        copy.wait()


def handover(arrays):
    specs = [pl.BlockSpec(memory_space=pltpu.HBM)] * len(arrays)
    return pl.pallas_call(
        handover_kernel,
        out_shape=[jax.ShapeDtypeStruct(a.shape, a.dtype) for a in arrays],
        in_specs=specs,
        out_specs=specs,
        scratch_shapes=[pltpu.VMEM(a.shape, a.dtype) for a in arrays] + [pltpu.SemaphoreType.DMA((2,))] * len(arrays),
        name="handover",
    )(*arrays)


def by_block(tokens, grids, keep_attn, keep_mlp, cotangent, *params):
    g1, s1, wq, bqv, wp, bp, g2, s2, w1, b1, w2, b2 = params
    rows = lambda v: v.reshape(ROWS_ALL, 768)
    vm, sm, hbm = (pl.BlockSpec(memory_space=m) for m in (pltpu.VMEM, pltpu.SMEM, pltpu.HBM))
    S = jax.ShapeDtypeStruct
    v = lambda *shape: pltpu.VMEM(shape, BF16)
    f = lambda *shape: pltpu.VMEM(shape, F32)
    dma = lambda *shape: pltpu.SemaphoreType.DMA(shape)
    outs = pl.pallas_call(
        layer_kernel,
        out_shape=[S((ROWS_ALL, 768), BF16), S((ROWS_ALL, 768), F32)]
        + [S(w.shape, F32) for w in (wq, wp, w1)]
        + [S((4, ROWS, 768), F32)]
        + [S(w.shape, F32) for w in (g1, s1, bqv, bp, g2, s2, b1, b2)],
        in_specs=[hbm] * 2 + [sm] * 3 + [vm] * 12,
        out_specs=[hbm] * 2 + [vm] * 12,
        scratch_shapes=[
            v(768, 768), v(768, 768), v(768, 768), v(768, 768), v(3, 768, 768), v(24, KEYS, IMAGE), v(768, 768), f(768, 768),
            v(768, 768), v(4, 4, 2, 2, ROWS, 768), v(768, 768), f(768, 768), f(768, 768),
            v(8, 4, 2, 2, ROWS, 768), v(4, 2, 2, 4, ROWS, 768), v(3, ROWS, 768), f(16, 128), f(4, 2, 2, 16, 128),
            f(8, 768), f(1, 2304), f(3, 1, 768), f(4, 1, 768), f(8, 768), f(2, 1, 768), f(4, 1, 768), f(3, ROWS, 768),
            f(4, 2, 2, 16, 128), f(16, 128),
            v(SLOTS, 4, 2, 2, ROWS, HALF), v(12, 2, 4, ROWS, HALF), v(12, 4, ROWS, HALF),
            v(12, 2, 4, ROWS, HALF), v(len(WIDE_SCATTER), 2, 4, ROWS, HALF),
            f(2, 4, 16, 128), f(4, 16, 128), f(3, 16, 128), f(16, 128),
            dma(12, 22), dma(12, 22), dma(12), dma(22), dma(22), dma(), dma(12, 12), dma(12, 12), dma(8), dma(8), dma(4),
        ],
        compiler_params=pltpu.CompilerParams(collective_id=0, has_side_effects=True, vmem_limit_bytes=62 << 20),
        cost_estimate=pl.CostEstimate(flops=36 * 10**9, bytes_accessed=10**7, transcendentals=10**7),
        name="layer",
    )(
        rows(tokens), rows(cotangent), grids, keep_attn, keep_mlp, g1, s1, bqv, bp, g2, s2, b1, b2, wq, wp, w1,
        w2.reshape(4, ROWS, 768),
    )
    out, gt, oq, op, o1, o2, og1, os1, obqv, obp, og2, os2, ob1, ob2 = handover(outs)
    return (
        out.reshape(tokens.shape), gt.reshape(tokens.shape), og1, os1, oq, obqv, op, obp, og2, os2, o1, ob1,
        o2.reshape(w2.shape), ob2,
    )


def layer_norm(stream, gain, shift):
    center = jnp.mean(stream, axis=-1, keepdims=True)
    shifted = stream - center
    inverse = lax.rsqrt(jnp.mean(shifted * shifted, axis=-1, keepdims=True) + epsilon)
    normed = shifted * inverse
    return (normed * gain + shift, normed, inverse)


def norm_back(grad_normed, normed, inverse, gain):
    scaled = grad_normed * gain
    grad_input = inverse * (
        scaled
        - jnp.mean(scaled, axis=-1, keepdims=True)
        - normed * jnp.mean(scaled * normed, axis=-1, keepdims=True)
    )
    return (grad_input, jnp.sum(grad_normed * normed, axis=0), jnp.sum(grad_normed, axis=0))


def gelu_exact(values):
    return 0.5 * values * (1.0 + lax.erf(values * root_half))


def outer_sum(left, right):
    return lax.dot_general(left, right, (((0,), (0,)), ((), ())), preferred_element_type=F32)


def back_dot(left, right):
    return lax.dot_general(left, right, (((1,), (1,)), ((), ())), preferred_element_type=F32)


def layer(tokens, grids, keep_attn, keep_mlp, cotangent, params):
    ln1_gain, ln1_shift, w_qkv, bias_qv, w_proj, bias_proj, ln2_gain, ln2_shift, w_fc1, bias_fc1, w_fc2, bias_fc2 = params
    images, seq_len, feat_dim = tokens.shape
    num_heads = feat_dim // HEAD
    row_count = images * seq_len
    lengths = grids[:, 0] * grids[:, 1] + 2
    key_valid = lax.broadcasted_iota(jnp.int32, (images, seq_len), 1) < lengths[:, None]
    scale_attn = jnp.broadcast_to((keep_attn.astype(F32) / 0.9)[:, None], (images, seq_len)).reshape(row_count, 1)
    scale_mlp = jnp.broadcast_to((keep_mlp.astype(F32) / 0.9)[:, None], (images, seq_len)).reshape(row_count, 1)
    stream = tokens.astype(F32).reshape(row_count, feat_dim)
    normed_out, normed_one, inverse_one = layer_norm(stream, ln1_gain, ln1_shift)
    normed_low_one = normed_out.astype(BF16)
    full_bias = jnp.concatenate([bias_qv[:feat_dim], jnp.zeros((feat_dim,), F32), bias_qv[feat_dim:]])
    triple = jnp.dot(normed_low_one, w_qkv, preferred_element_type=F32) + full_bias
    triple = triple.astype(BF16).reshape(images, seq_len, 3, num_heads, HEAD)
    queries, key_rows, values = triple[:, :, 0], triple[:, :, 1], triple[:, :, 2]
    scores = jnp.einsum("bqhe,bkhe->bhqk", queries, key_rows, preferred_element_type=F32) * 0.125
    scores = jnp.where(key_valid[:, None, None, :], scores, -1000000000.0)
    probs_full = jax.nn.softmax(scores, axis=-1)
    probs_low = probs_full.astype(BF16)
    mixed_low = jnp.einsum("bhqk,bkhe->bqhe", probs_low, values, preferred_element_type=F32)
    mixed_low = mixed_low.reshape(row_count, feat_dim).astype(BF16)
    branch = jnp.dot(mixed_low, w_proj, preferred_element_type=F32) + bias_proj
    middle = stream + scale_attn * branch
    normed_out, normed_two, inverse_two = layer_norm(middle, ln2_gain, ln2_shift)
    normed_low_two = normed_out.astype(BF16)
    pre_act = jnp.dot(normed_low_two, w_fc1, preferred_element_type=F32) + bias_fc1
    act_value, act_pullback = jax.vjp(gelu_exact, pre_act)
    act_low = act_value.astype(BF16)
    branch_two = jnp.dot(act_low, w_fc2, preferred_element_type=F32) + bias_fc2
    layer_out = (middle + scale_mlp * branch_two).astype(BF16).reshape(images, seq_len, feat_dim)
    grad_out = cotangent.astype(F32).reshape(row_count, feat_dim)
    grad_branch_two = (grad_out * scale_mlp).astype(BF16)
    grad_fc2 = outer_sum(act_low, grad_branch_two)
    grad_fc2_bias = jnp.sum(grad_branch_two.astype(F32), axis=0)
    grad_act = back_dot(grad_branch_two, w_fc2)
    grad_pre = act_pullback(grad_act)[0].astype(BF16)
    grad_fc1 = outer_sum(normed_low_two, grad_pre)
    grad_fc1_bias = jnp.sum(grad_pre.astype(F32), axis=0)
    grad_normed_two = back_dot(grad_pre, w_fc1)
    grad_middle, grad_gain_two, grad_shift_two = norm_back(grad_normed_two, normed_two, inverse_two, ln2_gain)
    grad_middle = grad_middle + grad_out
    grad_branch = (grad_middle * scale_attn).astype(BF16)
    grad_proj = outer_sum(mixed_low, grad_branch)
    grad_proj_bias = jnp.sum(grad_branch.astype(F32), axis=0)
    grad_mixed = back_dot(grad_branch, w_proj).astype(BF16).reshape(images, seq_len, num_heads, HEAD)
    grad_values = jnp.einsum("bhqk,bqhe->bkhe", probs_low, grad_mixed, preferred_element_type=F32)
    grad_probs = jnp.einsum("bqhe,bkhe->bhqk", grad_mixed, values, preferred_element_type=F32)
    row_delta = jnp.sum(probs_full * grad_probs, axis=-1, keepdims=True)
    grad_scores = (probs_full * (grad_probs - row_delta)).astype(BF16)
    grad_queries = jnp.einsum("bhqk,bkhe->bqhe", grad_scores, key_rows, preferred_element_type=F32) * 0.125
    grad_keys = jnp.einsum("bhqk,bqhe->bkhe", grad_scores, queries, preferred_element_type=F32) * 0.125
    grad_triple = jnp.stack([grad_queries, grad_keys, grad_values], axis=2).astype(BF16).reshape(row_count, 3 * feat_dim)
    grad_qkv = outer_sum(normed_low_one, grad_triple)
    column_sums = jnp.sum(grad_triple.astype(F32), axis=0)
    grad_pair = jnp.concatenate([column_sums[:feat_dim], column_sums[2 * feat_dim :]])
    grad_normed_one = back_dot(grad_triple, w_qkv)
    grad_input, grad_gain_one, grad_shift_one = norm_back(grad_normed_one, normed_one, inverse_one, ln1_gain)
    grad_input = (grad_input + grad_middle).reshape(images, seq_len, feat_dim)
    grads = (
        grad_gain_one, grad_shift_one, grad_qkv, grad_pair, grad_proj, grad_proj_bias,
        grad_gain_two, grad_shift_two, grad_fc1, grad_fc1_bias, grad_fc2, grad_fc2_bias,
    )
    return layer_out, grad_input, grads


def by_collectives(tokens, grids, keep_attn, keep_mlp, cotangent, *params):
    whole = [lax.all_gather(p, "fsdp", axis=0, tiled=True) for p in params]
    whole = [p.astype(F32) if p.ndim == 1 else p for p in whole]
    layer_out, grad_input, grads = layer(tokens, grids, keep_attn, keep_mlp, cotangent, whole)
    shards = [lax.psum_scatter(g, "fsdp", scatter_dimension=0, tiled=True) for g in grads]
    totals = [lax.psum(g.astype(BF16), "rep").astype(F32) for g in shards]
    return (layer_out, grad_input) + tuple(totals)


def solution(mesh):
    vec, mat, rows = P("fsdp"), P("fsdp", None), P(("rep", "fsdp"))
    image = P(("rep", "fsdp"), None, None)
    weights = (vec, vec, mat, vec, mat, vec, vec, vec, mat, vec, mat, vec)
    in_specs = (image, P(("rep", "fsdp"), None), rows, rows, image) + weights
    out_specs = (image, image) + weights
    block = mesh.shape["fsdp"] == 16 and mesh.shape["rep"] == 2
    return jax.shard_map(
        by_block if block else by_collectives, mesh=mesh, in_specs=in_specs, out_specs=out_specs, check_vma=False
    )
```

```python
import functools

import jax
import jax.numpy as jnp
from jax import lax
from jax.experimental import pallas as pl
from jax.experimental.pallas import tpu as pltpu
from jax.sharding import PartitionSpec as P

HEAD = 64
MESH = pl.DeviceIdType.MESH
F32 = jnp.float32
BF16 = jnp.bfloat16
epsilon = 1e-06
root_half = 0.7071067811865476

ROWS = 48
WIDE = 768
HALF = 384
ALL = slice(None)


class Place:
    def __init__(self):
        self.r = lax.axis_index("rep")
        self.i = lax.axis_index("fsdp")
        r, i = self.r, self.i
        self.z = i // 4
        self.y = (i // 2) % 2
        self.x = i % 2
        fx, fy = 1 - 2 * self.x, 1 - 2 * self.y
        self.dev_a = (r, i + (1 - r) * fx + r * 2 * fy)
        self.dev_b = (r, i + (1 - r) * 2 * fy + r * fx)
        self.dev_d = (1 - r, i)
        self.own = (self.y, self.x)
        self.col_a = (self.y + r * fy, self.x + (1 - r) * fx)
        self.col_b = (self.y + (1 - r) * fy, self.x + r * fx)
        self.col_ab = (1 - self.y, 1 - self.x)

    def z_dev(self, k):
        zz = (self.z + k) % 4
        return zz, (self.r, zz * 4 + self.i % 4)


def greet(place):
    barrier = pltpu.get_barrier_semaphore()
    for dev in (place.z_dev(1)[1], place.z_dev(2)[1], place.z_dev(3)[1], place.dev_a, place.dev_b, place.dev_d):
        pl.semaphore_signal(barrier, inc=1, device_id=dev, device_id_type=MESH)
    pl.semaphore_wait(barrier, 6)


def remote(src, dst, send, recv, dev):
    return pltpu.make_async_remote_copy(
        src_ref=src, dst_ref=dst, send_sem=send, recv_sem=recv, device_id=dev, device_id_type=MESH
    )


class LineGather:
    def __init__(self, gather, col, base, direct=False):
        self.g, self.col, self.base, self.direct = gather, col, base, direct

    def _straight(self, src, k):
        g = self.g
        p = g.p
        piece = g.part(p.z, *self.col, p.r)
        return g._copy(piece if src is None else src, piece, self.base + k - 1, p.z_dev(k)[1])

    def _send(self, src, zz, n, step):
        g = self.g
        p = g.p
        piece = g.part(ALL if g.plane is not None else zz, *self.col, p.r)
        dev = (p.r, p.i + 4 * step)
        return g._copy(piece if src is None else src, piece, self.base + n, dev)

    def sends(self, k, act, src=None):
        z, plane = self.g.p.z, self.g.plane
        if self.direct:
            for n in (3, 2, 1) if k == 0 else ():
                act(self._straight(src, n))
        elif plane is None:
            pl.when(jnp.logical_and(z >= k, z < 3))(lambda: act(self._send(src, z - k, k, 1)))
            pl.when(jnp.logical_and(z <= 3 - k, z > 0))(lambda: act(self._send(src, z + k, 3 + k, -1)))
        else:
            if plane + k < 3:
                pl.when(z == plane + k)(lambda: act(self._send(src, z, 0, 1)))
            if plane - k > 0:
                pl.when(z == plane - k)(lambda: act(self._send(src, z, 3, -1)))

    def start(self, src):
        self.sends(0, lambda copy: copy.start(), src)

    def hop(self, k):
        z, plane = self.g.p.z, self.g.plane
        if self.direct:
            for n in (1, 2, 3) if k == 3 else ():
                self._straight(None, n).wait_recv()
        elif plane is None:
            pl.when(z >= k)(lambda: self._send(None, z, k - 1, 0).wait_recv())
            pl.when(z <= 3 - k)(lambda: self._send(None, z, 2 + k, 0).wait_recv())
        else:
            if plane + k <= 3:
                pl.when(z == plane + k)(lambda: self._send(None, z, 0, 0).wait_recv())
            if plane - k >= 0:
                pl.when(z == plane - k)(lambda: self._send(None, z, 3, 0).wait_recv())
        if k < 3:
            self.sends(k, lambda copy: copy.start())

    def drain(self):
        for k in range(3):
            self.sends(k, lambda copy: copy.wait_send())


class Gather:
    def __init__(self, place, part, own, sems, local, halves=True, wide=False, plane=None, direct=False):
        self.p, self.part, self.own, self.plane = place, part, own, plane
        self.send, self.recv = sems
        self.local, self.halves, self.wide = local, halves, wide
        self.line = LineGather(self, place.own, 10, direct)
        self.line_a = LineGather(self, place.col_a, 16)

    def _mine(self):
        p = self.p
        return self.part(p.z if self.plane is None else ALL, *p.own, p.r)

    def _source(self, act):
        if self.plane is None:
            act()
        else:
            pl.when(self.p.z == self.plane)(act)

    def _copy(self, src, dst, n, dev):
        return remote(src, dst, self.send.at[n], self.recv.at[n], dev)

    def _a(self):
        p = self.p
        if self.wide:
            return self._copy(self.own(p.r), self._mine(), 0, p.dev_a)
        return self._col(p.own, 0, p.dev_a)

    def _col(self, col, n, dev):
        piece = self.part(ALL, *col, self.p.r)
        return self._copy(piece, piece, n, dev)

    def _d(self, n):
        p = self.p
        return self._col((p.own, p.col_a, p.col_b, p.col_ab)[n], 3 + n, p.dev_d)

    def _keep(self):
        return pltpu.make_async_copy(self.own(self.p.r), self._mine(), self.local)

    def start(self):
        if self.wide:
            self._source(lambda: self._a().start())
        self._source(lambda: self._keep().start())
        self.line.start(self.own(self.p.r))

    def hop_one(self):
        self.line.hop(1)
        if self.wide:
            self._source(lambda: self._a().wait_recv())
            self.line_a.start(None)

    def hop_two(self):
        self.line.hop(2)
        if self.wide:
            self.line_a.hop(1)

    def after_z(self):
        p = self.p
        self._source(lambda: self._keep().wait())
        self.line.hop(3)
        if not self.wide:
            self._a().start()
        self._col(p.own, 1, p.dev_b).start()
        if self.halves:
            self._d(0).start()
        if self.wide:
            self.line_a.hop(2)

    def after_a(self):
        p = self.p
        if self.wide:
            self.line_a.hop(3)
        else:
            self._a().wait_recv()
        self._col(p.col_a, 2, p.dev_b).start()
        if self.halves:
            self._d(1).start()

    def after_b(self):
        p = self.p
        self._col(p.own, 1, p.dev_b).wait_recv()
        if self.halves:
            self._d(2).start()
        self._col(p.own, 2, p.dev_b).wait_recv()
        if self.halves:
            self._d(3).start()

    def done(self):
        if self.halves:
            for n in range(4):
                self._d(n).wait_recv()

    def drain(self):
        p = self.p
        self.line.drain()
        if self.wide:
            self.line_a.drain()
            self._source(lambda: self._a().wait_send())
        else:
            self._a().wait_send()
        self._col(p.own, 1, p.dev_b).wait_send()
        self._col(p.own, 2, p.dev_b).wait_send()
        if self.halves:
            for n in range(4):
                self._d(n).wait_send()


def add_into(dst, src):
    dst[...] = dst[...] + src[...]


class LineScatter:
    def __init__(self, scatter, col, base, down, up, direct=False):
        self.s, self.col, self.base, self.down, self.up, self.direct = scatter, col, base, down, up, direct

    def _straight(self, k):
        s = self.s
        zz, dev = s.p.z_dev(k)
        return s._copy(self._piece(zz), self.down.at[k], self.base + k, dev)

    def _piece(self, zs):
        s = self.s
        return s.part(zs, *self.col, s.p.r)

    def _send(self, lo, hi, step):
        s = self.s
        buf, n = (self.up, 0) if step > 0 else (self.down, 1)
        return s._copy(self._piece(slice(lo, hi)), buf.at[slice(lo, hi)], self.base + n, (s.p.r, s.p.i + 4 * step))

    def _moves(self):
        j = self.s.plane
        if j is None:
            return [(0, 3, 0, 3, -1), (0, 0, 1, 4, 1), (1, 2, 0, 2, -1), (1, 1, 2, 4, 1), (2, 1, 0, 1, -1), (2, 2, 3, 4, 1)]
        return [(3 - z, z, 0, 4, -1) for z in range(3, j, -1)] + [(z, z, 0, 4, 1) for z in range(j)]

    def _take(self, lo, hi, step):
        buf = self.up if step > 0 else self.down
        self._send(lo, hi, step).wait_recv()
        add_into(self._piece(slice(lo, hi)), buf.at[slice(lo, hi)])

    def step(self, k):
        if self.direct:
            if k == 0:
                for n in (3, 2, 1):
                    self._straight(n).start()
            if k == 3:
                for n in (1, 2, 3):
                    self._straight(n).wait_recv()
                    add_into(self._piece(self.s.p.z), self.down.at[n])
            return
        moves = self._moves()
        for rnd, z, lo, hi, way in moves:
            if rnd == k - 1:
                pl.when(self.s.p.z == z + way)(functools.partial(self._take, lo, hi, way))
        for rnd, z, lo, hi, way in moves:
            if rnd == k:
                pl.when(self.s.p.z == z)(lambda lo=lo, hi=hi, way=way: self._send(lo, hi, way).start())

    def drain(self):
        if self.direct:
            for n in (1, 2, 3):
                self._straight(n).wait_send()
            return
        for _, z, lo, hi, way in self._moves():
            pl.when(self.s.p.z == z)(lambda lo=lo, hi=hi, way=way: self._send(lo, hi, way).wait_send())


class Scatter:
    def __init__(self, place, part, bufs, out, sems, plane=None, wide=False, direct=False):
        self.p, self.part, self.out, self.plane, self.wide = place, part, out, plane, wide
        self.dbuf, self.bbuf, self.abuf, down, up, down_a, up_a = bufs
        self.send, self.recv = sems
        self.line = LineScatter(self, place.own, 8, down, up, direct)
        self.line_a = LineScatter(self, place.col_a, 10, down_a, up_a)

    def _copy(self, src, dst, n, dev):
        return remote(src, dst, self.send.at[n], self.recv.at[n], dev)

    def _d(self, zz):
        p = self.p
        return self._copy(self.part(zz, ALL, ALL, 1 - p.r), self.dbuf.at[zz], zz, p.dev_d)

    def _b(self, n):
        p = self.p
        col = (p.col_b, p.col_ab)[n]
        return self._copy(self.part(ALL, *col, p.r), self.bbuf.at[n], 4 + n, p.dev_b)

    def _a(self):
        p = self.p
        if self.wide and self.plane is None:
            return self._copy(self.part(p.z, *p.col_a, p.r), self.abuf.at[0], 6, p.dev_a)
        return self._copy(self.part(ALL, *p.col_a, p.r), self.abuf, 6, p.dev_a)

    def _here(self, act):
        if self.plane is None:
            act()
        else:
            pl.when(self.p.z == self.plane)(act)

    def _f(self):
        p = self.p
        return self._copy(self.out(p.r), self.out(p.r), 7, p.dev_d)

    def start(self):
        for zz in range(4):
            self._d(zz).start()

    def after_d(self):
        p = self.p
        for zz in range(4):
            self._d(zz).wait_recv()
        for n, col in enumerate((p.col_b, p.col_ab, p.col_a, p.own)):
            add_into(self.part(ALL, *col, p.r), self.dbuf.at[(ALL,) + col])
            if n < 2:
                self._b(n).start()

    def after_b(self):
        p = self.p
        self._b(1).wait_recv()
        add_into(self.part(ALL, *p.col_a, p.r), self.bbuf.at[1])
        if self.wide:
            self.line_a.step(0)
        else:
            self._a().start()
        self._b(0).wait_recv()
        add_into(self.part(ALL, *p.own, p.r), self.bbuf.at[0])
        if self.wide:
            self.line.step(0)

    def after_a(self):
        p = self.p
        if self.wide:
            self.line_a.step(1)
            self.line.step(1)
        else:
            self._a().wait_recv()
            add_into(self.part(ALL, *p.own, p.r), self.abuf)
            self.line.step(0)

    def line_one(self):
        if self.wide:
            self.line_a.step(2)
            self.line.step(2)
        else:
            self.line.step(1)

    def line_two(self):
        if self.wide:
            self.line_a.step(3)
            self._here(lambda: self._a().start())
        else:
            self.line.step(2)

    def last(self):
        self.line.step(3)
        self._here(self._finish)

    def _finish(self):
        p = self.p
        total = self.part(p.z if self.plane is None else ALL, *p.own, p.r)[...].astype(F32)
        if self.wide:
            self._a().wait_recv()
            total = total + self.abuf[0 if self.plane is None else ALL].astype(F32)
        self.out(p.r)[...] = total
        self._f().start()

    def done(self):
        self._here(lambda: self._f().wait_recv())

    def drain(self):
        for zz in range(4):
            self._d(zz).wait_send()
        for n in range(2):
            self._b(n).wait_send()
        self.line.drain()
        if self.wide:
            self.line_a.drain()
            self._here(lambda: self._a().wait_send())
        else:
            self._a().wait_send()
        self._here(lambda: self._f().wait_send())


class ScatterSmall:
    def __init__(self, place, ref, bufs, out, sems):
        self.p, self.ref, self.out = place, ref, out
        self.bbuf, self.abuf, self.zbuf, self.fbuf = bufs
        self.send, self.recv = sems

    def _copy(self, src, dst, n, dev):
        return remote(src, dst, self.send.at[n], self.recv.at[n], dev)

    def _b(self, n):
        p = self.p
        col = (p.col_b, p.col_ab)[n]
        return self._copy(self.ref.at[(ALL,) + col], self.bbuf.at[n], n, p.dev_b)

    def _a(self):
        p = self.p
        return self._copy(self.ref.at[(ALL,) + p.col_a], self.abuf, 2, p.dev_a)

    def _z(self, k):
        p = self.p
        zz, dev = p.z_dev(k)
        return self._copy(self.ref.at[(zz,) + p.own], self.zbuf.at[k - 1], 2 + k, dev)

    def _f(self):
        p = self.p
        return self._copy(self.out, self.fbuf, 6, p.dev_d)

    def start(self):
        self._b(0).start()
        self._b(1).start()

    def after_b(self):
        p = self.p
        self._b(0).wait_recv()
        self._b(1).wait_recv()
        self.ref[(ALL,) + p.col_a] += self.bbuf[1]
        self.ref[(ALL,) + p.own] += self.bbuf[0]
        self._a().start()

    def after_a(self):
        p = self.p
        self._a().wait_recv()
        self.ref[(ALL,) + p.own] += self.abuf[...]
        for k in (1, 2, 3):
            self._z(k).start()

    def after_z(self):
        p = self.p
        for k in (1, 2, 3):
            self._z(k).wait_recv()
        self.out[...] = self.ref[(p.z,) + p.own] + self.zbuf[0] + self.zbuf[1] + self.zbuf[2]
        self._f().start()

    def done(self):
        self._f().wait_recv()
        self._f().wait_send()
        self.out[...] = self.out[...] + self.fbuf[...]

    def drain(self):
        self._b(0).wait_send()
        self._b(1).wait_send()
        self._a().wait_send()
        for k in (1, 2, 3):
            self._z(k).wait_send()


ROWS_ALL = 768
IMAGE = 384
KEYS = 288
ALWAYS = 192
SLOTS = 4
WIDE_GATHER = (7, 9)
WIDE_SCATTER = (1, 3, 5)
DIRECT_GATHER = (0,)
DIRECT_SCATTER = (9, 10, 11)
NT = (((1,), (1,)), ((), ()))
TN = (((0,), (0,)), ((), ()))


def dots(a, b, dims=None):
    if dims is None:
        return jnp.dot(a, b, preferred_element_type=F32)
    return lax.dot_general(a, b, dims, preferred_element_type=F32)


def loop(count, body):
    def step(t, carry):
        body(t)
        return carry

    lax.fori_loop(0, count, step, 0)


def tiles(count, size, body):
    loop(count, lambda t: body(t, pl.ds(pl.multiple_of(t * size, size), size)))


def moments(v):
    centre = v - jnp.mean(v, axis=-1, keepdims=True)
    inverse = lax.rsqrt(jnp.mean(centre * centre, axis=-1, keepdims=True) + epsilon)
    return centre * inverse, inverse


def half(core):
    return pl.ds(pl.multiple_of(core * HALF, 128), HALF)


(OPEN, VECTORS, NORMED, GROUP, MIXED, PROJECT, SCALED, FEED, TWO, MIXED_BACK, PROJECT_BACK, BACK, GROWN, ONE, CLOSE) = range(15)
STEPS = (
    (Gather.start, Gather.hop_one, Gather.hop_two, Gather.after_z, Gather.after_a, Gather.after_b, Gather.done),
    (Scatter.start, Scatter.after_d, Scatter.after_b, Scatter.after_a, Scatter.line_one, Scatter.line_two, Scatter.last),
    (ScatterSmall.after_b, ScatterSmall.after_a, ScatterSmall.after_z),
)


PLAN = (
    ((OPEN,), ((0, 0, 0), (0, 1, 0), (0, 2, 0), (0, 3, 0), (0, 4, 0), (3, 0, 3), (0, 0, 1), (0, 0, 2), (0, 0, 3),
        (0, 1, 1), (0, 2, 1), (0, 5, 0), (3, 0, 4), (0, 3, 1), (0, 4, 1), (0, 1, 2), (0, 0, 4), (0, 2, 2), (3, 0, 5),
        (0, 1, 3), (0, 3, 2), (0, 5, 1), (0, 6, 0),)),
    ((VECTORS,), ((0, 0, 5), (0, 2, 3), (0, 7, 0),)),
    ((NORMED,), ((0, 4, 2),)),
    ((GROUP, 0, -1), ((0, 0, 6),)),
    ((GROUP, 0, -2), ((0, 3, 3),)),
    ((GROUP, 0, 0), ((0, 1, 4), (0, 5, 2),)),
    ((GROUP, 1, -1), ((0, 2, 4), (0, 6, 1), (0, 7, 1), (0, 3, 4), (0, 4, 3), (0, 8, 0), (0, 9, 0), (0, 5, 3),
        (0, 10, 0), (0, 1, 5), (0, 6, 2), (0, 6, 3), (0, 2, 5), (0, 1, 6),)),
    ((GROUP, 1, -2), ((0, 7, 2), (0, 3, 5), (0, 11, 0),)),
    ((GROUP, 1, 0), ((0, 4, 4), (0, 10, 1),)),
    ((GROUP, 1, 1), ((0, 8, 1),)),
    ((GROUP, 2, -1), ((0, 2, 6),)),
    ((GROUP, 2, -2), ((0, 9, 1),)),
    ((GROUP, 2, 0), ((0, 5, 4), (0, 7, 3),)),
    ((GROUP, 2, 0), ((0, 11, 1),)),
    ((MIXED,), ((0, 3, 6),)),
    ((PROJECT, 0), ((0, 6, 4), (0, 10, 2),)),
    ((PROJECT, 1), ((0, 8, 2), (0, 8, 3),)),
    ((SCALED,), ((0, 4, 5), (0, 9, 2),)),
    ((FEED, 0, 0), ((0, 7, 4), (0, 5, 5), (0, 11, 2), (0, 4, 6),)),
    ((FEED, 0, 2), ((0, 5, 6),)),
    ((FEED, 0, 3), ((0, 6, 5), (0, 10, 3),)),
    ((FEED, 0, 4), ((0, 8, 4), (0, 9, 3), (0, 11, 3),)),
    ((FEED, 0, 5), ((1, 0, 0),)),
    ((FEED, 0, 6), ((0, 7, 5),)),
    ((FEED, 0, 7), ((1, 1, 0),)),
    ((FEED, 1, 0), ((0, 6, 6),)),
    ((FEED, 1, 1), ((0, 9, 4), (0, 10, 4),)),
    ((FEED, 1, 2), ((0, 7, 6),)),
    ((FEED, 1, 3), ((0, 8, 5), (1, 1, 1),)),
    ((FEED, 1, 5), ((0, 11, 4), (1, 0, 1), (1, 2, 0),)),
    ((FEED, 1, 7), ((1, 3, 0), (1, 2, 1),)),
    ((FEED, 2, 0), ((0, 8, 6),)),
    ((FEED, 2, 1), ((0, 9, 5),)),
    ((FEED, 2, 2), ((0, 10, 5), (1, 3, 1), (0, 9, 6),)),
    ((FEED, 2, 3), ((1, 1, 2),)),
    ((FEED, 2, 4), ((0, 11, 5),)),
    ((FEED, 2, 5), ((1, 4, 0),)),
    ((FEED, 2, 7), ((1, 5, 0), (1, 0, 2), (1, 4, 1),)),
    ((FEED, 3, 0), ((0, 10, 6),)),
    ((FEED, 3, 2), ((0, 11, 6),)),
    ((FEED, 3, 3), ((1, 1, 3), (1, 2, 2), (1, 5, 1),)),
    ((FEED, 3, 5), ((1, 6, 0), (1, 3, 2),)),
    ((FEED, 3, 6), ((1, 0, 3),)),
    ((FEED, 3, 7), ((1, 7, 0), (1, 6, 1),)),
    ((TWO, 1), ((1, 1, 4), (1, 4, 2),)),
    ((TWO, 3), ((1, 2, 3), (1, 7, 1),)),
    ((PROJECT_BACK,), ((1, 8, 0), (1, 3, 3), (1, 5, 2), (1, 1, 5),)),
    ((BACK, 0, 1), ((1, 0, 4), (1, 6, 2), (1, 8, 1),)),
    ((BACK, 0, 1), ((1, 4, 3),)),
    ((BACK, 0, -1), ((1, 9, 0),)),
    ((BACK, 1, 0), ((1, 2, 4),)),
    ((BACK, 1, 0), ((1, 3, 4), (1, 7, 2),)),
    ((BACK, 1, 1), ((1, 1, 6), (1, 9, 1),)),
    ((BACK, 1, 1), ((1, 6, 3), (1, 0, 5),)),
    ((BACK, 1, -1), ((1, 10, 0), (1, 5, 3),)),
    ((BACK, 2, 0), ((1, 3, 5), (1, 2, 5), (1, 2, 6), (1, 8, 2),)),
    ((BACK, 2, 1), ((1, 4, 4), (1, 7, 3), (1, 10, 1),)),
    ((BACK, 2, -1), ((1, 11, 0), (1, 0, 6), (1, 6, 4),)),
    ((GROWN, 0), ((1, 3, 6), (1, 5, 4), (1, 9, 2),)),
    ((GROWN, 1), ((1, 8, 3), (1, 11, 1),)),
    ((GROWN, 2), ((1, 4, 5), (1, 4, 6), (1, 7, 4),)),
    ((ONE, 2), ((1, 10, 2),)),
    ((ONE, 4), ((1, 5, 5),)),
    ((ONE, 5), ((1, 9, 3), (1, 6, 5), (1, 9, 4), (1, 9, 5),)),
    ((CLOSE,), ((1, 8, 4), (1, 7, 5), (1, 11, 2), (1, 10, 3), (1, 10, 4), (1, 10, 5), (1, 5, 6), (2, 0, 0),
        (1, 9, 6), (1, 11, 3), (1, 11, 4), (1, 8, 5), (1, 11, 5), (1, 6, 6), (2, 0, 1), (1, 7, 6), (1, 10, 6),
        (2, 0, 2), (1, 11, 6), (1, 8, 6),)),
)


class Agenda:
    def __init__(self):
        self.calls = {}

    def at(self, point, *calls):
        self.calls.setdefault(point, []).extend(calls)

    def run(self, point):
        for call in self.calls.pop(point, []):
            call()

    def here(self, *place):
        for point in list(self.calls):
            if len(point) != len(place):
                continue
            test, fits = None, True
            for value, index in zip(point, place):
                if isinstance(index, int):
                    fits = fits and value == index
                elif value < 0:
                    fits = False
                else:
                    same = index == value
                    test = same if test is None else jnp.logical_and(test, same)
            if fits and test is None:
                self.run(point)
            elif fits:
                pl.when(test)(functools.partial(self.run, point))


def layer_kernel(
    tokens, cot, grids, keep_a, keep_m, g1, s1, bqv, bp, g2, s2, b1, b2, wq, wp, w1, w2,
    out_h, gt_h, oq_h, op_h, o1_h, o2_h, og1, os1, obqv, obp, og2, os2, ob1, ob2,
    x, ct, dz, h1, qkv, probs, mixed, y1, h2, dact, act, acc, dh,
    gu, gw2, stage, pack, packs, vec, flat, vqkv, vb1, dvec, dbqv, db1, outq, op, o1, o2, smalls, opack,
    dbuf, bbuf, abuf, lbuf, wbuf, sb, sa, sz, sf,
    gsend, grecv, glocal, tsend, trecv, tlocal, ssend, srecv, usend, urecv, local,
):
    place = Place()
    load_x = pltpu.make_async_copy(tokens, x, local.at[0])
    load_c = pltpu.make_async_copy(cot, ct, local.at[1])
    groups_of_four = [(g, k, slice(256 * k, 256 * k + 256), slice(768 * k + 256 * g, 768 * k + 256 * g + 256)) for g in range(3) for k in range(3)]
    regroup = [pltpu.make_async_copy(wq.at[:, there], stage.at[g, :, here], local.at[4 + 3 * g + k]) for g, k, here, there in groups_of_four]
    for copy in regroup:
        copy.start()
    load_x.start()
    load_c.start()
    pack[...] = jnp.zeros_like(pack)
    for row, ref in enumerate((g1, s1, bp, g2, s2, b2)):
        pack[row : row + 1, 0:48] = ref[...].astype(F32).reshape(1, 48)
    pack[6:7, 0:96] = bqv[...].astype(F32).reshape(1, 96)
    both = b1[...].astype(F32).reshape(1, 192)
    pack[7:8, 0:96] = both[:, :96]
    pack[8:9, 0:96] = both[:, 96:]
    greet(place)

    tiny = Gather(place, lambda zs, y, xx, core: packs.at[zs, y, xx], lambda core: pack, (tsend, trecv), tlocal, halves=False, direct=True)

    def block(u):
        return lambda zs, y, xx, core: gu.at[u, zs, y, xx, :, half(core)]

    def plane_part(j):
        return lambda zs, y, xx, core: gw2.at[j, y, xx, zs, :, half(core)]

    def fc1_cols(j, core):
        return pl.ds(pl.multiple_of(WIDE * j + core * HALF, 128), HALF)

    pieces = [(block(g), lambda core, g=g: stage.at[g, :, half(core)], None) for g in range(3)]
    pieces.append((block(3), lambda core: wp.at[:, half(core)], None))
    for j in range(4):
        pieces.append((plane_part(j), lambda core: w2.at[:, :, half(core)], j))
        pieces.append((block(4 + j), lambda core, j=j: w1.at[:, fc1_cols(j, core)], None))
    units = [
        Gather(place, part, own, (gsend.at[n], grecv.at[n]), glocal.at[n], wide=n in WIDE_GATHER, plane=plane, direct=n in DIRECT_GATHER)
        for n, (part, own, plane) in enumerate(pieces)
    ]

    def gq_part(g):
        return lambda zs, y, xx, core: dact.at[g, zs, y, xx, :, half(core)]

    plans = []
    for j in range(4):
        plans.append((plane_part(j), lambda core: o2.at[:, :, half(core)], j))
        plans.append((block(4 + j), lambda core, j=j: o1.at[:, fc1_cols(j, core)], None))
    plans.append((block(3), lambda core: op.at[:, half(core)], None))
    for g in range(3):
        plans.append((gq_part(g), lambda core, g=g: outq.at[g, :, half(core)], None))
    sends = []
    for n, (part, out, plane) in enumerate(plans):
        wide = n in WIDE_SCATTER
        extra = [wbuf.at[WIDE_SCATTER.index(n), k] for k in range(2)] if wide else [None, None]
        bufs = [dbuf.at[n % SLOTS], bbuf.at[n], abuf.at[n], lbuf.at[n, 0], lbuf.at[n, 1]] + extra
        sends.append(Scatter(place, part, bufs, out, (ssend.at[n], srecv.at[n]), plane, wide, n in DIRECT_SCATTER))
    small = ScatterSmall(place, smalls, (sb, sa, sz, sf), opack, (usend, urecv))

    agenda = Agenda()
    groups = (units, sends, [small], [tiny])
    for point, steps in PLAN:
        for kind, n, step in steps:
            step = STEPS[min(kind, 2)][step] if kind < 3 else STEPS[0][step]
            agenda.at(point, functools.partial(step, groups[kind][n]))

    tiny.start()
    for copy in regroup:
        copy.wait()
    agenda.here(OPEN)
    for s in range(16):
        at = (s // 4, (s // 2) % 2, s % 2)
        vec[:, 48 * s : 48 * s + 48] = packs[at + (slice(0, 8), slice(0, 48))]
        c = 192 * (s % 4)
        vb1[s // 4, :, c : c + 96] = packs[at + (slice(7, 8), slice(0, 96))]
        vb1[s // 4, :, c + 96 : c + 192] = packs[at + (slice(8, 9), slice(0, 96))]
        c = 96 * s + 768 * (s // 8)
        flat[:, c : c + 96] = packs[at + (slice(6, 7), slice(0, 96))]
    flat[:, 768:1536] = jnp.zeros((1, 768), F32)
    for g in range(3):
        for k in range(3):
            vqkv[g, :, 256 * k : 256 * k + 256] = flat[:, 768 * k + 256 * g : 768 * k + 256 * g + 256]
    dvec[...] = jnp.zeros_like(dvec)
    dbqv[...] = jnp.zeros_like(dbqv)

    agenda.here(VECTORS)
    load_x.wait()

    def norm_one(t, rows):
        n, _ = moments(x[rows, :].astype(F32))
        h1[rows, :] = (n * vec[0:1, :] + vec[1:2, :]).astype(BF16)

    tiles(6, 128, norm_one)
    agenda.here(NORMED)

    lane = lax.broadcasted_iota(jnp.int32, (1, 128), 1) // HEAD

    def pair(g, t):
        base = pl.multiple_of(t // 2 * IMAGE, IMAGE)
        at = [pl.ds(pl.multiple_of(256 * k + 128 * (t % 2), 128), 128) for k in range(3)]
        q = qkv[g, pl.ds(base, IMAGE), at[0]] * BF16(0.125)
        k = qkv[g, pl.ds(base, KEYS), at[1]]
        v = qkv[g, pl.ds(base, KEYS), at[2]]
        col = pl.ds(pl.multiple_of(256 * g + 128 * (t % 2), 128), 128)
        return base, at, q, k, v, col

    def attend(g, i):
        length = grids[i, 0] * grids[i, 1] + 2
        key = lax.broadcasted_iota(jnp.int32, (KEYS - ALWAYS, IMAGE), 0) + ALWAYS
        found = []
        for t in (2 * i, 2 * i + 1):
            base, at, q, k, v, col = pair(g, t)
            total, kept_probs = None, []
            for h in range(2):
                qh = jnp.where(lane == h, q, BF16(0))
                vh = jnp.where(lane == h, v, BF16(0))
                s = dots(k, qh, NT)
                s = jnp.concatenate([s[:ALWAYS], jnp.where(key < length, s[ALWAYS:], -1000000000.0)], axis=0)
                e = jnp.exp(s - jnp.max(s, axis=0, keepdims=True))
                p = (e * (1.0 / jnp.sum(e, axis=0, keepdims=True))).astype(BF16)
                kept_probs.append(p)
                o = dots(p, vh, TN)
                total = o if total is None else total + o
            found.append((t, base, col, total, kept_probs))
        for t, base, col, total, kept_probs in found:
            for h in range(2):
                probs[8 * g + 2 * t + h] = kept_probs[h]
            mixed[pl.ds(base, IMAGE), col] = total.astype(BF16)
        agenda.here(GROUP, g, i)

    def forward_group(g):
        agenda.here(GROUP, g, -1)
        qkv[g] = (dots(h1[...], gu[g].reshape(768, 768)) + vqkv[g]).astype(BF16)
        agenda.here(GROUP, g, -2)
        loop(2, functools.partial(attend, g))

    loop(3, forward_group)

    def kept(ref, b):
        return ref[b].astype(F32) * (1.0 / 0.9)

    agenda.here(MIXED)

    def project(b):
        rows = pl.ds(pl.multiple_of(b * IMAGE, IMAGE), IMAGE)
        y = x[rows, :].astype(F32) + kept(keep_a, b) * (dots(mixed[rows, :], gu[3].reshape(768, 768)) + vec[2:3, :])
        y1[rows, :] = y
        n, _ = moments(y)
        h2[rows, :] = (n * vec[3:4, :] + vec[4:5, :]).astype(BF16)
        agenda.here(PROJECT, b)

    loop(2, project)
    load_c.wait()

    def scale_dz(t, rows):
        d = (ct[rows, :].astype(F32) * kept(keep_m, t // 3)).astype(BF16)
        dz[rows, :] = d
        dvec[5:6, :] += jnp.sum(d.astype(F32), axis=0, keepdims=True)

    tiles(6, 128, scale_dz)
    acc[...] = jnp.zeros_like(acc)
    dh[...] = jnp.zeros_like(dh)
    agenda.here(SCALED)
    units[3].drain()

    def feed(j):
        agenda.here(FEED, j, 0)
        dact[j] = dots(dz[...], gw2[j].reshape(768, 768), NT).astype(BF16).reshape(4, 2, 2, ROWS, 768)
        agenda.here(FEED, j, 1)
        agenda.here(FEED, j, 2)
        pre = dots(h2[...], gu[j + 4].reshape(768, 768)) + vb1[j]
        u = 0.5 * (1.0 + lax.erf(pre * root_half))
        act[...] = (pre * u).astype(BF16)
        d = dact[j].reshape(768, 768).astype(F32) * (u + pre * jnp.exp(-0.5 * pre * pre) * 0.3989422804014327)
        db1[j] = jnp.sum(d, axis=0, keepdims=True)
        dact[j] = d.astype(BF16).reshape(4, 2, 2, ROWS, 768)
        agenda.here(FEED, j, 3)
        acc[...] += dots(act[...], gw2[j].reshape(768, 768))
        agenda.here(FEED, j, 4)
        for n in range(4):
            pl.when(j == n)(units[4 + 2 * n].drain)
        gw2[j] = dots(act[...], dz[...], TN).astype(BF16).reshape(2, 2, 4, ROWS, 768)
        agenda.here(FEED, j, 5)
        dh[...] += dots(dact[j].reshape(768, 768), gu[j + 4].reshape(768, 768), NT)
        agenda.here(FEED, j, 6)
        for n in range(4):
            pl.when(j == n)(units[5 + 2 * n].drain)
        gu[j + 4] = dots(h2[...], dact[j].reshape(768, 768), TN).astype(BF16).reshape(4, 2, 2, ROWS, 768)
        agenda.here(FEED, j, 7)

    loop(4, feed)

    def norm_two_back(t, rows):
        y = y1[rows, :]
        act[rows, :] = (y + kept(keep_m, t // 3) * (acc[rows, :] + vec[5:6, :])).astype(BF16)
        acc[rows, :] = jnp.zeros((128, 768), F32)
        n, inverse = moments(y)
        d = dh[rows, :]
        e = d * vec[3:4, :]
        back = inverse * (e - jnp.mean(e, axis=-1, keepdims=True) - n * jnp.mean(e * n, axis=-1, keepdims=True))
        back = ct[rows, :].astype(F32) + back
        dh[rows, :] = back
        da = (back * kept(keep_a, t // 3)).astype(BF16)
        h2[rows, :] = da
        dvec[3:4, :] += jnp.sum(d * n, axis=0, keepdims=True)
        dvec[4:5, :] += jnp.sum(d, axis=0, keepdims=True)
        dvec[2:3, :] += jnp.sum(da.astype(F32), axis=0, keepdims=True)
        agenda.here(TWO, t)

    tiles(6, 128, norm_two_back)
    save_out = pltpu.make_async_copy(act, out_h, local.at[2])
    save_out.start()
    dz[...] = dots(h2[...], gu[3].reshape(768, 768), NT).astype(BF16)
    agenda.here(MIXED_BACK)
    gu[3] = dots(mixed[...], h2[...], TN).astype(BF16).reshape(4, 2, 2, ROWS, 768)
    agenda.here(PROJECT_BACK)

    def attend_back(g, i):
        found = []
        for t in (2 * i, 2 * i + 1):
            base, at, q, k, v, col = pair(g, t)
            do = dz[pl.ds(base, IMAGE), col]
            dq = dk = dv = None
            for h in range(2):
                qh = jnp.where(lane == h, q, BF16(0))
                kh = jnp.where(lane == h, k, BF16(0))
                doh = jnp.where(lane == h, do, BF16(0))
                p = probs[8 * g + 2 * t + h]
                pf = p.astype(F32)
                dp = dots(v, doh, NT)
                ds = (pf * (dp - jnp.sum(pf * dp, axis=0, keepdims=True))).astype(BF16)
                new = (dots(ds, kh, TN), dots(ds, qh), dots(p, doh))
                dq, dk, dv = new if dq is None else (dq + new[0], dk + new[1], dv + new[2])
            found.append((base, at, col, dq * 0.125, dk, dv))
        none = jnp.zeros((IMAGE - KEYS, 128), BF16)
        for base, at, col, dq, dk, dv in found:
            qkv[g, pl.ds(base, IMAGE), at[0]] = dq.astype(BF16)
            qkv[g, pl.ds(base, KEYS), at[1]] = dk.astype(BF16)
            qkv[g, pl.ds(base, KEYS), at[2]] = dv.astype(BF16)
            qkv[g, pl.ds(base + KEYS, IMAGE - KEYS), at[1]] = none
            qkv[g, pl.ds(base + KEYS, IMAGE - KEYS), at[2]] = none
            dbqv[0, :, col] += jnp.sum(dq, axis=0, keepdims=True)
            dbqv[1, :, col] += jnp.sum(dv, axis=0, keepdims=True)
        agenda.here(BACK, g, i)

    def back_group(g):
        loop(2, functools.partial(attend_back, g))
        dact[g] = dots(h1[...], qkv[g], TN).astype(BF16).reshape(4, 2, 2, ROWS, 768)
        agenda.here(BACK, g, -1)

    loop(3, back_group)

    def grow(g):
        acc[...] += dots(qkv[g], gu[g].reshape(768, 768), NT)
        agenda.here(GROWN, g)

    loop(3, grow)

    def norm_one_back(t, rows):
        n, inverse = moments(x[rows, :].astype(F32))
        d = acc[rows, :]
        e = d * vec[0:1, :]
        back = inverse * (e - jnp.mean(e, axis=-1, keepdims=True) - n * jnp.mean(e * n, axis=-1, keepdims=True))
        dh[rows, :] += back
        dvec[0:1, :] += jnp.sum(d * n, axis=0, keepdims=True)
        dvec[1:2, :] += jnp.sum(d, axis=0, keepdims=True)
        agenda.here(ONE, t)

    tiles(6, 128, norm_one_back)
    save_gt = pltpu.make_async_copy(dh, gt_h, local.at[3])
    save_gt.start()
    smalls[...] = jnp.zeros_like(smalls)
    for s in range(16):
        at = (s // 4, (s // 2) % 2, s % 2)
        smalls[at + (slice(0, 8), slice(0, 48))] = dvec[:, 48 * s : 48 * s + 48]
        c = 96 * (s % 8)
        smalls[at + (slice(6, 7), slice(0, 96))] = dbqv[s // 8, :, c : c + 96]
        c = 192 * (s % 4)
        smalls[at + (slice(7, 8), slice(0, 96))] = db1[s // 4, :, c : c + 96]
        smalls[at + (slice(8, 9), slice(0, 96))] = db1[s // 4, :, c + 96 : c + 192]
    small.start()
    agenda.here(CLOSE)
    saves = []
    for n, unit in enumerate(sends):
        unit.done()
        if n < 8 and n % 2 == 0:
            continue
        if n == 7:
            pairs = [(o1, o1_h), (o2, o2_h)]
        elif n == 8:
            pairs = [(op, op_h)]
        elif n > 8:
            pairs = [(outq.at[g, :, here], oq_h.at[:, there]) for g, k, here, there in groups_of_four if g == n - 9]
        else:
            pairs = []
        for src, dst in pairs:
            saves.append(pltpu.make_async_copy(src, dst, local.at[13 + len(saves)]))
            saves[-1].start()
    small.done()
    assert not agenda.calls
    for row, ref in enumerate((og1, os1, obp, og2, os2, ob2)):
        ref[...] = opack[row : row + 1, 0:48].reshape(48)
    obqv[...] = opack[6:7, 0:96].reshape(96)
    ob1[...] = jnp.concatenate([opack[7:8, 0:96], opack[8:9, 0:96]], axis=1).reshape(192)
    for unit in [units[0], units[1], units[2], tiny, small] + sends:
        unit.drain()
    for copy in [save_out, save_gt] + saves:
        copy.wait()


def handover_kernel(*refs):
    count = len(refs) // 4
    ins, outs, held, sems = (refs[n * count : (n + 1) * count] for n in range(4))
    takes = [pltpu.make_async_copy(ins[n], held[n], sems[n].at[0]) for n in range(count)]
    gives = [pltpu.make_async_copy(held[n], outs[n], sems[n].at[1]) for n in range(count)]
    for copy in takes:
        copy.start()
    for take, give in zip(takes, gives):
        take.wait()
        give.start()
    for copy in gives:
        copy.wait()


def handover(arrays):
    specs = [pl.BlockSpec(memory_space=pltpu.HBM)] * len(arrays)
    return pl.pallas_call(
        handover_kernel,
        out_shape=[jax.ShapeDtypeStruct(a.shape, a.dtype) for a in arrays],
        in_specs=specs,
        out_specs=specs,
        scratch_shapes=[pltpu.VMEM(a.shape, a.dtype) for a in arrays] + [pltpu.SemaphoreType.DMA((2,))] * len(arrays),
        name="handover",
    )(*arrays)


def by_block(tokens, grids, keep_attn, keep_mlp, cotangent, *params):
    g1, s1, wq, bqv, wp, bp, g2, s2, w1, b1, w2, b2 = params
    rows = lambda v: v.reshape(ROWS_ALL, 768)
    vm, sm, hbm = (pl.BlockSpec(memory_space=m) for m in (pltpu.VMEM, pltpu.SMEM, pltpu.HBM))
    S = jax.ShapeDtypeStruct
    v = lambda *shape: pltpu.VMEM(shape, BF16)
    f = lambda *shape: pltpu.VMEM(shape, F32)
    dma = lambda *shape: pltpu.SemaphoreType.DMA(shape)
    outs = pl.pallas_call(
        layer_kernel,
        out_shape=[S((ROWS_ALL, 768), BF16), S((ROWS_ALL, 768), F32)]
        + [S(w.shape, F32) for w in (wq, wp, w1)]
        + [S((4, ROWS, 768), F32)]
        + [S(w.shape, F32) for w in (g1, s1, bqv, bp, g2, s2, b1, b2)],
        in_specs=[hbm] * 2 + [sm] * 3 + [vm] * 8 + [hbm] * 4,
        out_specs=[hbm] * 6 + [vm] * 8,
        scratch_shapes=[
            v(768, 768), v(768, 768), v(768, 768), v(768, 768), v(3, 768, 768), v(24, KEYS, IMAGE), v(768, 768), f(768, 768),
            v(768, 768), v(4, 4, 2, 2, ROWS, 768), v(768, 768), f(768, 768), f(768, 768),
            v(8, 4, 2, 2, ROWS, 768), v(4, 2, 2, 4, ROWS, 768), v(3, ROWS, 768), f(16, 128), f(4, 2, 2, 16, 128),
            f(8, 768), f(1, 2304), f(3, 1, 768), f(4, 1, 768), f(8, 768), f(2, 1, 768), f(4, 1, 768), f(3, ROWS, 768),
            f(ROWS, 768), f(ROWS, 3072), f(4, ROWS, 768), f(4, 2, 2, 16, 128), f(16, 128),
            v(SLOTS, 4, 2, 2, ROWS, HALF), v(12, 2, 4, ROWS, HALF), v(12, 4, ROWS, HALF),
            v(12, 2, 4, ROWS, HALF), v(len(WIDE_SCATTER), 2, 4, ROWS, HALF),
            f(2, 4, 16, 128), f(4, 16, 128), f(3, 16, 128), f(16, 128),
            dma(12, 22), dma(12, 22), dma(12), dma(22), dma(22), dma(), dma(12, 12), dma(12, 12), dma(8), dma(8), dma(26),
        ],
        compiler_params=pltpu.CompilerParams(collective_id=0, has_side_effects=True, vmem_limit_bytes=62 << 20),
        cost_estimate=pl.CostEstimate(flops=36 * 10**9, bytes_accessed=10**7, transcendentals=10**7),
        name="layer",
    )(
        rows(tokens), rows(cotangent), grids, keep_attn, keep_mlp, g1, s1, bqv, bp, g2, s2, b1, b2, wq, wp, w1,
        w2.reshape(4, ROWS, 768),
    )
    out, gt, oq, op, o1, o2, og1, os1, obqv, obp, og2, os2, ob1, ob2 = handover(outs)
    return (
        out.reshape(tokens.shape), gt.reshape(tokens.shape), og1, os1, oq, obqv, op, obp, og2, os2, o1, ob1,
        o2.reshape(w2.shape), ob2,
    )


def layer_norm(stream, gain, shift):
    center = jnp.mean(stream, axis=-1, keepdims=True)
    shifted = stream - center
    inverse = lax.rsqrt(jnp.mean(shifted * shifted, axis=-1, keepdims=True) + epsilon)
    normed = shifted * inverse
    return (normed * gain + shift, normed, inverse)


def norm_back(grad_normed, normed, inverse, gain):
    scaled = grad_normed * gain
    grad_input = inverse * (
        scaled
        - jnp.mean(scaled, axis=-1, keepdims=True)
        - normed * jnp.mean(scaled * normed, axis=-1, keepdims=True)
    )
    return (grad_input, jnp.sum(grad_normed * normed, axis=0), jnp.sum(grad_normed, axis=0))


def gelu_exact(values):
    return 0.5 * values * (1.0 + lax.erf(values * root_half))


def outer_sum(left, right):
    return lax.dot_general(left, right, (((0,), (0,)), ((), ())), preferred_element_type=F32)


def back_dot(left, right):
    return lax.dot_general(left, right, (((1,), (1,)), ((), ())), preferred_element_type=F32)


def layer(tokens, grids, keep_attn, keep_mlp, cotangent, params):
    ln1_gain, ln1_shift, w_qkv, bias_qv, w_proj, bias_proj, ln2_gain, ln2_shift, w_fc1, bias_fc1, w_fc2, bias_fc2 = params
    images, seq_len, feat_dim = tokens.shape
    num_heads = feat_dim // HEAD
    row_count = images * seq_len
    lengths = grids[:, 0] * grids[:, 1] + 2
    key_valid = lax.broadcasted_iota(jnp.int32, (images, seq_len), 1) < lengths[:, None]
    scale_attn = jnp.broadcast_to((keep_attn.astype(F32) / 0.9)[:, None], (images, seq_len)).reshape(row_count, 1)
    scale_mlp = jnp.broadcast_to((keep_mlp.astype(F32) / 0.9)[:, None], (images, seq_len)).reshape(row_count, 1)
    stream = tokens.astype(F32).reshape(row_count, feat_dim)
    normed_out, normed_one, inverse_one = layer_norm(stream, ln1_gain, ln1_shift)
    normed_low_one = normed_out.astype(BF16)
    full_bias = jnp.concatenate([bias_qv[:feat_dim], jnp.zeros((feat_dim,), F32), bias_qv[feat_dim:]])
    triple = jnp.dot(normed_low_one, w_qkv, preferred_element_type=F32) + full_bias
    triple = triple.astype(BF16).reshape(images, seq_len, 3, num_heads, HEAD)
    queries, key_rows, values = triple[:, :, 0], triple[:, :, 1], triple[:, :, 2]
    scores = jnp.einsum("bqhe,bkhe->bhqk", queries, key_rows, preferred_element_type=F32) * 0.125
    scores = jnp.where(key_valid[:, None, None, :], scores, -1000000000.0)
    probs_full = jax.nn.softmax(scores, axis=-1)
    probs_low = probs_full.astype(BF16)
    mixed_low = jnp.einsum("bhqk,bkhe->bqhe", probs_low, values, preferred_element_type=F32)
    mixed_low = mixed_low.reshape(row_count, feat_dim).astype(BF16)
    branch = jnp.dot(mixed_low, w_proj, preferred_element_type=F32) + bias_proj
    middle = stream + scale_attn * branch
    normed_out, normed_two, inverse_two = layer_norm(middle, ln2_gain, ln2_shift)
    normed_low_two = normed_out.astype(BF16)
    pre_act = jnp.dot(normed_low_two, w_fc1, preferred_element_type=F32) + bias_fc1
    act_value, act_pullback = jax.vjp(gelu_exact, pre_act)
    act_low = act_value.astype(BF16)
    branch_two = jnp.dot(act_low, w_fc2, preferred_element_type=F32) + bias_fc2
    layer_out = (middle + scale_mlp * branch_two).astype(BF16).reshape(images, seq_len, feat_dim)
    grad_out = cotangent.astype(F32).reshape(row_count, feat_dim)
    grad_branch_two = (grad_out * scale_mlp).astype(BF16)
    grad_fc2 = outer_sum(act_low, grad_branch_two)
    grad_fc2_bias = jnp.sum(grad_branch_two.astype(F32), axis=0)
    grad_act = back_dot(grad_branch_two, w_fc2)
    grad_pre = act_pullback(grad_act)[0].astype(BF16)
    grad_fc1 = outer_sum(normed_low_two, grad_pre)
    grad_fc1_bias = jnp.sum(grad_pre.astype(F32), axis=0)
    grad_normed_two = back_dot(grad_pre, w_fc1)
    grad_middle, grad_gain_two, grad_shift_two = norm_back(grad_normed_two, normed_two, inverse_two, ln2_gain)
    grad_middle = grad_middle + grad_out
    grad_branch = (grad_middle * scale_attn).astype(BF16)
    grad_proj = outer_sum(mixed_low, grad_branch)
    grad_proj_bias = jnp.sum(grad_branch.astype(F32), axis=0)
    grad_mixed = back_dot(grad_branch, w_proj).astype(BF16).reshape(images, seq_len, num_heads, HEAD)
    grad_values = jnp.einsum("bhqk,bqhe->bkhe", probs_low, grad_mixed, preferred_element_type=F32)
    grad_probs = jnp.einsum("bqhe,bkhe->bhqk", grad_mixed, values, preferred_element_type=F32)
    row_delta = jnp.sum(probs_full * grad_probs, axis=-1, keepdims=True)
    grad_scores = (probs_full * (grad_probs - row_delta)).astype(BF16)
    grad_queries = jnp.einsum("bhqk,bkhe->bqhe", grad_scores, key_rows, preferred_element_type=F32) * 0.125
    grad_keys = jnp.einsum("bhqk,bqhe->bkhe", grad_scores, queries, preferred_element_type=F32) * 0.125
    grad_triple = jnp.stack([grad_queries, grad_keys, grad_values], axis=2).astype(BF16).reshape(row_count, 3 * feat_dim)
    grad_qkv = outer_sum(normed_low_one, grad_triple)
    column_sums = jnp.sum(grad_triple.astype(F32), axis=0)
    grad_pair = jnp.concatenate([column_sums[:feat_dim], column_sums[2 * feat_dim :]])
    grad_normed_one = back_dot(grad_triple, w_qkv)
    grad_input, grad_gain_one, grad_shift_one = norm_back(grad_normed_one, normed_one, inverse_one, ln1_gain)
    grad_input = (grad_input + grad_middle).reshape(images, seq_len, feat_dim)
    grads = (
        grad_gain_one, grad_shift_one, grad_qkv, grad_pair, grad_proj, grad_proj_bias,
        grad_gain_two, grad_shift_two, grad_fc1, grad_fc1_bias, grad_fc2, grad_fc2_bias,
    )
    return layer_out, grad_input, grads


def by_collectives(tokens, grids, keep_attn, keep_mlp, cotangent, *params):
    whole = [lax.all_gather(p, "fsdp", axis=0, tiled=True) for p in params]
    whole = [p.astype(F32) if p.ndim == 1 else p for p in whole]
    layer_out, grad_input, grads = layer(tokens, grids, keep_attn, keep_mlp, cotangent, whole)
    shards = [lax.psum_scatter(g, "fsdp", scatter_dimension=0, tiled=True) for g in grads]
    totals = [lax.psum(g.astype(BF16), "rep").astype(F32) for g in shards]
    return (layer_out, grad_input) + tuple(totals)


def solution(mesh):
    vec, mat, rows = P("fsdp"), P("fsdp", None), P(("rep", "fsdp"))
    image = P(("rep", "fsdp"), None, None)
    weights = (vec, vec, mat, vec, mat, vec, vec, vec, mat, vec, mat, vec)
    in_specs = (image, P(("rep", "fsdp"), None), rows, rows, image) + weights
    out_specs = (image, image) + weights
    block = mesh.shape["fsdp"] == 16 and mesh.shape["rep"] == 2
    return jax.shard_map(
        by_block if block else by_collectives, mesh=mesh, in_specs=in_specs, out_specs=out_specs, check_vma=False
    )
```

```python
import functools

import jax
import jax.numpy as jnp
from jax import lax
from jax.experimental import pallas as pl
from jax.experimental.pallas import tpu as pltpu
from jax.sharding import PartitionSpec as P

HEAD = 64
MESH = pl.DeviceIdType.MESH
F32 = jnp.float32
BF16 = jnp.bfloat16
epsilon = 1e-06
root_half = 0.7071067811865476

ROWS = 48
WIDE = 768
HALF = 384
ALL = slice(None)


class Place:
    def __init__(self):
        self.r = lax.axis_index("rep")
        self.i = lax.axis_index("fsdp")
        r, i = self.r, self.i
        self.z = i // 4
        self.y = (i // 2) % 2
        self.x = i % 2
        fx, fy = 1 - 2 * self.x, 1 - 2 * self.y
        self.dev_a = (r, i + (1 - r) * fx + r * 2 * fy)
        self.dev_b = (r, i + (1 - r) * 2 * fy + r * fx)
        self.dev_d = (1 - r, i)
        self.own = (self.y, self.x)
        self.col_a = (self.y + r * fy, self.x + (1 - r) * fx)
        self.col_b = (self.y + (1 - r) * fy, self.x + r * fx)
        self.col_ab = (1 - self.y, 1 - self.x)

    def z_dev(self, k):
        zz = (self.z + k) % 4
        return zz, (self.r, zz * 4 + self.i % 4)


def greet(place):
    barrier = pltpu.get_barrier_semaphore()
    for dev in (place.z_dev(1)[1], place.z_dev(2)[1], place.z_dev(3)[1], place.dev_a, place.dev_b, place.dev_d):
        pl.semaphore_signal(barrier, inc=1, device_id=dev, device_id_type=MESH)
    pl.semaphore_wait(barrier, 6)


def remote(src, dst, send, recv, dev):
    return pltpu.make_async_remote_copy(
        src_ref=src, dst_ref=dst, send_sem=send, recv_sem=recv, device_id=dev, device_id_type=MESH
    )


class LineGather:
    def __init__(self, gather, col, base, direct=False):
        self.g, self.col, self.base, self.direct = gather, col, base, direct

    def _straight(self, src, k):
        g = self.g
        p = g.p
        piece = g.part(p.z, *self.col, p.r)
        return g._copy(piece if src is None else src, piece, self.base + k - 1, p.z_dev(k)[1])

    def _send(self, src, zz, n, step):
        g = self.g
        p = g.p
        piece = g.part(ALL if g.plane is not None else zz, *self.col, p.r)
        dev = (p.r, p.i + 4 * step)
        return g._copy(piece if src is None else src, piece, self.base + n, dev)

    def sends(self, k, act, src=None):
        z, plane = self.g.p.z, self.g.plane
        if self.direct:
            for n in (3, 2, 1) if k == 0 else ():
                act(self._straight(src, n))
        elif plane is None:
            pl.when(jnp.logical_and(z >= k, z < 3))(lambda: act(self._send(src, z - k, k, 1)))
            pl.when(jnp.logical_and(z <= 3 - k, z > 0))(lambda: act(self._send(src, z + k, 3 + k, -1)))
        else:
            if plane + k < 3:
                pl.when(z == plane + k)(lambda: act(self._send(src, z, 0, 1)))
            if plane - k > 0:
                pl.when(z == plane - k)(lambda: act(self._send(src, z, 3, -1)))

    def start(self, src):
        self.sends(0, lambda copy: copy.start(), src)

    def hop(self, k):
        z, plane = self.g.p.z, self.g.plane
        if self.direct:
            for n in (1, 2, 3) if k == 3 else ():
                self._straight(None, n).wait_recv()
        elif plane is None:
            pl.when(z >= k)(lambda: self._send(None, z, k - 1, 0).wait_recv())
            pl.when(z <= 3 - k)(lambda: self._send(None, z, 2 + k, 0).wait_recv())
        else:
            if plane + k <= 3:
                pl.when(z == plane + k)(lambda: self._send(None, z, 0, 0).wait_recv())
            if plane - k >= 0:
                pl.when(z == plane - k)(lambda: self._send(None, z, 3, 0).wait_recv())
        if k < 3:
            self.sends(k, lambda copy: copy.start())

    def drain(self):
        for k in range(3):
            self.sends(k, lambda copy: copy.wait_send())


class Gather:
    def __init__(self, place, part, own, sems, local, halves=True, wide=False, plane=None, direct=False):
        self.p, self.part, self.own, self.plane = place, part, own, plane
        self.send, self.recv = sems
        self.local, self.halves, self.wide = local, halves, wide
        self.line = LineGather(self, place.own, 10, direct)
        self.line_a = LineGather(self, place.col_a, 16)

    def _mine(self):
        p = self.p
        return self.part(p.z if self.plane is None else ALL, *p.own, p.r)

    def _source(self, act):
        if self.plane is None:
            act()
        else:
            pl.when(self.p.z == self.plane)(act)

    def _copy(self, src, dst, n, dev):
        return remote(src, dst, self.send.at[n], self.recv.at[n], dev)

    def _a(self):
        p = self.p
        if self.wide:
            return self._copy(self.own(p.r), self._mine(), 0, p.dev_a)
        return self._col(p.own, 0, p.dev_a)

    def _col(self, col, n, dev):
        piece = self.part(ALL, *col, self.p.r)
        return self._copy(piece, piece, n, dev)

    def _d(self, n):
        p = self.p
        return self._col((p.own, p.col_a, p.col_b, p.col_ab)[n], 3 + n, p.dev_d)

    def _keep(self):
        return pltpu.make_async_copy(self.own(self.p.r), self._mine(), self.local)

    def start(self):
        if self.wide:
            self._source(lambda: self._a().start())
        self._source(lambda: self._keep().start())
        self.line.start(self.own(self.p.r))

    def hop_one(self):
        self.line.hop(1)
        if self.wide:
            self._source(lambda: self._a().wait_recv())
            self.line_a.start(None)

    def hop_two(self):
        self.line.hop(2)
        if self.wide:
            self.line_a.hop(1)

    def after_z(self):
        p = self.p
        self._source(lambda: self._keep().wait())
        self.line.hop(3)
        if not self.wide:
            self._a().start()
        self._col(p.own, 1, p.dev_b).start()
        if self.halves:
            self._d(0).start()
        if self.wide:
            self.line_a.hop(2)

    def after_a(self):
        p = self.p
        if self.wide:
            self.line_a.hop(3)
        else:
            self._a().wait_recv()
        self._col(p.col_a, 2, p.dev_b).start()
        if self.halves:
            self._d(1).start()

    def after_b(self):
        p = self.p
        self._col(p.own, 1, p.dev_b).wait_recv()
        if self.halves:
            self._d(2).start()
        self._col(p.own, 2, p.dev_b).wait_recv()
        if self.halves:
            self._d(3).start()

    def done(self):
        if self.halves:
            for n in range(4):
                self._d(n).wait_recv()

    def drain(self):
        p = self.p
        self.line.drain()
        if self.wide:
            self.line_a.drain()
            self._source(lambda: self._a().wait_send())
        else:
            self._a().wait_send()
        self._col(p.own, 1, p.dev_b).wait_send()
        self._col(p.own, 2, p.dev_b).wait_send()
        if self.halves:
            for n in range(4):
                self._d(n).wait_send()


def add_into(dst, src):
    dst[...] = dst[...] + src[...]


class LineScatter:
    def __init__(self, scatter, col, base, down, up, direct=False):
        self.s, self.col, self.base, self.down, self.up, self.direct = scatter, col, base, down, up, direct

    def _straight(self, k):
        s = self.s
        zz, dev = s.p.z_dev(k)
        return s._copy(self._piece(zz), self.down.at[k], self.base + k, dev)

    def _piece(self, zs):
        s = self.s
        return s.part(zs, *self.col, s.p.r)

    def _send(self, lo, hi, step):
        s = self.s
        buf, n = (self.up, 0) if step > 0 else (self.down, 1)
        return s._copy(self._piece(slice(lo, hi)), buf.at[slice(lo, hi)], self.base + n, (s.p.r, s.p.i + 4 * step))

    def _moves(self):
        j = self.s.plane
        if j is None:
            return [(0, 3, 0, 3, -1), (0, 0, 1, 4, 1), (1, 2, 0, 2, -1), (1, 1, 2, 4, 1), (2, 1, 0, 1, -1), (2, 2, 3, 4, 1)]
        return [(3 - z, z, 0, 4, -1) for z in range(3, j, -1)] + [(z, z, 0, 4, 1) for z in range(j)]

    def _take(self, lo, hi, step):
        buf = self.up if step > 0 else self.down
        self._send(lo, hi, step).wait_recv()
        add_into(self._piece(slice(lo, hi)), buf.at[slice(lo, hi)])

    def step(self, k):
        if self.direct:
            if k == 0:
                for n in (3, 2, 1):
                    self._straight(n).start()
            if k == 3:
                for n in (1, 2, 3):
                    self._straight(n).wait_recv()
                    add_into(self._piece(self.s.p.z), self.down.at[n])
            return
        moves = self._moves()
        for rnd, z, lo, hi, way in moves:
            if rnd == k - 1:
                pl.when(self.s.p.z == z + way)(functools.partial(self._take, lo, hi, way))
        for rnd, z, lo, hi, way in moves:
            if rnd == k:
                pl.when(self.s.p.z == z)(lambda lo=lo, hi=hi, way=way: self._send(lo, hi, way).start())

    def drain(self):
        if self.direct:
            for n in (1, 2, 3):
                self._straight(n).wait_send()
            return
        for _, z, lo, hi, way in self._moves():
            pl.when(self.s.p.z == z)(lambda lo=lo, hi=hi, way=way: self._send(lo, hi, way).wait_send())


class Scatter:
    def __init__(self, place, part, bufs, out, sems, plane=None, wide=False, direct=False):
        self.p, self.part, self.out, self.plane, self.wide = place, part, out, plane, wide
        self.dbuf, self.bbuf, self.abuf, down, up, down_a, up_a = bufs
        self.send, self.recv = sems
        self.line = LineScatter(self, place.own, 8, down, up, direct)
        self.line_a = LineScatter(self, place.col_a, 10, down_a, up_a)

    def _copy(self, src, dst, n, dev):
        return remote(src, dst, self.send.at[n], self.recv.at[n], dev)

    def _d(self, zz):
        p = self.p
        return self._copy(self.part(zz, ALL, ALL, 1 - p.r), self.dbuf.at[zz], zz, p.dev_d)

    def _b(self, n):
        p = self.p
        col = (p.col_b, p.col_ab)[n]
        return self._copy(self.part(ALL, *col, p.r), self.bbuf.at[n], 4 + n, p.dev_b)

    def _a(self):
        p = self.p
        if self.wide and self.plane is None:
            return self._copy(self.part(p.z, *p.col_a, p.r), self.abuf.at[0], 6, p.dev_a)
        return self._copy(self.part(ALL, *p.col_a, p.r), self.abuf, 6, p.dev_a)

    def _here(self, act):
        if self.plane is None:
            act()
        else:
            pl.when(self.p.z == self.plane)(act)

    def _f(self):
        p = self.p
        return self._copy(self.out(p.r), self.out(p.r), 7, p.dev_d)

    def start(self):
        for zz in range(4):
            self._d(zz).start()

    def after_d(self):
        p = self.p
        for zz in range(4):
            self._d(zz).wait_recv()
        for n, col in enumerate((p.col_b, p.col_ab, p.col_a, p.own)):
            add_into(self.part(ALL, *col, p.r), self.dbuf.at[(ALL,) + col])
            if n < 2:
                self._b(n).start()

    def after_b(self):
        p = self.p
        self._b(1).wait_recv()
        add_into(self.part(ALL, *p.col_a, p.r), self.bbuf.at[1])
        if self.wide:
            self.line_a.step(0)
        else:
            self._a().start()
        self._b(0).wait_recv()
        add_into(self.part(ALL, *p.own, p.r), self.bbuf.at[0])
        if self.wide:
            self.line.step(0)

    def after_a(self):
        p = self.p
        if self.wide:
            self.line_a.step(1)
            self.line.step(1)
        else:
            self._a().wait_recv()
            add_into(self.part(ALL, *p.own, p.r), self.abuf)
            self.line.step(0)

    def line_one(self):
        if self.wide:
            self.line_a.step(2)
            self.line.step(2)
        else:
            self.line.step(1)

    def line_two(self):
        if self.wide:
            self.line_a.step(3)
            self._here(lambda: self._a().start())
        else:
            self.line.step(2)

    def last(self):
        self.line.step(3)
        self._here(self._finish)

    def _finish(self):
        p = self.p
        total = self.part(p.z if self.plane is None else ALL, *p.own, p.r)[...].astype(F32)
        if self.wide:
            self._a().wait_recv()
            total = total + self.abuf[0 if self.plane is None else ALL].astype(F32)
        self.out(p.r)[...] = total
        self._f().start()

    def done(self):
        self._here(lambda: self._f().wait_recv())

    def drain(self):
        for zz in range(4):
            self._d(zz).wait_send()
        for n in range(2):
            self._b(n).wait_send()
        self.line.drain()
        if self.wide:
            self.line_a.drain()
            self._here(lambda: self._a().wait_send())
        else:
            self._a().wait_send()
        self._here(lambda: self._f().wait_send())


class ScatterSmall:
    def __init__(self, place, ref, bufs, out, sems):
        self.p, self.ref, self.out = place, ref, out
        self.bbuf, self.abuf, self.zbuf, self.fbuf = bufs
        self.send, self.recv = sems

    def _copy(self, src, dst, n, dev):
        return remote(src, dst, self.send.at[n], self.recv.at[n], dev)

    def _b(self, n):
        p = self.p
        col = (p.col_b, p.col_ab)[n]
        return self._copy(self.ref.at[(ALL,) + col], self.bbuf.at[n], n, p.dev_b)

    def _a(self):
        p = self.p
        return self._copy(self.ref.at[(ALL,) + p.col_a], self.abuf, 2, p.dev_a)

    def _z(self, k):
        p = self.p
        zz, dev = p.z_dev(k)
        return self._copy(self.ref.at[(zz,) + p.own], self.zbuf.at[k - 1], 2 + k, dev)

    def _f(self):
        p = self.p
        return self._copy(self.out, self.fbuf, 6, p.dev_d)

    def start(self):
        self._b(0).start()
        self._b(1).start()

    def after_b(self):
        p = self.p
        self._b(0).wait_recv()
        self._b(1).wait_recv()
        self.ref[(ALL,) + p.col_a] += self.bbuf[1]
        self.ref[(ALL,) + p.own] += self.bbuf[0]
        self._a().start()

    def after_a(self):
        p = self.p
        self._a().wait_recv()
        self.ref[(ALL,) + p.own] += self.abuf[...]
        for k in (1, 2, 3):
            self._z(k).start()

    def after_z(self):
        p = self.p
        for k in (1, 2, 3):
            self._z(k).wait_recv()
        self.out[...] = self.ref[(p.z,) + p.own] + self.zbuf[0] + self.zbuf[1] + self.zbuf[2]
        self._f().start()

    def done(self):
        self._f().wait_recv()
        self._f().wait_send()
        self.out[...] = self.out[...] + self.fbuf[...]

    def drain(self):
        self._b(0).wait_send()
        self._b(1).wait_send()
        self._a().wait_send()
        for k in (1, 2, 3):
            self._z(k).wait_send()


ROWS_ALL = 768
IMAGE = 384
KEYS = 288
ALWAYS = 192
SLOTS = 4
WIDE_GATHER = (7, 9)
WIDE_SCATTER = (1, 3, 5)
DIRECT_GATHER = (0,)
DIRECT_SCATTER = (9, 10, 11)
NT = (((1,), (1,)), ((), ()))
TN = (((0,), (0,)), ((), ()))


def dots(a, b, dims=None):
    if dims is None:
        return jnp.dot(a, b, preferred_element_type=F32)
    return lax.dot_general(a, b, dims, preferred_element_type=F32)


def loop(count, body):
    def step(t, carry):
        body(t)
        return carry

    lax.fori_loop(0, count, step, 0)


def tiles(count, size, body):
    loop(count, lambda t: body(t, pl.ds(pl.multiple_of(t * size, size), size)))


def moments(v):
    centre = v - jnp.mean(v, axis=-1, keepdims=True)
    inverse = lax.rsqrt(jnp.mean(centre * centre, axis=-1, keepdims=True) + epsilon)
    return centre * inverse, inverse


def half(core):
    return pl.ds(pl.multiple_of(core * HALF, 128), HALF)


(OPEN, VECTORS, NORMED, GROUP, MIXED, PROJECT, SCALED, FEED, TWO, MIXED_BACK, PROJECT_BACK, BACK, GROWN, ONE, CLOSE) = range(15)
STEPS = (
    (Gather.start, Gather.hop_one, Gather.hop_two, Gather.after_z, Gather.after_a, Gather.after_b, Gather.done),
    (Scatter.start, Scatter.after_d, Scatter.after_b, Scatter.after_a, Scatter.line_one, Scatter.line_two, Scatter.last),
    (ScatterSmall.after_b, ScatterSmall.after_a, ScatterSmall.after_z),
)


PLAN = (
    ((OPEN,), ((0, 0, 0), (0, 1, 0), (0, 2, 0), (0, 3, 0), (0, 4, 0), (3, 0, 3), (0, 0, 1), (0, 0, 2), (0, 0, 3),
        (0, 1, 1), (0, 2, 1), (0, 5, 0), (3, 0, 4), (0, 3, 1), (0, 4, 1), (0, 1, 2), (0, 0, 4), (0, 2, 2), (3, 0, 5),
        (0, 1, 3), (0, 3, 2), (0, 5, 1), (0, 6, 0),)),
    ((VECTORS,), ((0, 0, 5), (0, 2, 3), (0, 7, 0),)),
    ((NORMED,), ((0, 4, 2),)),
    ((GROUP, 0, -1), ((0, 0, 6),)),
    ((GROUP, 0, -2), ((0, 3, 3),)),
    ((GROUP, 0, 0), ((0, 1, 4), (0, 5, 2),)),
    ((GROUP, 1, -1), ((0, 2, 4), (0, 6, 1), (0, 7, 1), (0, 3, 4), (0, 4, 3), (0, 8, 0), (0, 9, 0), (0, 5, 3),
        (0, 10, 0), (0, 1, 5), (0, 6, 2), (0, 6, 3), (0, 2, 5), (0, 1, 6),)),
    ((GROUP, 1, -2), ((0, 7, 2), (0, 3, 5), (0, 11, 0),)),
    ((GROUP, 1, 0), ((0, 4, 4), (0, 10, 1),)),
    ((GROUP, 1, 1), ((0, 8, 1),)),
    ((GROUP, 2, -1), ((0, 2, 6),)),
    ((GROUP, 2, -2), ((0, 9, 1),)),
    ((GROUP, 2, 0), ((0, 5, 4), (0, 7, 3),)),
    ((GROUP, 2, 0), ((0, 11, 1),)),
    ((MIXED,), ((0, 3, 6),)),
    ((PROJECT, 0), ((0, 6, 4), (0, 10, 2),)),
    ((PROJECT, 1), ((0, 8, 2), (0, 8, 3),)),
    ((SCALED,), ((0, 4, 5), (0, 9, 2),)),
    ((FEED, 0, 0), ((0, 7, 4), (0, 5, 5), (0, 11, 2), (0, 4, 6),)),
    ((FEED, 0, 2), ((0, 5, 6),)),
    ((FEED, 0, 3), ((0, 6, 5), (0, 10, 3),)),
    ((FEED, 0, 4), ((0, 8, 4), (0, 9, 3), (0, 11, 3),)),
    ((FEED, 0, 5), ((1, 0, 0),)),
    ((FEED, 0, 6), ((0, 7, 5),)),
    ((FEED, 0, 7), ((1, 1, 0),)),
    ((FEED, 1, 0), ((0, 6, 6),)),
    ((FEED, 1, 1), ((0, 9, 4), (0, 10, 4),)),
    ((FEED, 1, 2), ((0, 7, 6),)),
    ((FEED, 1, 3), ((0, 8, 5), (1, 1, 1),)),
    ((FEED, 1, 5), ((0, 11, 4), (1, 0, 1), (1, 2, 0),)),
    ((FEED, 1, 7), ((1, 3, 0), (1, 2, 1),)),
    ((FEED, 2, 0), ((0, 8, 6),)),
    ((FEED, 2, 1), ((0, 9, 5),)),
    ((FEED, 2, 2), ((0, 10, 5), (1, 3, 1), (0, 9, 6),)),
    ((FEED, 2, 3), ((1, 1, 2),)),
    ((FEED, 2, 4), ((0, 11, 5),)),
    ((FEED, 2, 5), ((1, 4, 0),)),
    ((FEED, 2, 7), ((1, 5, 0), (1, 0, 2), (1, 4, 1),)),
    ((FEED, 3, 0), ((0, 10, 6),)),
    ((FEED, 3, 2), ((0, 11, 6),)),
    ((FEED, 3, 3), ((1, 1, 3), (1, 2, 2), (1, 5, 1),)),
    ((FEED, 3, 5), ((1, 6, 0), (1, 3, 2),)),
    ((FEED, 3, 6), ((1, 0, 3),)),
    ((FEED, 3, 7), ((1, 7, 0), (1, 6, 1),)),
    ((TWO, 1), ((1, 1, 4), (1, 4, 2),)),
    ((TWO, 3), ((1, 2, 3), (1, 7, 1),)),
    ((PROJECT_BACK,), ((1, 8, 0), (1, 3, 3), (1, 5, 2), (1, 1, 5),)),
    ((BACK, 0, 1), ((1, 0, 4), (1, 6, 2), (1, 8, 1),)),
    ((BACK, 0, 1), ((1, 4, 3),)),
    ((BACK, 0, -1), ((1, 9, 0),)),
    ((BACK, 1, 0), ((1, 2, 4),)),
    ((BACK, 1, 0), ((1, 3, 4), (1, 7, 2),)),
    ((BACK, 1, 1), ((1, 1, 6), (1, 9, 1),)),
    ((BACK, 1, 1), ((1, 6, 3), (1, 0, 5),)),
    ((BACK, 1, -1), ((1, 10, 0), (1, 5, 3),)),
    ((BACK, 2, 0), ((1, 3, 5), (1, 2, 5), (1, 2, 6), (1, 8, 2),)),
    ((BACK, 2, 1), ((1, 4, 4), (1, 7, 3), (1, 10, 1),)),
    ((BACK, 2, -1), ((1, 11, 0), (1, 0, 6), (1, 6, 4),)),
    ((GROWN, 0), ((1, 3, 6), (1, 5, 4), (1, 9, 2),)),
    ((GROWN, 1), ((1, 8, 3), (1, 11, 1),)),
    ((GROWN, 2), ((1, 4, 5), (1, 4, 6), (1, 7, 4),)),
    ((ONE, 2), ((1, 10, 2),)),
    ((ONE, 4), ((1, 5, 5),)),
    ((ONE, 5), ((1, 9, 3), (1, 6, 5), (1, 9, 4), (1, 9, 5),)),
    ((CLOSE,), ((1, 8, 4), (1, 7, 5), (1, 11, 2), (1, 10, 3), (1, 10, 4), (1, 10, 5), (1, 5, 6), (2, 0, 0),
        (1, 9, 6), (1, 11, 3), (1, 11, 4), (1, 8, 5), (1, 11, 5), (1, 6, 6), (2, 0, 1), (1, 7, 6), (1, 10, 6),
        (2, 0, 2), (1, 11, 6), (1, 8, 6),)),
)


class Agenda:
    def __init__(self):
        self.calls = {}

    def at(self, point, *calls):
        self.calls.setdefault(point, []).extend(calls)

    def run(self, point):
        for call in self.calls.pop(point, []):
            call()

    def here(self, *place):
        for point in list(self.calls):
            if len(point) != len(place):
                continue
            test, fits = None, True
            for value, index in zip(point, place):
                if isinstance(index, int):
                    fits = fits and value == index
                elif value < 0:
                    fits = False
                else:
                    same = index == value
                    test = same if test is None else jnp.logical_and(test, same)
            if fits and test is None:
                self.run(point)
            elif fits:
                pl.when(test)(functools.partial(self.run, point))


def layer_kernel(
    tokens, cot, grids, keep_a, keep_m, g1, s1, bqv, bp, g2, s2, b1, b2, wq, wp, w1, w2,
    out_h, gt_h, oq_h, op_h, o1_h, o2_h, og1, os1, obqv, obp, og2, os2, ob1, ob2,
    x, ct, dz, h1, qkv, probs, mixed, y1, h2, dact, act, acc, dh,
    gu, gw2, stage, pack, packs, vec, flat, vqkv, vb1, dvec, dbqv, db1, outq, op, o1, o2, smalls, opack,
    dbuf, bbuf, abuf, lbuf, wbuf, sb, sa, sz, sf,
    gsend, grecv, glocal, tsend, trecv, tlocal, ssend, srecv, usend, urecv, local,
):
    place = Place()
    load_x = pltpu.make_async_copy(tokens, x, local.at[0])
    load_c = pltpu.make_async_copy(cot, ct, local.at[1])
    groups_of_four = [(g, k, slice(256 * k, 256 * k + 256), slice(768 * k + 256 * g, 768 * k + 256 * g + 256)) for g in range(3) for k in range(3)]
    regroup = [pltpu.make_async_copy(wq.at[:, there], stage.at[g, :, here], local.at[4 + 3 * g + k]) for g, k, here, there in groups_of_four]
    for copy in regroup:
        copy.start()
    load_x.start()
    load_c.start()
    pack[...] = jnp.zeros_like(pack)
    for row, ref in enumerate((g1, s1, bp, g2, s2, b2)):
        pack[row : row + 1, 0:48] = ref[...].astype(F32).reshape(1, 48)
    pack[6:7, 0:96] = bqv[...].astype(F32).reshape(1, 96)
    both = b1[...].astype(F32).reshape(1, 192)
    pack[7:8, 0:96] = both[:, :96]
    pack[8:9, 0:96] = both[:, 96:]
    greet(place)

    tiny = Gather(place, lambda zs, y, xx, core: packs.at[zs, y, xx], lambda core: pack, (tsend, trecv), tlocal, halves=False, direct=True)

    def block(u):
        return lambda zs, y, xx, core: gu.at[u, zs, y, xx, :, half(core)]

    def plane_part(j):
        return lambda zs, y, xx, core: gw2.at[j, y, xx, zs, :, half(core)]

    def fc1_cols(j, core):
        return pl.ds(pl.multiple_of(WIDE * j + core * HALF, 128), HALF)

    pieces = [(block(g), lambda core, g=g: stage.at[g, :, half(core)], None) for g in range(3)]
    pieces.append((block(3), lambda core: wp.at[:, half(core)], None))
    for j in range(4):
        pieces.append((plane_part(j), lambda core: w2.at[:, :, half(core)], j))
        pieces.append((block(4 + j), lambda core, j=j: w1.at[:, fc1_cols(j, core)], None))
    units = [
        Gather(place, part, own, (gsend.at[n], grecv.at[n]), glocal.at[n], wide=n in WIDE_GATHER, plane=plane, direct=n in DIRECT_GATHER)
        for n, (part, own, plane) in enumerate(pieces)
    ]

    def gq_part(g):
        return lambda zs, y, xx, core: dact.at[g, zs, y, xx, :, half(core)]

    plans = []
    for j in range(4):
        plans.append((plane_part(j), lambda core: o2.at[:, :, half(core)], j))
        plans.append((block(4 + j), lambda core, j=j: o1.at[:, fc1_cols(j, core)], None))
    plans.append((block(3), lambda core: op.at[:, half(core)], None))
    for g in range(3):
        plans.append((gq_part(g), lambda core, g=g: outq.at[g, :, half(core)], None))
    sends = []
    for n, (part, out, plane) in enumerate(plans):
        wide = n in WIDE_SCATTER
        extra = [wbuf.at[WIDE_SCATTER.index(n), k] for k in range(2)] if wide else [None, None]
        bufs = [dbuf.at[n % SLOTS], bbuf.at[n], abuf.at[n], lbuf.at[n, 0], lbuf.at[n, 1]] + extra
        sends.append(Scatter(place, part, bufs, out, (ssend.at[n], srecv.at[n]), plane, wide, n in DIRECT_SCATTER))
    small = ScatterSmall(place, smalls, (sb, sa, sz, sf), opack, (usend, urecv))

    agenda = Agenda()
    groups = (units, sends, [small], [tiny])
    for point, steps in PLAN:
        for kind, n, step in steps:
            step = STEPS[min(kind, 2)][step] if kind < 3 else STEPS[0][step]
            agenda.at(point, functools.partial(step, groups[kind][n]))

    tiny.start()
    for copy in regroup:
        copy.wait()
    agenda.here(OPEN)
    for s in range(16):
        at = (s // 4, (s // 2) % 2, s % 2)
        vec[:, 48 * s : 48 * s + 48] = packs[at + (slice(0, 8), slice(0, 48))]
        c = 192 * (s % 4)
        vb1[s // 4, :, c : c + 96] = packs[at + (slice(7, 8), slice(0, 96))]
        vb1[s // 4, :, c + 96 : c + 192] = packs[at + (slice(8, 9), slice(0, 96))]
        c = 96 * s + 768 * (s // 8)
        flat[:, c : c + 96] = packs[at + (slice(6, 7), slice(0, 96))]
    flat[:, 768:1536] = jnp.zeros((1, 768), F32)
    for g in range(3):
        for k in range(3):
            vqkv[g, :, 256 * k : 256 * k + 256] = flat[:, 768 * k + 256 * g : 768 * k + 256 * g + 256]
    dvec[...] = jnp.zeros_like(dvec)
    dbqv[...] = jnp.zeros_like(dbqv)

    agenda.here(VECTORS)
    load_x.wait()

    def norm_one(t, rows):
        n, _ = moments(x[rows, :].astype(F32))
        h1[rows, :] = (n * vec[0:1, :] + vec[1:2, :]).astype(BF16)

    tiles(6, 128, norm_one)
    agenda.here(NORMED)

    lane = lax.broadcasted_iota(jnp.int32, (1, 128), 1) // HEAD

    def pair(g, t):
        base = pl.multiple_of(t // 2 * IMAGE, IMAGE)
        at = [pl.ds(pl.multiple_of(256 * k + 128 * (t % 2), 128), 128) for k in range(3)]
        q = qkv[g, pl.ds(base, IMAGE), at[0]] * BF16(0.125)
        k = qkv[g, pl.ds(base, KEYS), at[1]]
        v = qkv[g, pl.ds(base, KEYS), at[2]]
        col = pl.ds(pl.multiple_of(256 * g + 128 * (t % 2), 128), 128)
        return base, at, q, k, v, col

    def attend(g, i):
        length = grids[i, 0] * grids[i, 1] + 2
        key = lax.broadcasted_iota(jnp.int32, (KEYS - ALWAYS, IMAGE), 0) + ALWAYS
        found = []
        for t in (2 * i, 2 * i + 1):
            base, at, q, k, v, col = pair(g, t)
            total, kept_probs = None, []
            for h in range(2):
                qh = jnp.where(lane == h, q, BF16(0))
                vh = jnp.where(lane == h, v, BF16(0))
                s = dots(k, qh, NT)
                s = jnp.concatenate([s[:ALWAYS], jnp.where(key < length, s[ALWAYS:], -1000000000.0)], axis=0)
                e = jnp.exp(s - jnp.max(s, axis=0, keepdims=True))
                p = (e * (1.0 / jnp.sum(e, axis=0, keepdims=True))).astype(BF16)
                kept_probs.append(p)
                o = dots(p, vh, TN)
                total = o if total is None else total + o
            found.append((t, base, col, total, kept_probs))
        for t, base, col, total, kept_probs in found:
            for h in range(2):
                probs[8 * g + 2 * t + h] = kept_probs[h]
            mixed[pl.ds(base, IMAGE), col] = total.astype(BF16)
        agenda.here(GROUP, g, i)

    def forward_group(g):
        agenda.here(GROUP, g, -1)
        qkv[g] = (dots(h1[...], gu[g].reshape(768, 768)) + vqkv[g]).astype(BF16)
        agenda.here(GROUP, g, -2)
        loop(2, functools.partial(attend, g))

    loop(3, forward_group)

    def kept(ref, b):
        return ref[b].astype(F32) * (1.0 / 0.9)

    agenda.here(MIXED)

    def project(b):
        rows = pl.ds(pl.multiple_of(b * IMAGE, IMAGE), IMAGE)
        y = x[rows, :].astype(F32) + kept(keep_a, b) * (dots(mixed[rows, :], gu[3].reshape(768, 768)) + vec[2:3, :])
        y1[rows, :] = y
        n, _ = moments(y)
        h2[rows, :] = (n * vec[3:4, :] + vec[4:5, :]).astype(BF16)
        agenda.here(PROJECT, b)

    loop(2, project)
    load_c.wait()

    def scale_dz(t, rows):
        d = (ct[rows, :].astype(F32) * kept(keep_m, t // 3)).astype(BF16)
        dz[rows, :] = d
        dvec[5:6, :] += jnp.sum(d.astype(F32), axis=0, keepdims=True)

    tiles(6, 128, scale_dz)
    acc[...] = jnp.zeros_like(acc)
    dh[...] = jnp.zeros_like(dh)
    agenda.here(SCALED)
    units[3].drain()

    def feed(j):
        agenda.here(FEED, j, 0)
        dact[j] = dots(dz[...], gw2[j].reshape(768, 768), NT).astype(BF16).reshape(4, 2, 2, ROWS, 768)
        agenda.here(FEED, j, 1)
        agenda.here(FEED, j, 2)
        pre = dots(h2[...], gu[j + 4].reshape(768, 768)) + vb1[j]
        u = 0.5 * (1.0 + lax.erf(pre * root_half))
        act[...] = (pre * u).astype(BF16)
        d = dact[j].reshape(768, 768).astype(F32) * (u + pre * jnp.exp(-0.5 * pre * pre) * 0.3989422804014327)
        db1[j] = jnp.sum(d, axis=0, keepdims=True)
        dact[j] = d.astype(BF16).reshape(4, 2, 2, ROWS, 768)
        agenda.here(FEED, j, 3)
        acc[...] += dots(act[...], gw2[j].reshape(768, 768))
        agenda.here(FEED, j, 4)
        for n in range(4):
            pl.when(j == n)(units[4 + 2 * n].drain)
        gw2[j] = dots(act[...], dz[...], TN).astype(BF16).reshape(2, 2, 4, ROWS, 768)
        agenda.here(FEED, j, 5)
        dh[...] += dots(dact[j].reshape(768, 768), gu[j + 4].reshape(768, 768), NT)
        agenda.here(FEED, j, 6)
        for n in range(4):
            pl.when(j == n)(units[5 + 2 * n].drain)
        gu[j + 4] = dots(h2[...], dact[j].reshape(768, 768), TN).astype(BF16).reshape(4, 2, 2, ROWS, 768)
        agenda.here(FEED, j, 7)

    loop(4, feed)

    def norm_two_back(t, rows):
        y = y1[rows, :]
        n, inverse = moments(y)
        d = dh[rows, :]
        e = d * vec[3:4, :]
        back = inverse * (e - jnp.mean(e, axis=-1, keepdims=True) - n * jnp.mean(e * n, axis=-1, keepdims=True))
        back = ct[rows, :].astype(F32) + back
        dh[rows, :] = back
        da = (back * kept(keep_a, t // 3)).astype(BF16)
        h2[rows, :] = da
        dvec[3:4, :] += jnp.sum(d * n, axis=0, keepdims=True)
        dvec[4:5, :] += jnp.sum(d, axis=0, keepdims=True)
        dvec[2:3, :] += jnp.sum(da.astype(F32), axis=0, keepdims=True)
        agenda.here(TWO, t)

    tiles(6, 128, norm_two_back)
    dz[...] = dots(h2[...], gu[3].reshape(768, 768), NT).astype(BF16)
    agenda.here(MIXED_BACK)
    gu[3] = dots(mixed[...], h2[...], TN).astype(BF16).reshape(4, 2, 2, ROWS, 768)
    agenda.here(PROJECT_BACK)

    def attend_back(g, i):
        found = []
        for t in (2 * i, 2 * i + 1):
            base, at, q, k, v, col = pair(g, t)
            do = dz[pl.ds(base, IMAGE), col]
            dq = dk = dv = None
            for h in range(2):
                qh = jnp.where(lane == h, q, BF16(0))
                kh = jnp.where(lane == h, k, BF16(0))
                doh = jnp.where(lane == h, do, BF16(0))
                p = probs[8 * g + 2 * t + h]
                pf = p.astype(F32)
                dp = dots(v, doh, NT)
                ds = (pf * (dp - jnp.sum(pf * dp, axis=0, keepdims=True))).astype(BF16)
                new = (dots(ds, kh, TN), dots(ds, qh), dots(p, doh))
                dq, dk, dv = new if dq is None else (dq + new[0], dk + new[1], dv + new[2])
            found.append((base, at, col, dq * 0.125, dk, dv))
        none = jnp.zeros((IMAGE - KEYS, 128), BF16)
        for base, at, col, dq, dk, dv in found:
            qkv[g, pl.ds(base, IMAGE), at[0]] = dq.astype(BF16)
            qkv[g, pl.ds(base, KEYS), at[1]] = dk.astype(BF16)
            qkv[g, pl.ds(base, KEYS), at[2]] = dv.astype(BF16)
            qkv[g, pl.ds(base + KEYS, IMAGE - KEYS), at[1]] = none
            qkv[g, pl.ds(base + KEYS, IMAGE - KEYS), at[2]] = none
            dbqv[0, :, col] += jnp.sum(dq, axis=0, keepdims=True)
            dbqv[1, :, col] += jnp.sum(dv, axis=0, keepdims=True)
        agenda.here(BACK, g, i)

    def back_group(g):
        loop(2, functools.partial(attend_back, g))
        dact[g] = dots(h1[...], qkv[g], TN).astype(BF16).reshape(4, 2, 2, ROWS, 768)
        agenda.here(BACK, g, -1)

    loop(3, back_group)

    def put_out(t, rows):
        act[rows, :] = (y1[rows, :] + kept(keep_m, t // 3) * (acc[rows, :] + vec[5:6, :])).astype(BF16)
        acc[rows, :] = jnp.zeros((128, 768), F32)

    tiles(6, 128, put_out)
    save_out = pltpu.make_async_copy(act, out_h, local.at[2])
    save_out.start()

    def grow(g):
        acc[...] += dots(qkv[g], gu[g].reshape(768, 768), NT)
        agenda.here(GROWN, g)

    loop(3, grow)

    def norm_one_back(t, rows):
        n, inverse = moments(x[rows, :].astype(F32))
        d = acc[rows, :]
        e = d * vec[0:1, :]
        back = inverse * (e - jnp.mean(e, axis=-1, keepdims=True) - n * jnp.mean(e * n, axis=-1, keepdims=True))
        dh[rows, :] += back
        dvec[0:1, :] += jnp.sum(d * n, axis=0, keepdims=True)
        dvec[1:2, :] += jnp.sum(d, axis=0, keepdims=True)
        agenda.here(ONE, t)

    tiles(6, 128, norm_one_back)
    save_gt = pltpu.make_async_copy(dh, gt_h, local.at[3])
    save_gt.start()
    smalls[...] = jnp.zeros_like(smalls)
    for s in range(16):
        at = (s // 4, (s // 2) % 2, s % 2)
        smalls[at + (slice(0, 8), slice(0, 48))] = dvec[:, 48 * s : 48 * s + 48]
        c = 96 * (s % 8)
        smalls[at + (slice(6, 7), slice(0, 96))] = dbqv[s // 8, :, c : c + 96]
        c = 192 * (s % 4)
        smalls[at + (slice(7, 8), slice(0, 96))] = db1[s // 4, :, c : c + 96]
        smalls[at + (slice(8, 9), slice(0, 96))] = db1[s // 4, :, c + 96 : c + 192]
    small.start()
    agenda.here(CLOSE)
    saves = []
    for n, unit in enumerate(sends):
        unit.done()
        if n < 8 and n % 2 == 0:
            continue
        if n == 7:
            pairs = [(o1, o1_h), (o2, o2_h)]
        elif n == 8:
            pairs = [(op, op_h)]
        elif n > 8:
            pairs = [(outq.at[g, :, here], oq_h.at[:, there]) for g, k, here, there in groups_of_four if g == n - 9]
        else:
            pairs = []
        for src, dst in pairs:
            saves.append(pltpu.make_async_copy(src, dst, local.at[13 + len(saves)]))
            saves[-1].start()
    small.done()
    assert not agenda.calls
    for row, ref in enumerate((og1, os1, obp, og2, os2, ob2)):
        ref[...] = opack[row : row + 1, 0:48].reshape(48)
    obqv[...] = opack[6:7, 0:96].reshape(96)
    ob1[...] = jnp.concatenate([opack[7:8, 0:96], opack[8:9, 0:96]], axis=1).reshape(192)
    for unit in [units[0], units[1], units[2], tiny, small] + sends:
        unit.drain()
    for copy in [save_out, save_gt] + saves:
        copy.wait()


def handover_kernel(*refs):
    count = len(refs) // 4
    ins, outs, held, sems = (refs[n * count : (n + 1) * count] for n in range(4))
    takes = [pltpu.make_async_copy(ins[n], held[n], sems[n].at[0]) for n in range(count)]
    gives = [pltpu.make_async_copy(held[n], outs[n], sems[n].at[1]) for n in range(count)]
    for copy in takes:
        copy.start()
    for take, give in zip(takes, gives):
        take.wait()
        give.start()
    for copy in gives:
        copy.wait()


def handover(arrays):
    specs = [pl.BlockSpec(memory_space=pltpu.HBM)] * len(arrays)
    return pl.pallas_call(
        handover_kernel,
        out_shape=[jax.ShapeDtypeStruct(a.shape, a.dtype) for a in arrays],
        in_specs=specs,
        out_specs=specs,
        scratch_shapes=[pltpu.VMEM(a.shape, a.dtype) for a in arrays] + [pltpu.SemaphoreType.DMA((2,))] * len(arrays),
        name="handover",
    )(*arrays)


def by_block(tokens, grids, keep_attn, keep_mlp, cotangent, *params):
    g1, s1, wq, bqv, wp, bp, g2, s2, w1, b1, w2, b2 = params
    rows = lambda v: v.reshape(ROWS_ALL, 768)
    vm, sm, hbm = (pl.BlockSpec(memory_space=m) for m in (pltpu.VMEM, pltpu.SMEM, pltpu.HBM))
    S = jax.ShapeDtypeStruct
    v = lambda *shape: pltpu.VMEM(shape, BF16)
    f = lambda *shape: pltpu.VMEM(shape, F32)
    dma = lambda *shape: pltpu.SemaphoreType.DMA(shape)
    outs = pl.pallas_call(
        layer_kernel,
        out_shape=[S((ROWS_ALL, 768), BF16), S((ROWS_ALL, 768), F32)]
        + [S(w.shape, F32) for w in (wq, wp, w1)]
        + [S((4, ROWS, 768), F32)]
        + [S(w.shape, F32) for w in (g1, s1, bqv, bp, g2, s2, b1, b2)],
        in_specs=[hbm] * 2 + [sm] * 3 + [vm] * 8 + [hbm] * 4,
        out_specs=[hbm] * 6 + [vm] * 8,
        scratch_shapes=[
            v(768, 768), v(768, 768), v(768, 768), v(768, 768), v(3, 768, 768), v(24, KEYS, IMAGE), v(768, 768), f(768, 768),
            v(768, 768), v(4, 4, 2, 2, ROWS, 768), v(768, 768), f(768, 768), f(768, 768),
            v(8, 4, 2, 2, ROWS, 768), v(4, 2, 2, 4, ROWS, 768), v(3, ROWS, 768), f(16, 128), f(4, 2, 2, 16, 128),
            f(8, 768), f(1, 2304), f(3, 1, 768), f(4, 1, 768), f(8, 768), f(2, 1, 768), f(4, 1, 768), f(3, ROWS, 768),
            f(ROWS, 768), f(ROWS, 3072), f(4, ROWS, 768), f(4, 2, 2, 16, 128), f(16, 128),
            v(SLOTS, 4, 2, 2, ROWS, HALF), v(12, 2, 4, ROWS, HALF), v(12, 4, ROWS, HALF),
            v(12, 2, 4, ROWS, HALF), v(len(WIDE_SCATTER), 2, 4, ROWS, HALF),
            f(2, 4, 16, 128), f(4, 16, 128), f(3, 16, 128), f(16, 128),
            dma(12, 22), dma(12, 22), dma(12), dma(22), dma(22), dma(), dma(12, 12), dma(12, 12), dma(8), dma(8), dma(26),
        ],
        compiler_params=pltpu.CompilerParams(collective_id=0, has_side_effects=True, vmem_limit_bytes=62 << 20),
        cost_estimate=pl.CostEstimate(flops=36 * 10**9, bytes_accessed=10**7, transcendentals=10**7),
        name="layer",
    )(
        rows(tokens), rows(cotangent), grids, keep_attn, keep_mlp, g1, s1, bqv, bp, g2, s2, b1, b2, wq, wp, w1,
        w2.reshape(4, ROWS, 768),
    )
    out, gt, oq, op, o1, o2, og1, os1, obqv, obp, og2, os2, ob1, ob2 = handover(outs)
    return (
        out.reshape(tokens.shape), gt.reshape(tokens.shape), og1, os1, oq, obqv, op, obp, og2, os2, o1, ob1,
        o2.reshape(w2.shape), ob2,
    )


def layer_norm(stream, gain, shift):
    center = jnp.mean(stream, axis=-1, keepdims=True)
    shifted = stream - center
    inverse = lax.rsqrt(jnp.mean(shifted * shifted, axis=-1, keepdims=True) + epsilon)
    normed = shifted * inverse
    return (normed * gain + shift, normed, inverse)


def norm_back(grad_normed, normed, inverse, gain):
    scaled = grad_normed * gain
    grad_input = inverse * (
        scaled
        - jnp.mean(scaled, axis=-1, keepdims=True)
        - normed * jnp.mean(scaled * normed, axis=-1, keepdims=True)
    )
    return (grad_input, jnp.sum(grad_normed * normed, axis=0), jnp.sum(grad_normed, axis=0))


def gelu_exact(values):
    return 0.5 * values * (1.0 + lax.erf(values * root_half))


def outer_sum(left, right):
    return lax.dot_general(left, right, (((0,), (0,)), ((), ())), preferred_element_type=F32)


def back_dot(left, right):
    return lax.dot_general(left, right, (((1,), (1,)), ((), ())), preferred_element_type=F32)


def layer(tokens, grids, keep_attn, keep_mlp, cotangent, params):
    ln1_gain, ln1_shift, w_qkv, bias_qv, w_proj, bias_proj, ln2_gain, ln2_shift, w_fc1, bias_fc1, w_fc2, bias_fc2 = params
    images, seq_len, feat_dim = tokens.shape
    num_heads = feat_dim // HEAD
    row_count = images * seq_len
    lengths = grids[:, 0] * grids[:, 1] + 2
    key_valid = lax.broadcasted_iota(jnp.int32, (images, seq_len), 1) < lengths[:, None]
    scale_attn = jnp.broadcast_to((keep_attn.astype(F32) / 0.9)[:, None], (images, seq_len)).reshape(row_count, 1)
    scale_mlp = jnp.broadcast_to((keep_mlp.astype(F32) / 0.9)[:, None], (images, seq_len)).reshape(row_count, 1)
    stream = tokens.astype(F32).reshape(row_count, feat_dim)
    normed_out, normed_one, inverse_one = layer_norm(stream, ln1_gain, ln1_shift)
    normed_low_one = normed_out.astype(BF16)
    full_bias = jnp.concatenate([bias_qv[:feat_dim], jnp.zeros((feat_dim,), F32), bias_qv[feat_dim:]])
    triple = jnp.dot(normed_low_one, w_qkv, preferred_element_type=F32) + full_bias
    triple = triple.astype(BF16).reshape(images, seq_len, 3, num_heads, HEAD)
    queries, key_rows, values = triple[:, :, 0], triple[:, :, 1], triple[:, :, 2]
    scores = jnp.einsum("bqhe,bkhe->bhqk", queries, key_rows, preferred_element_type=F32) * 0.125
    scores = jnp.where(key_valid[:, None, None, :], scores, -1000000000.0)
    probs_full = jax.nn.softmax(scores, axis=-1)
    probs_low = probs_full.astype(BF16)
    mixed_low = jnp.einsum("bhqk,bkhe->bqhe", probs_low, values, preferred_element_type=F32)
    mixed_low = mixed_low.reshape(row_count, feat_dim).astype(BF16)
    branch = jnp.dot(mixed_low, w_proj, preferred_element_type=F32) + bias_proj
    middle = stream + scale_attn * branch
    normed_out, normed_two, inverse_two = layer_norm(middle, ln2_gain, ln2_shift)
    normed_low_two = normed_out.astype(BF16)
    pre_act = jnp.dot(normed_low_two, w_fc1, preferred_element_type=F32) + bias_fc1
    act_value, act_pullback = jax.vjp(gelu_exact, pre_act)
    act_low = act_value.astype(BF16)
    branch_two = jnp.dot(act_low, w_fc2, preferred_element_type=F32) + bias_fc2
    layer_out = (middle + scale_mlp * branch_two).astype(BF16).reshape(images, seq_len, feat_dim)
    grad_out = cotangent.astype(F32).reshape(row_count, feat_dim)
    grad_branch_two = (grad_out * scale_mlp).astype(BF16)
    grad_fc2 = outer_sum(act_low, grad_branch_two)
    grad_fc2_bias = jnp.sum(grad_branch_two.astype(F32), axis=0)
    grad_act = back_dot(grad_branch_two, w_fc2)
    grad_pre = act_pullback(grad_act)[0].astype(BF16)
    grad_fc1 = outer_sum(normed_low_two, grad_pre)
    grad_fc1_bias = jnp.sum(grad_pre.astype(F32), axis=0)
    grad_normed_two = back_dot(grad_pre, w_fc1)
    grad_middle, grad_gain_two, grad_shift_two = norm_back(grad_normed_two, normed_two, inverse_two, ln2_gain)
    grad_middle = grad_middle + grad_out
    grad_branch = (grad_middle * scale_attn).astype(BF16)
    grad_proj = outer_sum(mixed_low, grad_branch)
    grad_proj_bias = jnp.sum(grad_branch.astype(F32), axis=0)
    grad_mixed = back_dot(grad_branch, w_proj).astype(BF16).reshape(images, seq_len, num_heads, HEAD)
    grad_values = jnp.einsum("bhqk,bqhe->bkhe", probs_low, grad_mixed, preferred_element_type=F32)
    grad_probs = jnp.einsum("bqhe,bkhe->bhqk", grad_mixed, values, preferred_element_type=F32)
    row_delta = jnp.sum(probs_full * grad_probs, axis=-1, keepdims=True)
    grad_scores = (probs_full * (grad_probs - row_delta)).astype(BF16)
    grad_queries = jnp.einsum("bhqk,bkhe->bqhe", grad_scores, key_rows, preferred_element_type=F32) * 0.125
    grad_keys = jnp.einsum("bhqk,bqhe->bkhe", grad_scores, queries, preferred_element_type=F32) * 0.125
    grad_triple = jnp.stack([grad_queries, grad_keys, grad_values], axis=2).astype(BF16).reshape(row_count, 3 * feat_dim)
    grad_qkv = outer_sum(normed_low_one, grad_triple)
    column_sums = jnp.sum(grad_triple.astype(F32), axis=0)
    grad_pair = jnp.concatenate([column_sums[:feat_dim], column_sums[2 * feat_dim :]])
    grad_normed_one = back_dot(grad_triple, w_qkv)
    grad_input, grad_gain_one, grad_shift_one = norm_back(grad_normed_one, normed_one, inverse_one, ln1_gain)
    grad_input = (grad_input + grad_middle).reshape(images, seq_len, feat_dim)
    grads = (
        grad_gain_one, grad_shift_one, grad_qkv, grad_pair, grad_proj, grad_proj_bias,
        grad_gain_two, grad_shift_two, grad_fc1, grad_fc1_bias, grad_fc2, grad_fc2_bias,
    )
    return layer_out, grad_input, grads


def by_collectives(tokens, grids, keep_attn, keep_mlp, cotangent, *params):
    whole = [lax.all_gather(p, "fsdp", axis=0, tiled=True) for p in params]
    whole = [p.astype(F32) if p.ndim == 1 else p for p in whole]
    layer_out, grad_input, grads = layer(tokens, grids, keep_attn, keep_mlp, cotangent, whole)
    shards = [lax.psum_scatter(g, "fsdp", scatter_dimension=0, tiled=True) for g in grads]
    totals = [lax.psum(g.astype(BF16), "rep").astype(F32) for g in shards]
    return (layer_out, grad_input) + tuple(totals)


def solution(mesh):
    vec, mat, rows = P("fsdp"), P("fsdp", None), P(("rep", "fsdp"))
    image = P(("rep", "fsdp"), None, None)
    weights = (vec, vec, mat, vec, mat, vec, vec, vec, mat, vec, mat, vec)
    in_specs = (image, P(("rep", "fsdp"), None), rows, rows, image) + weights
    out_specs = (image, image) + weights
    block = mesh.shape["fsdp"] == 16 and mesh.shape["rep"] == 2
    return jax.shard_map(
        by_block if block else by_collectives, mesh=mesh, in_specs=in_specs, out_specs=out_specs, check_vma=False
    )
```
